256 devices in a mesh: grp: 2 (over core), head: 16 (over y, x), seq: 8 (over z).
Axes of the slice: x: 4, y: 4, z: 8, core: 2. Of those that a mesh axis runs over, the one named last changes fastest.
Arguments:
- seq_in: bfloat16 [4096, 4096], P('seq', 'head'), may hold values from -36 to 36
- w_proj: bfloat16 [2, 3, 4096, 4096], P('grp', None, None, 'head')
- w_out: bfloat16 [2, 4096, 4096], P('grp', 'head'), may hold values from -0.09375 to 0.09375
- filters: float32 [4096, 4096], P(('head', 'seq'))
Outputs:
- paired: bfloat16 [2, 4096, 4096], P('grp', 'seq', 'head')
- grad_filters: float32 [4096, 4096], P(('head', 'seq'), 'grp')
The draws below stay inside these ranges and needn't reach their ends.
All inputs are finite; a program needn't handle non-finite values.
Results may differ from the reference program's by a relative error of at most 0.015.
Values may be sent and summed in bfloat16 or wider, within the bound.
No kernel may reach another device: no remote copies, remote signals or barrier semaphores. Data moves between devices by JAX's collectives and lax.ppermute only.
A program may use at most 64 MiB of HBM per device.

```python
import math
import jax
import jax.numpy as jnp
from jax import lax

D = 4096
HD = 128
L = 4096


def draw_seq_in(key, part):
    base = jax.random.normal(jax.random.fold_in(key, 11), (L, D), jnp.float32)
    base = jnp.clip(base, -6.0, 6.0)
    return base.astype(jnp.bfloat16)


def draw_w_proj(key, part):
    raw = jax.random.normal(jax.random.fold_in(key, 21), (2, 3, D, D), jnp.float32)
    raw = jnp.clip(raw, -6.0, 6.0) * D ** (-0.5)
    return raw.astype(jnp.bfloat16)


def draw_filters(key, part):
    places = jnp.arange(L, dtype=jnp.float32)
    lograte = jax.random.uniform(jax.random.fold_in(key, 31), (D,), jnp.float32, math.log(1.0 / (4 * L)), math.log(1.0 / 40))
    noise = jnp.clip(jax.random.normal(jax.random.fold_in(key, 32), (D, L), jnp.float32), -6.0, 6.0)
    rate = jnp.exp(lograte)
    energy = (1.0 - jnp.exp(-2.0 * rate * L)) / (1.0 - jnp.exp(-2.0 * rate))
    return noise * jnp.exp(-rate[:, None] * places[None, :]) * jnp.sqrt(L / energy)[:, None]


def block_scale(key, extent, cuts, low, high):
    level, own = 1.0, jax.random.fold_in(key, 6)
    for axis_at, shards_of in cuts:
        draws = jnp.exp(jax.random.uniform(jax.random.fold_in(own, axis_at), (shards_of,), jnp.float32, low / len(cuts), high / len(cuts)))
        level = level * jnp.repeat(draws, extent[axis_at] // shards_of).reshape([-1 if axis == axis_at else 1 for axis in range(len(extent))])
    return level


def bell_draw(key, shape, scale, limit, split=(), kind=jnp.bfloat16):
    drawn = jax.random.normal(key, shape, jnp.float32) * scale
    if len(split) > 0:
        drawn = block_scale(key, shape, split, -0.22, 0.18) * drawn
    return jnp.clip(drawn, min=-limit, max=limit).astype(kind)


def setup_inputs(seed: int = 0) -> dict:
    splits = jax.random.split(jax.random.key(seed), 5)
    return {
        "seq_in": draw_seq_in(jax.random.fold_in(splits[4], 71), 0),
        "w_proj": draw_w_proj(jax.random.fold_in(splits[4], 71), 0),
        "w_out": bell_draw(splits[2], (2, D, D), D ** -0.5, 0.09375, ((0, 2), (1, 16))),
        "filters": draw_filters(jax.random.fold_in(splits[4], 71), 0),
    }


def attend_heads(query, keys, values):
    length = query.shape[0]
    places = jnp.arange(length, dtype=jnp.int32)
    causal = places[None, :] <= places[:, None]
    factor = HD ** -0.5

    def one_head(triple):
        head_q, head_k, head_v = triple
        scores = jnp.dot(head_q, head_k.T, preferred_element_type=jnp.float32) * factor
        scores = jnp.where(causal, scores, -jnp.inf)
        highest = jnp.max(scores, axis=1, keepdims=True)
        expos = jnp.exp(scores - highest)
        totals = jnp.sum(expos, axis=1, keepdims=True)
        return jnp.dot(expos.astype(jnp.bfloat16), head_v, preferred_element_type=jnp.float32) / totals

    shaped = tuple(member.reshape(length, -1, HD).transpose(1, 0, 2) for member in (query, keys, values))
    heads_out = lax.map(one_head, shaped)
    return heads_out.transpose(1, 0, 2).reshape(length, -1).astype(jnp.bfloat16)


def spectra_of(signal, along):
    return jnp.fft.rfft(signal, n=2 * L, axis=along)


def back_of(spectrum):
    return jnp.fft.irfft(spectrum, n=2 * L, axis=0)[:L]


def reference(seq_in, w_proj, w_out, filters):
    def project(group):
        return [jnp.dot(seq_in, w_proj[group, which], preferred_element_type=jnp.float32).astype(jnp.bfloat16) for which in range(3)]

    query, keys_t, values_t = project(0)
    attended = attend_heads(query, keys_t, values_t)
    target = jnp.dot(attended, w_out[0], preferred_element_type=jnp.float32).astype(jnp.bfloat16)
    value_s, gate_in, gate_out = project(1)
    taps = filters * (L ** -0.5)
    carried = gate_in.astype(jnp.float32) * value_s.astype(jnp.float32)
    spec_u = spectra_of(carried, 0)
    spec_h = spectra_of(taps, 1).T
    conv = back_of(spec_u * spec_h)
    gated = (gate_out.astype(jnp.float32) * conv).astype(jnp.bfloat16)
    student = jnp.dot(gated, w_out[1], preferred_element_type=jnp.float32).astype(jnp.bfloat16)
    diff = (student.astype(jnp.float32) - target.astype(jnp.float32)).astype(jnp.bfloat16)
    d_gated = jnp.dot(diff, w_out[1].T, preferred_element_type=jnp.float32).astype(jnp.bfloat16)
    d_conv = gate_out.astype(jnp.float32) * d_gated.astype(jnp.float32)
    d_gate_out = (conv * d_gated.astype(jnp.float32)).astype(jnp.bfloat16)
    spec_d = spectra_of(d_conv, 0)
    d_carried = back_of(jnp.conj(spec_h) * spec_d)
    d_taps = back_of(jnp.conj(spec_u) * spec_d)
    d_gate_in = (d_carried * value_s.astype(jnp.float32)).astype(jnp.bfloat16)
    d_value = (d_carried * gate_in.astype(jnp.float32)).astype(jnp.bfloat16)
    grad_in = jnp.dot(d_value, w_proj[1, 0].T, preferred_element_type=jnp.float32)
    grad_in = grad_in + jnp.dot(d_gate_in, w_proj[1, 1].T, preferred_element_type=jnp.float32)
    grad_in = grad_in + jnp.dot(d_gate_out, w_proj[1, 2].T, preferred_element_type=jnp.float32)
    paired = jnp.stack([target, grad_in.astype(jnp.bfloat16)])
    grad_filters = (d_taps * (L ** -0.5)).T
    return (paired, grad_filters)
```

```python
import functools
import math

import jax
import jax.numpy as jnp
import numpy as np
from jax import lax
from jax.experimental import pallas as pl
from jax.experimental.pallas import tpu as pltpu
from jax.sharding import Mesh
from jax.sharding import PartitionSpec as P

F32 = jnp.float32
BF = jnp.bfloat16
HX = ("grp", "hy", "hx")
GZ = ("grp", "seq")
HEAD = ("hy", "hx")
VM = pl.BlockSpec(memory_space=pltpu.VMEM)
SM = pl.BlockSpec(memory_space=pltpu.SMEM)

ROOT_HALF = math.sqrt(0.5)

KEPT = [(k0, k1) for k0 in (1, 2, 3) for k1 in range(8)]
KEPT += [(0, k1) for k1 in range(5)] + [(4, k1) for k1 in range(4)]
NK = len(KEPT)


def dft_constants():
    m = np.arange(128)
    k = np.array([k0 + 8 * k1 for k0, k1 in KEPT])
    twist = np.exp(-2j * np.pi * np.outer(k, m) / 8192.0)
    weight = np.array([1.0 if kk in (0, 32) else 2.0 for kk in k]) / 8192.0
    back = np.conj(twist) * weight[:, None]
    inner = np.exp(-2j * np.pi * np.outer(m, m) / 128.0)
    c, s = inner.real, inner.imag
    forward = np.block([[c, s], [-s, c]])
    inverse = np.block([[c, -s], [s, c]])

    def split(mat):
        mat = jnp.asarray(mat, F32)
        hi = mat.astype(BF)
        lo = (mat - hi.astype(F32)).astype(BF)
        return jnp.stack([hi, lo])

    tw = np.stack([twist.real, twist.imag, back.real, back.imag]).astype(np.float32)
    return jnp.asarray(tw), split(forward), split(inverse)


def add_(a, b):
    if a is None:
        return b
    return a if b is None else a + b


def sub_(a, b):
    if b is None:
        return a
    return -b if a is None else a - b


def cadd(p, q):
    return (add_(p[0], q[0]), add_(p[1], q[1]))


def csub(p, q):
    return (sub_(p[0], q[0]), sub_(p[1], q[1]))


def scaled(a, by):
    if a is None or by == 0.0:
        return None
    return a if by == 1.0 else (-a if by == -1.0 else a * np.float32(by))


def turned(p, angle):
    eighth = angle / (math.pi / 4)
    near = round(eighth)
    re, im = p
    if abs(eighth - near) < 1e-9:
        near %= 8
        if near == 0:
            return p
        if near == 4:
            return (scaled(re, -1.0), scaled(im, -1.0))
        if near == 2:
            return (scaled(im, -1.0), re)
        if near == 6:
            return (im, scaled(re, -1.0))
        cc = ROOT_HALF if near in (1, 7) else -ROOT_HALF
        ss = ROOT_HALF if near in (1, 3) else -ROOT_HALF
        if re is not None and im is not None:
            if cc * ss > 0:
                return (scaled(re - im, cc), scaled(re + im, cc))
            return (scaled(re + im, cc), scaled(im - re, cc))
        return (sub_(scaled(re, cc), scaled(im, ss)), add_(scaled(re, ss), scaled(im, cc)))
    cc, ss = math.cos(angle), math.sin(angle)
    return (sub_(scaled(re, cc), scaled(im, ss)), add_(scaled(re, ss), scaled(im, cc)))


def dft_small(values, sign):
    count = len(values)
    if count == 1:
        return values
    even = dft_small(values[0::2], sign)
    odd = dft_small(values[1::2], sign)
    half = count // 2
    first, second = [], []
    for i in range(half):
        t = turned(odd[i], sign * 2 * math.pi * i / count)
        first.append(cadd(even[i], t))
        second.append(csub(even[i], t))
    return first + second


def outer_forward(x):
    c = np.float32(ROOT_HALF)
    cols = {k0: [] for k0 in range(5)}
    for b in range(8):
        x0, x1, x2, x3 = x[b], x[8 + b], x[16 + b], x[24 + b]
        e02, e13, d02 = x0 + x2, x1 + x3, x0 - x2
        cd, cs = c * (x1 - x3), c * e13
        part = {
            0: (e02 + e13, None),
            4: (e02 - e13, None),
            2: (d02, x3 - x1),
            1: (x0 + cd, -x2 - cs),
            3: (x0 - cd, x2 - cs),
        }
        for k0 in range(5):
            cols[k0].append(turned(part[k0], -2 * math.pi * b * k0 / 64))
    found = {k0: dft_small(cols[k0], -1) for k0 in range(5)}
    return [found[k0][k1] for k0, k1 in KEPT]


def outer_inverse(z):
    at = {kk: z[i] for i, kk in enumerate(KEPT)}
    zero = (None, None)
    grown = {}
    for k0 in (1, 2, 3):
        spread = dft_small([at[k0, k1] for k1 in range(8)], 1)
        grown[k0] = [turned(spread[b], 2 * math.pi * b * k0 / 64) for b in range(8)]
    real0 = dft_small([at[0, k1] if k1 < 5 else zero for k1 in range(8)], 1)
    spread4 = dft_small([at[4, k1] if k1 < 4 else zero for k1 in range(8)], 1)
    out = [None] * 32
    c = np.float32(ROOT_HALF)
    for b in range(8):
        r4 = turned(spread4[b], 2 * math.pi * b * 4 / 64)[0]
        g1, g2, g3 = grown[1][b], grown[2][b], grown[3][b]
        plus, minus = real0[b][0] + r4, real0[b][0] - r4
        out[b] = plus + g1[0] + g2[0] + g3[0]
        out[16 + b] = plus - g1[1] - g2[0] + g3[1]
        diag, anti = c * (g1[0] - g3[0]), c * (g1[1] + g3[1])
        out[8 + b] = minus + diag - anti - g2[1]
        out[24 + b] = minus - diag - anti + g2[1]
    return out


def store_split(hi_ref, lo_ref, k, rows, re, im):
    rh, ih = re.astype(BF), im.astype(BF)
    hi_ref[k, rows, 0:128] = rh
    hi_ref[k, rows, 128:256] = ih
    lo_ref[k, rows, 0:128] = (re - rh.astype(F32)).astype(BF)
    lo_ref[k, rows, 128:256] = (im - ih.astype(F32)).astype(BF)


def inner_product(hi_ref, lo_ref, mat_ref, out_ref):
    chans = hi_ref.shape[1]
    hi = hi_ref[...].reshape(NK * chans, 256)
    lo = lo_ref[...].reshape(NK * chans, 256)
    out = jnp.dot(hi, mat_ref[0], preferred_element_type=F32)
    out += jnp.dot(hi, mat_ref[1], preferred_element_type=F32)
    out += jnp.dot(lo, mat_ref[0], preferred_element_type=F32)
    out_ref[...] = out.reshape(NK, chans, 256)


def forward_spectrum(read, tw_ref, fwd_ref, hi_ref, lo_ref, out_ref):
    for part in range(2):
        rows = slice(16 * part, 16 * part + 16)
        outs = outer_forward([read(n, rows) for n in range(32)])
        for k in range(NK):
            re, im = outs[k]
            tr, ti = tw_ref[0, k : k + 1, :], tw_ref[1, k : k + 1, :]
            if im is None:
                store_split(hi_ref, lo_ref, k, rows, re * tr, re * ti)
            else:
                store_split(hi_ref, lo_ref, k, rows, re * tr - im * ti, re * ti + im * tr)
    inner_product(hi_ref, lo_ref, fwd_ref, out_ref)


def multiply_spectra(a_ref, b_ref, conj, hi_ref, lo_ref):
    chans = a_ref.shape[1]

    def one(k, carry):
        ar, ai = a_ref[k, :, 0:128], a_ref[k, :, 128:256]
        br, bi = b_ref[k, :, 0:128], b_ref[k, :, 128:256]
        if conj:
            re, im = ar * br + ai * bi, ar * bi - ai * br
        else:
            re, im = ar * br - ai * bi, ar * bi + ai * br
        store_split(hi_ref, lo_ref, k, slice(0, chans), re, im)
        return carry

    lax.fori_loop(0, NK, one, 0)


def inverse_field(hi_ref, lo_ref, inv_ref, tw_ref, mid_ref, write):
    inner_product(hi_ref, lo_ref, inv_ref, mid_ref)
    for part in range(2):
        rows = slice(16 * part, 16 * part + 16)
        z = []
        for k in range(NK):
            re, im = mid_ref[k, rows, 0:128], mid_ref[k, rows, 128:256]
            tr, ti = tw_ref[2, k : k + 1, :], tw_ref[3, k : k + 1, :]
            z.append((re * tr - im * ti, re * ti + im * tr))
        out = outer_inverse(z)
        for n in range(32):
            write(n, rows, out[n])


def spec_scratch(chans):
    return [
        pltpu.VMEM((NK, chans, 256), BF),
        pltpu.VMEM((NK, chans, 256), BF),
        pltpu.VMEM((NK, chans, 256), F32),
    ]


def filter_kernel(scale, f_ref, tw_ref, fwd_ref, out_ref, hi, lo, mid):
    def read(n, rows):
        return f_ref[rows, n * 128 : n * 128 + 128] * np.float32(scale)

    forward_spectrum(read, tw_ref, fwd_ref, hi, lo, out_ref)


def filter_spectrum(filters, tables, scale):
    tw, fwd, _ = tables
    chans = filters.shape[0]
    return pl.pallas_call(
        functools.partial(filter_kernel, scale),
        out_shape=jax.ShapeDtypeStruct((NK, chans, 256), F32),
        in_specs=[VM] * 3,
        out_specs=VM,
        scratch_shapes=spec_scratch(chans),
        name="filter_spectrum",
    )(filters, tw, fwd)


def conv_kernel(x_ref, h_ref, tw_ref, fwd_ref, inv_ref, gated_ref, conv_ref, u_ref, hi, lo, mid):
    def read(n, rows):
        z, i = divmod(n, 4)
        return x_ref[z, 0, i, rows, :].astype(F32) * x_ref[z, 1, i, rows, :].astype(F32)

    def write(n, rows, value):
        z, i = divmod(n, 4)
        conv_ref[n, rows, :] = value
        gated_ref[z, i, rows, :] = (x_ref[z, 2, i, rows, :].astype(F32) * value).astype(BF)

    forward_spectrum(read, tw_ref, fwd_ref, hi, lo, u_ref)
    multiply_spectra(u_ref, h_ref, False, hi, lo)
    inverse_field(hi, lo, inv_ref, tw_ref, mid, write)


def conv_forward(fields, spec_h, tables):
    tw, fwd, inv = tables
    chans = fields.shape[3]
    return pl.pallas_call(
        conv_kernel,
        out_shape=(
            jax.ShapeDtypeStruct((8, 4, chans, 128), BF),
            jax.ShapeDtypeStruct((32, chans, 128), F32),
            jax.ShapeDtypeStruct((NK, chans, 256), F32),
        ),
        in_specs=[VM] * 5,
        out_specs=(VM, VM, VM),
        scratch_shapes=spec_scratch(chans),
        name="conv_forward",
    )(fields, spec_h, tw, fwd, inv)


def back_kernel(
    g_ref, x_ref, conv_ref, h_ref, tw_ref, fwd_ref, inv_ref, out_ref, d_ref, hi, lo, mid
):
    def read(n, rows):
        z, i = divmod(n, 4)
        grad = g_ref[z, i, rows, :].astype(F32)
        out_ref[z, 2, i, rows, :] = (conv_ref[n, rows, :] * grad).astype(BF)
        return x_ref[z, 2, i, rows, :].astype(F32) * grad

    def write(n, rows, value):
        z, i = divmod(n, 4)
        out_ref[z, 0, i, rows, :] = (value * x_ref[z, 1, i, rows, :].astype(F32)).astype(BF)
        out_ref[z, 1, i, rows, :] = (value * x_ref[z, 0, i, rows, :].astype(F32)).astype(BF)

    forward_spectrum(read, tw_ref, fwd_ref, hi, lo, d_ref)
    multiply_spectra(h_ref, d_ref, True, hi, lo)
    inverse_field(hi, lo, inv_ref, tw_ref, mid, write)


def conv_backward(grads, fields, conv, spec_h, tables):
    tw, fwd, inv = tables
    chans = fields.shape[3]
    return pl.pallas_call(
        back_kernel,
        out_shape=(
            jax.ShapeDtypeStruct((8, 3, 4, chans, 128), BF),
            jax.ShapeDtypeStruct((NK, chans, 256), F32),
        ),
        in_specs=[VM] * 7,
        out_specs=(VM, VM),
        scratch_shapes=spec_scratch(chans),
        name="conv_backward",
    )(grads, fields, conv, spec_h, tw, fwd, inv)


def taps_kernel(scale, u_ref, d_ref, tw_ref, inv_ref, out_ref, hi, lo, mid):
    def write(n, rows, value):
        out_ref[rows, n * 128 : n * 128 + 128] = value * np.float32(scale)

    multiply_spectra(u_ref, d_ref, True, hi, lo)
    inverse_field(hi, lo, inv_ref, tw_ref, mid, write)


def taps_gradient(spec_u, spec_d, tables, scale):
    tw, _, inv = tables
    chans = spec_u.shape[1]
    return pl.pallas_call(
        functools.partial(taps_kernel, scale),
        out_shape=jax.ShapeDtypeStruct((chans, 4096), F32),
        in_specs=[VM] * 4,
        out_specs=VM,
        scratch_shapes=spec_scratch(chans),
        name="taps_gradient",
    )(spec_u, spec_d, tw, inv)


def gather_kernel(pos_ref, *refs):
    mine, other = refs[0:4], refs[4:8]
    w_ref, out_ref, fld_ref, x_ref = refs[8:12]
    g, y, x = pos_ref[0], pos_ref[1], pos_ref[2]

    @pl.when(pl.program_id(0) == 0)
    def _():
        for k2 in range(4):
            for k1 in range(4):
                first, second = lax.rem(4 - k1 + jnp.where(g == 0, x, y), 4), lax.rem(
                    4 - k2 + jnp.where(g == 0, y, x), 4
                )
                src = jnp.where(g == 0, second * 4 + first, first * 4 + second)
                a = pl.multiple_of(src * 256 + g * 128, 128)
                b = pl.multiple_of(src * 256 + (1 - g) * 128, 128)
                x_ref[:, pl.ds(a, 128)] = mine[k2][k1]
                x_ref[:, pl.ds(b, 128)] = other[k1][k2]

    acc = jnp.dot(x_ref[...], w_ref[0], preferred_element_type=F32)
    out_ref[0] = acc.astype(BF)

    @pl.when(g == 1)
    def _():
        for i in range(4):
            turned_acc = acc[i * 128 : i * 128 + 128, :].T.astype(BF)
            for z in range(8):
                fld_ref[z, 0, i] = turned_acc[z * 32 : z * 32 + 32, :]


def project(pos, mine, other, w):
    whole = pl.BlockSpec((4, 512, 128), lambda k, p: (0, 0, 0))
    return pl.pallas_call(
        gather_kernel,
        grid_spec=pltpu.PrefetchScalarGridSpec(
            num_scalar_prefetch=1,
            grid=(3,),
            in_specs=[whole] * 8 + [pl.BlockSpec((1, 4096, 256), lambda k, p: (k, 0, 0))],
            out_specs=[
                pl.BlockSpec((1, 512, 256), lambda k, p: (k, 0, 0)),
                pl.BlockSpec((8, 1, 4, 32, 128), lambda k, p: (0, k, 0, 0, 0)),
            ],
            scratch_shapes=[pltpu.VMEM((512, 4096), BF)],
        ),
        out_shape=(
            jax.ShapeDtypeStruct((3, 512, 256), BF),
            jax.ShapeDtypeStruct((8, 3, 4, 32, 128), BF),
        ),
        name="project",
    )(pos, *mine, *other, w)


SCORE = 128 ** (-0.5) * math.log2(math.e)


def attend_kernel(first, last, steps, count, pos_ref, q_ref, *refs):
    kv = refs[: 2 * count]
    refs = refs[2 * count :]
    if not first:
        m_in, l_in, a_in = refs[:3]
        refs = refs[3:]
    if last:
        out_ref, m_ref, l_ref, a_ref = refs
    else:
        m_ref, l_ref, a_ref = refs
    z = pos_ref[3]
    if not first:
        m_ref[...] = m_in[...]
        l_ref[...] = l_in[...]
        a_ref[...] = a_in[...]

    def block(k_ref, v_ref, h):
        cols = slice(h * 128, h * 128 + 128)
        s = lax.dot_general(
            k_ref[:, cols], q_ref[:, cols], (((1,), (1,)), ((), ())), preferred_element_type=F32
        ) * np.float32(SCORE)
        if first:
            key = lax.broadcasted_iota(jnp.int32, s.shape, 0)
            qry = lax.broadcasted_iota(jnp.int32, s.shape, 1)
            s = jnp.where(key <= qry, s, np.float32(-1e30))
            top = jnp.max(s, axis=0, keepdims=True)
        else:
            old = m_ref[h, 0:1, :]
            top = jnp.maximum(old, jnp.max(s, axis=0, keepdims=True))
        p = jnp.exp2(s - top)
        total = jnp.sum(p, axis=0, keepdims=True)
        prod = lax.dot_general(
            v_ref[:, cols], p.astype(BF), (((0,), (0,)), ((), ())), preferred_element_type=F32
        )
        if not first:
            fade = jnp.exp2(old - top)
            total += l_ref[h, 0:1, :] * fade
            prod += a_ref[h] * fade
        m_ref[h, 0:1, :] = top
        l_ref[h, 0:1, :] = total
        a_ref[h] = prod

    for i in range(count):
        if first:
            for h in range(2):
                block(kv[0], kv[1], h)
        else:
            step, forward = steps[i]

            @pl.when(z >= step if forward else z + step >= 8)
            def _():
                for h in range(2):
                    block(kv[2 * i], kv[2 * i + 1], h)

    if last:
        for h in range(2):
            done = a_ref[h] / l_ref[h, 0:1, :]
            out_ref[:, h * 128 : h * 128 + 128] = done.T.astype(BF)


def attend(pos, q, parts, state, steps, last):
    count = len(parts)
    first = state is None
    shapes = [
        jax.ShapeDtypeStruct((2, 8, 512), F32),
        jax.ShapeDtypeStruct((2, 8, 512), F32),
        jax.ShapeDtypeStruct((2, 128, 512), F32),
    ]
    scratch = []
    if last:
        scratch = [pltpu.VMEM(s.shape, s.dtype) for s in shapes]
        shapes = [jax.ShapeDtypeStruct((512, 256), BF)]
    flat = [leaf for pair in parts for leaf in pair]
    ins = [pos, q] + flat + ([] if first else list(state))

    return pl.pallas_call(
        functools.partial(attend_kernel, first, last, steps, count),
        out_shape=tuple(shapes),
        in_specs=[SM] + [VM] * (len(ins) - 1),
        out_specs=tuple([VM] * len(shapes)),
        scratch_shapes=scratch,
        name="attend",
    )(*ins)


def turn_kernel(in_ref, out_ref, t_ref):
    for z in range(8):
        for i in range(4):
            t_ref[z * 32 : z * 32 + 32, i * 128 : i * 128 + 128] = in_ref[z, i].astype(F32)
    out_ref[...] = t_ref[...].T.astype(BF)


def turn_fields(parts):
    return pl.pallas_call(
        turn_kernel,
        out_shape=jax.ShapeDtypeStruct((512, 256), BF),
        in_specs=[VM],
        out_specs=VM,
        scratch_shapes=[pltpu.VMEM((256, 512), F32)],
        name="turn_fields",
    )(parts)


def spread_kernel(pos_ref, x_ref, w_ref, *outs):
    y, x = pos_ref[1], pos_ref[2]
    a_refs, b_refs = outs[:4], outs[4:]
    for dx in range(4):
        for dy in range(4):
            dest = lax.rem(y + dy, 4) * 4 + lax.rem(x + dx, 4)
            cols = pl.ds(pl.multiple_of(dest * 256, 256), 256)
            part = jnp.dot(x_ref[...], w_ref[:, cols], preferred_element_type=F32).astype(BF)
            a_refs[dx][dy] = part[:, :128]
            b_refs[dy][dx] = part[:, 128:]


def spread_out(pos, mixed, w):
    shape = jax.ShapeDtypeStruct((4, 512, 128), BF)
    outs = pl.pallas_call(
        spread_kernel,
        out_shape=(shape,) * 8,
        in_specs=[SM, VM, VM],
        out_specs=(VM,) * 8,
        name="spread_out",
    )(pos, mixed, w)
    return outs[:4], outs[4:]


def gated_kernel(x_ref, w_ref, out_ref):
    acc = jnp.zeros((256, 512), F32)
    for s in range(16):
        acc += lax.dot_general(
            w_ref[:, s * 256 : s * 256 + 256],
            x_ref[s],
            (((1,), (1,)), ((), ())),
            preferred_element_type=F32,
        )
    low = acc.astype(BF)
    for z in range(8):
        for i in range(4):
            out_ref[z, i] = low[z * 32 : z * 32 + 32, i * 128 : i * 128 + 128]


def gated_gradient(diff, w):
    return pl.pallas_call(
        gated_kernel,
        out_shape=jax.ShapeDtypeStruct((8, 4, 32, 128), BF),
        in_specs=[VM, VM],
        out_specs=VM,
        name="gated_gradient",
    )(diff, w)


def input_kernel(d_ref, w_ref, out_ref, t_ref, l_ref):
    @pl.when(pl.program_id(0) == 0)
    def _():
        for k in range(3):
            for z in range(8):
                for i in range(4):
                    t_ref[z * 32 : z * 32 + 32, i * 128 : i * 128 + 128] = d_ref[z, k, i].astype(
                        F32
                    )
            l_ref[:, k * 256 : k * 256 + 256] = t_ref[...].T.astype(BF)

    acc = None
    for k in range(3):
        part = lax.dot_general(
            l_ref[:, k * 256 : k * 256 + 256],
            w_ref[k],
            (((1,), (1,)), ((), ())),
            preferred_element_type=F32,
        )
        acc = part if acc is None else acc + part
    out_ref[0] = acc.astype(BF)


def input_gradient(d_rows, w):
    return pl.pallas_call(
        input_kernel,
        grid=(16,),
        out_shape=jax.ShapeDtypeStruct((16, 512, 256), BF),
        in_specs=[
            pl.BlockSpec((8, 3, 4, 32, 128), lambda h: (0, 0, 0, 0, 0)),
            pl.BlockSpec((3, 256, 256), lambda h: (0, h, 0)),
        ],
        out_specs=pl.BlockSpec((1, 512, 256), lambda h: (h, 0, 0)),
        scratch_shapes=[pltpu.VMEM((256, 512), F32), pltpu.VMEM((512, 768), BF)],
        name="input_gradient",
    )(d_rows, w)


def sum_kernel(x_ref, out_ref):
    acc = x_ref[0].astype(F32)
    for i in range(1, 16):
        acc += x_ref[i].astype(F32)
    out_ref[...] = acc.astype(BF)


def sum_blocks(blocks):
    return pl.pallas_call(
        sum_kernel,
        out_shape=jax.ShapeDtypeStruct((512, 256), BF),
        in_specs=[VM],
        out_specs=VM,
        name="sum_blocks",
    )(blocks)


def plane_pairs(axes, by):
    pairs = []
    for g in range(2):
        for y in range(4):
            for x in range(4):
                ty, tx = (y, (x + by) % 4) if axes[g] == "x" else ((y + by) % 4, x)
                pairs.append((g * 16 + y * 4 + x, g * 16 + ty * 4 + tx))
    return pairs


def along(value, axes, by):
    return lax.ppermute(value, HX, plane_pairs(axes, by))


def ring(value, by):
    return lax.ppermute(value, "seq", [(i, (i + by) % 8) for i in range(8)])


def swapped(value):
    return lax.ppermute(value, "grp", [(0, 1), (1, 0)])


def gather_features(half):
    stack = jnp.stack([half] + [along(half, ("x", "y"), d) for d in (1, 2, 3)])
    mine = [stack] + [along(stack, ("y", "x"), d) for d in (1, 2, 3)]
    other = [swapped(part) for part in mine]
    return mine, other


def added(first, others):
    total = first.astype(F32)
    for other in others:
        total += other.astype(F32)
    return total.astype(BF)


def scatter_features(a, b):
    order = (1, 3, 2)
    ra = [along(a[d], ("x", "x"), d) for d in order]
    rb = [along(b[d], ("y", "y"), d) for d in order]
    sa, sb = added(a[0], ra), added(b[0], rb)
    ta = [along(sa[d], ("y", "y"), d) for d in order]
    tb = [along(sb[d], ("x", "x"), d) for d in order]
    return jnp.concatenate([added(sa[0], ta), added(sb[0], tb)], axis=1)


def body(seq_in, w_proj, w_out, filters):
    g, y, x, z = (lax.axis_index(name) for name in ("grp", "hy", "hx", "seq"))
    teacher = g == 0
    pos = jnp.stack([g, y, x, z]).astype(jnp.int32)
    weights_in, weights_out = w_proj[0], w_out[0]
    length = 4096
    tap_scale = length ** (-0.5)
    tables = dft_constants()

    half = lax.dynamic_slice_in_dim(seq_in, g * 128, 128, 1)
    mine, other = gather_features(half)
    spec_h = filter_spectrum(filters, tables, tap_scale)
    projected, fields_out = project(pos, mine, other, weights_in)

    def teach(operands):
        projected, fields_out = operands
        q, key, value = projected[0], projected[1], projected[2]
        state = attend(pos, q, [(key, value)], None, None, False)
        fk, fv, bk, bv = key, value, key, value
        attended = None
        for step in range(1, 5):
            fk, fv = ring(fk, 1), ring(fv, 1)
            parts, steps = [(fk, fv)], [(step, True)]
            if step < 4:
                bk, bv = ring(bk, -1), ring(bv, -1)
                parts.append((bk, bv))
                steps.append((step, False))
            state = attend(pos, q, parts, state, steps, step == 4)
        return (
            state[0],
            jnp.zeros((8, 3, 4, 32, 128), BF),
            jnp.zeros((32, 32, 128), F32),
            jnp.zeros((NK, 32, 256), F32),
        )

    def learn(operands):
        projected, fields_out = operands
        fields = lax.all_to_all(fields_out, "seq", 0, 0, tiled=True)
        gated, conv, spec_u = conv_forward(fields, spec_h, tables)
        returned = lax.all_to_all(gated, "seq", 0, 0, tiled=True)
        return (turn_fields(returned), fields, conv, spec_u)

    mixed, fields, conv, spec_u = lax.cond(teacher, teach, learn, (projected, fields_out))
    y_own = scatter_features(*spread_out(pos, mixed, weights_out))
    target = swapped(y_own)

    def rest(operands):
        return (jnp.zeros((512, 256), BF), jnp.zeros((32, 4096), F32))

    def learn_back(operands):
        y_own, target, fields, conv, spec_u = operands
        diff = (y_own.astype(F32) - target.astype(F32)).astype(BF)
        spread = jnp.broadcast_to(diff[None], (16, 512, 256))
        everyone = lax.all_to_all(spread, HEAD, 0, 0, tiled=True)
        d_gated = gated_gradient(everyone, weights_out)
        d_spread = lax.all_to_all(d_gated, "seq", 0, 0, tiled=True)
        d_fields, spec_d = conv_backward(d_spread, fields, conv, spec_h, tables)
        d_rows = lax.all_to_all(d_fields, "seq", 0, 0, tiled=True)
        d_taps = taps_gradient(spec_u, spec_d, tables, tap_scale)
        sums = input_gradient(d_rows, weights_in)
        gathered = lax.all_to_all(sums, HEAD, 0, 0, tiled=True)
        return (sum_blocks(gathered), d_taps)

    d_input, d_taps = lax.cond(
        teacher, rest, learn_back, (y_own, target, fields, conv, spec_u)
    )
    lower = swapped(d_taps[:, :2048].astype(BF)).astype(F32)
    paired = jnp.where(teacher, y_own, d_input)[None]
    grad_filters = jnp.where(teacher, lower, d_taps[:, 2048:])
    return (paired, grad_filters)


def solution(mesh):
    fine = Mesh(mesh.devices.reshape(2, 4, 4, 8), ("grp", "hy", "hx", "seq"))
    return jax.shard_map(
        body,
        mesh=fine,
        in_specs=(
            P("seq", HEAD),
            P("grp", None, None, HEAD),
            P("grp", HEAD, None),
            P(HEAD + ("seq",), None),
        ),
        out_specs=(P("grp", "seq", HEAD), P(HEAD + ("seq",), "grp")),
        check_vma=False,
    )
```

```python
import functools
import math

import jax
import jax.numpy as jnp
import numpy as np
from jax import lax
from jax.experimental import pallas as pl
from jax.experimental.pallas import tpu as pltpu
from jax.sharding import Mesh
from jax.sharding import PartitionSpec as P

F32 = jnp.float32
BF = jnp.bfloat16
HX = ("grp", "hy", "hx")
GZ = ("grp", "seq")
HEAD = ("hy", "hx")
VM = pl.BlockSpec(memory_space=pltpu.VMEM)
SM = pl.BlockSpec(memory_space=pltpu.SMEM)

ROOT_HALF = math.sqrt(0.5)

KEPT = [(k0, k1) for k0 in (1, 2, 3) for k1 in range(8)]
KEPT += [(0, k1) for k1 in range(5)] + [(4, k1) for k1 in range(4)]
NK = len(KEPT)


def dft_constants():
    m = np.arange(128)
    k = np.array([k0 + 8 * k1 for k0, k1 in KEPT])
    twist = np.exp(-2j * np.pi * np.outer(k, m) / 8192.0)
    weight = np.array([1.0 if kk in (0, 32) else 2.0 for kk in k]) / 8192.0
    back = np.conj(twist) * weight[:, None]
    inner = np.exp(-2j * np.pi * np.outer(m, m) / 128.0)
    c, s = inner.real, inner.imag
    forward = np.block([[c, s], [-s, c]])
    inverse = np.block([[c, -s], [s, c]])

    def split(mat):
        mat = jnp.asarray(mat, F32)
        hi = mat.astype(BF)
        lo = (mat - hi.astype(F32)).astype(BF)
        return jnp.stack([hi, lo])

    tw = np.stack([twist.real, twist.imag, back.real, back.imag]).astype(np.float32)
    return jnp.asarray(tw), split(forward), split(inverse)


def add_(a, b):
    if a is None:
        return b
    return a if b is None else a + b


def sub_(a, b):
    if b is None:
        return a
    return -b if a is None else a - b


def cadd(p, q):
    return (add_(p[0], q[0]), add_(p[1], q[1]))


def csub(p, q):
    return (sub_(p[0], q[0]), sub_(p[1], q[1]))


def scaled(a, by):
    if a is None or by == 0.0:
        return None
    return a if by == 1.0 else (-a if by == -1.0 else a * np.float32(by))


def turned(p, angle):
    eighth = angle / (math.pi / 4)
    near = round(eighth)
    re, im = p
    if abs(eighth - near) < 1e-9:
        near %= 8
        if near == 0:
            return p
        if near == 4:
            return (scaled(re, -1.0), scaled(im, -1.0))
        if near == 2:
            return (scaled(im, -1.0), re)
        if near == 6:
            return (im, scaled(re, -1.0))
        cc = ROOT_HALF if near in (1, 7) else -ROOT_HALF
        ss = ROOT_HALF if near in (1, 3) else -ROOT_HALF
        if re is not None and im is not None:
            if cc * ss > 0:
                return (scaled(re - im, cc), scaled(re + im, cc))
            return (scaled(re + im, cc), scaled(im - re, cc))
        return (sub_(scaled(re, cc), scaled(im, ss)), add_(scaled(re, ss), scaled(im, cc)))
    cc, ss = math.cos(angle), math.sin(angle)
    return (sub_(scaled(re, cc), scaled(im, ss)), add_(scaled(re, ss), scaled(im, cc)))


def dft_small(values, sign):
    count = len(values)
    if count == 1:
        return values
    even = dft_small(values[0::2], sign)
    odd = dft_small(values[1::2], sign)
    half = count // 2
    first, second = [], []
    for i in range(half):
        t = turned(odd[i], sign * 2 * math.pi * i / count)
        first.append(cadd(even[i], t))
        second.append(csub(even[i], t))
    return first + second


def outer_forward(x):
    c = np.float32(ROOT_HALF)
    cols = {k0: [] for k0 in range(5)}
    for b in range(8):
        x0, x1, x2, x3 = x[b], x[8 + b], x[16 + b], x[24 + b]
        e02, e13, d02 = x0 + x2, x1 + x3, x0 - x2
        cd, cs = c * (x1 - x3), c * e13
        part = {
            0: (e02 + e13, None),
            4: (e02 - e13, None),
            2: (d02, x3 - x1),
            1: (x0 + cd, -x2 - cs),
            3: (x0 - cd, x2 - cs),
        }
        for k0 in range(5):
            cols[k0].append(turned(part[k0], -2 * math.pi * b * k0 / 64))
    found = {k0: dft_small(cols[k0], -1) for k0 in range(5)}
    return [found[k0][k1] for k0, k1 in KEPT]


def outer_inverse(z):
    at = {kk: z[i] for i, kk in enumerate(KEPT)}
    zero = (None, None)
    grown = {}
    for k0 in (1, 2, 3):
        spread = dft_small([at[k0, k1] for k1 in range(8)], 1)
        grown[k0] = [turned(spread[b], 2 * math.pi * b * k0 / 64) for b in range(8)]
    real0 = dft_small([at[0, k1] if k1 < 5 else zero for k1 in range(8)], 1)
    spread4 = dft_small([at[4, k1] if k1 < 4 else zero for k1 in range(8)], 1)
    out = [None] * 32
    c = np.float32(ROOT_HALF)
    for b in range(8):
        r4 = turned(spread4[b], 2 * math.pi * b * 4 / 64)[0]
        g1, g2, g3 = grown[1][b], grown[2][b], grown[3][b]
        plus, minus = real0[b][0] + r4, real0[b][0] - r4
        out[b] = plus + g1[0] + g2[0] + g3[0]
        out[16 + b] = plus - g1[1] - g2[0] + g3[1]
        diag, anti = c * (g1[0] - g3[0]), c * (g1[1] + g3[1])
        out[8 + b] = minus + diag - anti - g2[1]
        out[24 + b] = minus - diag - anti + g2[1]
    return out


def store_split(hi_ref, lo_ref, k, rows, re, im):
    rh, ih = re.astype(BF), im.astype(BF)
    hi_ref[k, rows, 0:128] = rh
    hi_ref[k, rows, 128:256] = ih
    lo_ref[k, rows, 0:128] = (re - rh.astype(F32)).astype(BF)
    lo_ref[k, rows, 128:256] = (im - ih.astype(F32)).astype(BF)


def inner_product(hi_ref, lo_ref, mat_ref, out_ref):
    chans = hi_ref.shape[1]
    hi = hi_ref[...].reshape(NK * chans, 256)
    lo = lo_ref[...].reshape(NK * chans, 256)
    out = jnp.dot(hi, mat_ref[0], preferred_element_type=F32)
    out += jnp.dot(hi, mat_ref[1], preferred_element_type=F32)
    out += jnp.dot(lo, mat_ref[0], preferred_element_type=F32)
    out_ref[...] = out.reshape(NK, chans, 256)


def over_rows(chans, step):
    def one(part, carry):
        step(pl.ds(pl.multiple_of(part * 16, 16), 16))
        return carry

    lax.fori_loop(0, chans // 16, one, 0)


def forward_spectrum(read, tw_ref, fwd_ref, hi_ref, lo_ref, out_ref):
    def step(rows):
        outs = outer_forward([read(n, rows) for n in range(32)])
        for k in range(NK):
            re, im = outs[k]
            tr, ti = tw_ref[0, k : k + 1, :], tw_ref[1, k : k + 1, :]
            if im is None:
                store_split(hi_ref, lo_ref, k, rows, re * tr, re * ti)
            else:
                store_split(hi_ref, lo_ref, k, rows, re * tr - im * ti, re * ti + im * tr)

    over_rows(hi_ref.shape[1], step)
    inner_product(hi_ref, lo_ref, fwd_ref, out_ref)


def multiply_spectra(a_ref, b_ref, conj, hi_ref, lo_ref):
    chans = a_ref.shape[1]

    def one(k, carry):
        ar, ai = a_ref[k, :, 0:128], a_ref[k, :, 128:256]
        br, bi = b_ref[k, :, 0:128], b_ref[k, :, 128:256]
        if conj:
            re, im = ar * br + ai * bi, ar * bi - ai * br
        else:
            re, im = ar * br - ai * bi, ar * bi + ai * br
        store_split(hi_ref, lo_ref, k, slice(0, chans), re, im)
        return carry

    lax.fori_loop(0, NK, one, 0)


def inverse_field(hi_ref, lo_ref, inv_ref, tw_ref, mid_ref, write):
    inner_product(hi_ref, lo_ref, inv_ref, mid_ref)

    def step(rows):
        z = []
        for k in range(NK):
            re, im = mid_ref[k, rows, 0:128], mid_ref[k, rows, 128:256]
            tr, ti = tw_ref[2, k : k + 1, :], tw_ref[3, k : k + 1, :]
            z.append((re * tr - im * ti, re * ti + im * tr))
        out = outer_inverse(z)
        for n in range(32):
            write(n, rows, out[n])

    over_rows(hi_ref.shape[1], step)


def spec_scratch(chans):
    return [
        pltpu.VMEM((NK, chans, 256), BF),
        pltpu.VMEM((NK, chans, 256), BF),
        pltpu.VMEM((NK, chans, 256), F32),
    ]


def filter_kernel(scale, f_ref, tw_ref, fwd_ref, out_ref, hi, lo, mid):
    def read(n, rows):
        return f_ref[rows, n * 128 : n * 128 + 128] * np.float32(scale)

    forward_spectrum(read, tw_ref, fwd_ref, hi, lo, out_ref)


def filter_spectrum(filters, tables, scale):
    tw, fwd, _ = tables
    chans = filters.shape[0]
    return pl.pallas_call(
        functools.partial(filter_kernel, scale),
        out_shape=jax.ShapeDtypeStruct((NK, chans, 256), F32),
        in_specs=[VM] * 3,
        out_specs=VM,
        scratch_shapes=spec_scratch(chans),
        name="filter_spectrum",
    )(filters, tw, fwd)


def conv_kernel(conj, x_ref, h_ref, tw_ref, fwd_ref, inv_ref, out_ref, u_ref, hi, lo, mid):
    def read(n, rows):
        z, i = divmod(n, 4)
        return x_ref[z, i, rows, :].astype(F32)

    def write(n, rows, value):
        z, i = divmod(n, 4)
        out_ref[z, i, rows, :] = value.astype(BF)

    forward_spectrum(read, tw_ref, fwd_ref, hi, lo, u_ref)
    multiply_spectra(h_ref, u_ref, conj, hi, lo)
    inverse_field(hi, lo, inv_ref, tw_ref, mid, write)


def convolve(field, spec_h, tables, conj):
    tw, fwd, inv = tables
    chans = field.shape[2]
    return pl.pallas_call(
        functools.partial(conv_kernel, conj),
        out_shape=(
            jax.ShapeDtypeStruct((8, 4, chans, 128), BF),
            jax.ShapeDtypeStruct((NK, chans, 256), F32),
        ),
        in_specs=[VM] * 5,
        out_specs=(VM, VM),
        scratch_shapes=spec_scratch(chans),
        name="convolve_back" if conj else "convolve",
    )(field, spec_h, tw, fwd, inv)


def taps_kernel(scale, u_ref, d_ref, tw_ref, inv_ref, out_ref, hi, lo, mid):
    def write(n, rows, value):
        out_ref[rows, n * 128 : n * 128 + 128] = value * np.float32(scale)

    multiply_spectra(u_ref, d_ref, True, hi, lo)
    inverse_field(hi, lo, inv_ref, tw_ref, mid, write)


def taps_gradient(spec_u, spec_d, tables, scale):
    tw, _, inv = tables
    chans = spec_u.shape[1]
    return pl.pallas_call(
        functools.partial(taps_kernel, scale),
        out_shape=jax.ShapeDtypeStruct((chans, 4096), F32),
        in_specs=[VM] * 4,
        out_specs=VM,
        scratch_shapes=spec_scratch(chans),
        name="taps_gradient",
    )(spec_u, spec_d, tw, inv)


def assemble(g, mine, other, x_ref):
    for i in range(4):
        for j in range(4):
            src = jnp.where(g == 0, i * 4 + j, j * 4 + i)
            a = pl.multiple_of(src * 256 + g * 128, 128)
            b = pl.multiple_of(src * 256 + (1 - g) * 128, 128)
            x_ref[:, pl.ds(a, 128)] = mine[i, j]
            x_ref[:, pl.ds(b, 128)] = other[j, i]


def to_blocks(rows, out_ref):
    for i in range(4):
        part = rows[i * 128 : i * 128 + 128, :].T.astype(BF)
        for z in range(8):
            out_ref[z, i] = part[z * 32 : z * 32 + 32, :]


def from_blocks(in_ref, t_ref):
    for z in range(8):
        for i in range(4):
            t_ref[z * 32 : z * 32 + 32, i * 128 : i * 128 + 128] = in_ref[z, i].astype(F32)
    return t_ref[...].T


def first_kernel(pos_ref, mine, other, w_ref, out_ref, car_ref, x_ref):
    g, step = pos_ref[0], pl.program_id(0)

    @pl.when(step == 0)
    def _():
        assemble(g, mine, other, x_ref)

    out_ref[step] = jnp.dot(x_ref[...], w_ref[0], preferred_element_type=F32).astype(BF)

    @pl.when((g == 1) & (step == 1))
    def _():
        to_blocks(out_ref[0].astype(F32) * out_ref[1].astype(F32), car_ref)


def project_first(pos, mine, other, w):
    whole = pl.BlockSpec((4, 4, 512, 128), lambda k, p: (0, 0, 0, 0))
    return pl.pallas_call(
        first_kernel,
        grid_spec=pltpu.PrefetchScalarGridSpec(
            num_scalar_prefetch=1,
            grid=(2,),
            in_specs=[whole] * 2
            + [pl.BlockSpec((1, 4096, 256), lambda k, p: (k + 1 - p[0], 0, 0))],
            out_specs=[
                pl.BlockSpec((2, 512, 256), lambda k, p: (0, 0, 0)),
                pl.BlockSpec((8, 4, 32, 128), lambda k, p: (0, 0, 0, 0)),
                pl.BlockSpec((512, 4096), lambda k, p: (0, 0)),
            ],
        ),
        out_shape=(
            jax.ShapeDtypeStruct((2, 512, 256), BF),
            jax.ShapeDtypeStruct((8, 4, 32, 128), BF),
            jax.ShapeDtypeStruct((512, 4096), BF),
        ),
        name="project_first",
    )(pos, mine, other, w)


def last_kernel(x_ref, w_ref, out_ref):
    out_ref[...] = jnp.dot(x_ref[...], w_ref[0], preferred_element_type=F32).astype(BF)


def project_last(x, w, which):
    return pl.pallas_call(
        last_kernel,
        grid=(1,),
        in_specs=[
            pl.BlockSpec((512, 4096), lambda i: (0, 0)),
            pl.BlockSpec((1, 4096, 256), lambda i: (which, 0, 0)),
        ],
        out_specs=pl.BlockSpec((512, 256), lambda i: (0, 0)),
        out_shape=jax.ShapeDtypeStruct((512, 256), BF),
        cost_estimate=pl.CostEstimate(
            flops=2 * 512 * 4096 * 256, bytes_accessed=6500000, transcendentals=0
        ),
        name="project_last",
    )(x, w)


SCORE = 128 ** (-0.5) * math.log2(math.e)


def attend_kernel(first, last, steps, pos_ref, q_ref, *refs):
    kv = refs[: len(steps)]
    refs = refs[len(steps) :]
    if not first:
        m_in, l_in, a_in = refs[:3]
        refs = refs[3:]
    if last:
        out_ref, m_ref, l_ref, a_ref = refs
    else:
        m_ref, l_ref, a_ref = refs
    z = pos_ref[3]
    if not first:
        m_ref[...] = m_in[...]
        l_ref[...] = l_in[...]
        a_ref[...] = a_in[...]

    def block(kv_ref):
        def one(h, carry):
            cols = pl.ds(pl.multiple_of(h * 128, 128), 128)
            s = lax.dot_general(
                kv_ref[0, :, cols],
                q_ref[:, cols],
                (((1,), (1,)), ((), ())),
                preferred_element_type=F32,
            ) * np.float32(SCORE)
            if first:
                key = lax.broadcasted_iota(jnp.int32, s.shape, 0)
                qry = lax.broadcasted_iota(jnp.int32, s.shape, 1)
                s = jnp.where(key <= qry, s, np.float32(-1e30))
                top = jnp.max(s, axis=0, keepdims=True)
            else:
                old = m_ref[h, 0:1, :]
                top = jnp.maximum(old, jnp.max(s, axis=0, keepdims=True))
            p = jnp.exp2(s - top)
            total = jnp.sum(p, axis=0, keepdims=True)
            prod = lax.dot_general(
                kv_ref[1, :, cols],
                p.astype(BF),
                (((0,), (0,)), ((), ())),
                preferred_element_type=F32,
            )
            if not first:
                fade = jnp.exp2(old - top)
                total += l_ref[h, 0:1, :] * fade
                prod += a_ref[h] * fade
            m_ref[h, 0:1, :] = top
            l_ref[h, 0:1, :] = total
            a_ref[h] = prod
            return carry

        lax.fori_loop(0, 2, one, 0)

    for i, (step, forward) in enumerate(steps):
        if first:
            block(kv[i])
        else:
            pl.when(z >= step if forward else z + step >= 8)(functools.partial(block, kv[i]))

    if last:
        for h in range(2):
            done = a_ref[h] / l_ref[h, 0:1, :]
            out_ref[:, h * 128 : h * 128 + 128] = done.T.astype(BF)


def attend(pos, q, blocks, state, steps, last):
    first = state is None
    shapes = [
        jax.ShapeDtypeStruct((2, 8, 512), F32),
        jax.ShapeDtypeStruct((2, 8, 512), F32),
        jax.ShapeDtypeStruct((2, 128, 512), F32),
    ]
    scratch = []
    if last:
        scratch = [pltpu.VMEM(s.shape, s.dtype) for s in shapes]
        shapes = [jax.ShapeDtypeStruct((512, 256), BF)]
    ins = [pos, q] + list(blocks) + ([] if first else list(state))
    return pl.pallas_call(
        functools.partial(attend_kernel, first, last, steps),
        out_shape=tuple(shapes),
        in_specs=[SM] + [VM] * (len(ins) - 1),
        out_specs=tuple([VM] * len(shapes)),
        scratch_shapes=scratch,
        cost_estimate=pl.CostEstimate(
            flops=1000000000 * len(steps), bytes_accessed=1000000, transcendentals=500000
        ),
        name="attend",
    )(*ins)


def gate_kernel(in_ref, gate_ref, mixed_ref, conv_ref, t_ref):
    conv = from_blocks(in_ref, t_ref)
    conv_ref[...] = conv.astype(BF)
    mixed_ref[...] = (gate_ref[...].astype(F32) * conv).astype(BF)


def gate_rows(blocks, gate):
    shape = jax.ShapeDtypeStruct((512, 256), BF)
    return pl.pallas_call(
        gate_kernel,
        out_shape=(shape, shape),
        in_specs=[VM, VM],
        out_specs=(VM, VM),
        scratch_shapes=[pltpu.VMEM((256, 512), F32)],
        name="gate_rows",
    )(blocks, gate)


def spread_kernel(pos_ref, x_ref, w_ref, *outs):
    y, x = pos_ref[1], pos_ref[2]
    a_refs, b_refs = outs[:4], outs[4:]
    for dx in range(4):
        for dy in range(4):
            dest = lax.rem(y + dy, 4) * 4 + lax.rem(x + dx, 4)
            cols = pl.ds(pl.multiple_of(dest * 256, 256), 256)
            part = jnp.dot(x_ref[...], w_ref[:, cols], preferred_element_type=F32).astype(BF)
            a_refs[dx][dy] = part[:, :128]
            b_refs[dy][dx] = part[:, 128:]


def spread_out(pos, mixed, w):
    shape = jax.ShapeDtypeStruct((4, 512, 128), BF)
    outs = pl.pallas_call(
        spread_kernel,
        out_shape=(shape,) * 8,
        in_specs=[SM, VM, VM],
        out_specs=(VM,) * 8,
        name="spread_out",
    )(pos, mixed, w)
    return outs[:4], outs[4:]


def gated_kernel(pos_ref, mine, other, w_ref, conv_ref, gate_ref, dconv_ref, dgate_ref, x_ref):
    assemble(pos_ref[0], mine, other, x_ref)
    acc = lax.dot_general(
        x_ref[...], w_ref[...], (((1,), (1,)), ((), ())), preferred_element_type=F32
    )
    grad = acc.astype(BF).astype(F32)
    dgate_ref[...] = (conv_ref[...].astype(F32) * grad).astype(BF)
    to_blocks(gate_ref[...].astype(F32) * grad, dconv_ref)


def gated_gradient(pos, mine, other, w, conv, gate):
    return pl.pallas_call(
        gated_kernel,
        out_shape=(
            jax.ShapeDtypeStruct((8, 4, 32, 128), BF),
            jax.ShapeDtypeStruct((512, 256), BF),
        ),
        in_specs=[SM] + [VM] * 5,
        out_specs=(VM, VM),
        scratch_shapes=[pltpu.VMEM((512, 4096), BF)],
        name="gated_gradient",
    )(pos, mine, other, w, conv, gate)


def input_kernel(d_ref, pair_ref, dgate_ref, w_ref, a_ref, b_ref, t_ref, l_ref, wide_ref):
    @pl.when(pl.program_id(0) == 0)
    def _():
        carried = from_blocks(d_ref, t_ref)
        l_ref[:, 0:256] = (carried * pair_ref[1].astype(F32)).astype(BF)
        l_ref[:, 256:512] = (carried * pair_ref[0].astype(F32)).astype(BF)
        l_ref[:, 512:768] = dgate_ref[...]

    for k in range(3):
        wide_ref[:, k * 256 : k * 256 + 256] = w_ref[k]
    for x in range(4):
        part = lax.dot_general(
            l_ref[...],
            wide_ref[x * 256 : x * 256 + 256, :],
            (((1,), (1,)), ((), ())),
            preferred_element_type=F32,
        ).astype(BF)
        a_ref[x, 0] = part[:, :128]
        b_ref[0, x] = part[:, 128:]


def input_gradient(d_blocks, pair, d_gate, w):
    shape = jax.ShapeDtypeStruct((4, 4, 512, 128), BF)
    return pl.pallas_call(
        input_kernel,
        grid=(4,),
        out_shape=(shape, shape),
        in_specs=[
            pl.BlockSpec((8, 4, 32, 128), lambda y: (0, 0, 0, 0)),
            pl.BlockSpec((2, 512, 256), lambda y: (0, 0, 0)),
            pl.BlockSpec((512, 256), lambda y: (0, 0)),
            pl.BlockSpec((3, 1024, 256), lambda y: (0, y, 0)),
        ],
        out_specs=(
            pl.BlockSpec((4, 1, 512, 128), lambda y: (0, y, 0, 0)),
            pl.BlockSpec((1, 4, 512, 128), lambda y: (y, 0, 0, 0)),
        ),
        scratch_shapes=[
            pltpu.VMEM((256, 512), F32),
            pltpu.VMEM((512, 768), BF),
            pltpu.VMEM((1024, 768), BF),
        ],
        name="input_gradient",
    )(d_blocks, pair, d_gate, w)


def blank_kernel(*refs):
    pass


def blank(pos, *shapes):
    anywhere = pl.BlockSpec(memory_space=pl.ANY)
    return pl.pallas_call(
        blank_kernel,
        out_shape=tuple(jax.ShapeDtypeStruct(shape, kind) for shape, kind in shapes),
        in_specs=[SM],
        out_specs=(anywhere,) * len(shapes),
        name="blank",
    )(pos)


def plane_pairs(axis, by):
    pairs = []
    for g in range(2):
        for y in range(4):
            for x in range(4):
                ty, tx = (y, (x + by) % 4) if axis == "x" else ((y + by) % 4, x)
                pairs.append((g * 16 + y * 4 + x, g * 16 + ty * 4 + tx))
    return pairs


def along(value, axis, by):
    return lax.ppermute(value, HX, plane_pairs(axis, by))


def ring(value, by):
    return lax.ppermute(value, "seq", [(i, (i + by) % 8) for i in range(8)])


def swapped(value):
    return lax.ppermute(value, "grp", [(0, 1), (1, 0)])


def exchanged(value, axis):
    return lax.all_to_all(value, axis, 0, 0, tiled=True)


def gather_half(teacher, half):
    def through(first, second):
        def run(own):
            row = exchanged(jnp.broadcast_to(own[None], (4,) + own.shape), first)
            return exchanged(jnp.broadcast_to(row[None], (4,) + row.shape), second)

        return run

    mine = lax.cond(teacher, through("hx", "hy"), through("hy", "hx"), half)
    return mine, swapped(mine)


def added(first, others):
    total = first.astype(F32)
    for other in others:
        total += other.astype(F32)
    return total.astype(BF)


def scatter_features(a, b):
    order = (1, 3, 2)
    ra = [along(a[d], "x", d) for d in order]
    rb = [along(b[d], "y", d) for d in order]
    sa, sb = added(a[0], ra), added(b[0], rb)
    ta = [along(sa[d], "y", d) for d in order]
    tb = [along(sb[d], "x", d) for d in order]
    return jnp.concatenate([added(sa[0], ta), added(sb[0], tb)], axis=1)


def scatter_half(teacher, a, b):
    def through(which, first, second):
        def run(operands):
            got = exchanged(operands[which], first)
            row = added(got[0], [got[1], got[2], got[3]])
            got = exchanged(row, second)
            return added(got[0], [got[1], got[2], got[3]])

        return run

    return lax.cond(teacher, through(0, "hx", "hy"), through(1, "hy", "hx"), (a, b))


def body(seq_in, w_proj, w_out, filters):
    g, y, x, z = (lax.axis_index(name) for name in ("grp", "hy", "hx", "seq"))
    teacher = g == 0
    pos = jnp.stack([g, y, x, z]).astype(jnp.int32)
    weights_in, weights_out = w_proj[0], w_out[0]
    length = 4096
    tap_scale = length ** (-0.5)
    tables = dft_constants()
    spec_shape = ((NK, 32, 256), F32)
    row_shape = ((512, 256), BF)

    half = lax.dynamic_slice_in_dim(seq_in, g * 128, 128, 1)
    mine, other = gather_half(teacher, half)
    pair, carried, gathered = project_first(pos, mine, other, weights_in)

    def teach(operands):
        pair, carried, gathered = operands
        q = project_last(gathered, weights_in, 0)
        moved = (ring(pair, 1), ring(pair, -1))
        state = attend(pos, q, [pair], None, [(0, True)], False)
        for step in range(1, 5):
            moved, state = lax.optimization_barrier((moved, state))
            blocks, steps = moved, [(step, True), (step, False)]
            if step < 3:
                moved = (ring(blocks[0], 1), ring(blocks[1], -1))
            elif step == 3:
                moved = (ring(blocks[0], 1),)
            else:
                steps = steps[:1]
            state = attend(pos, q, blocks, state, steps, step == 4)
        return (state[0],) + tuple(blank(pos, row_shape, row_shape, spec_shape, spec_shape))

    def learn(operands):
        pair, carried, gathered = operands
        field = exchanged(carried, "seq")
        gate = project_last(gathered, weights_in, 2)
        spec_h = filter_spectrum(filters, tables, tap_scale)
        conv, spec_u = convolve(field, spec_h, tables, False)
        mixed, conv_rows = gate_rows(exchanged(conv, "seq"), gate)
        return (mixed, conv_rows, gate, spec_u, spec_h)

    mixed, conv_rows, gate, spec_u, spec_h = lax.cond(
        teacher, teach, learn, (pair, carried, gathered)
    )
    y_own = scatter_features(*spread_out(pos, mixed, weights_out))
    sent = jnp.where(teacher, y_own[:, 128:], y_own[:, :128])
    kept = jnp.where(teacher, y_own[:, :128], y_own[:, 128:])
    got = swapped(sent)
    low, high = kept.astype(F32), got.astype(F32)
    diff = jnp.where(teacher, high - low, low - high).astype(BF)
    mine, other = gather_half(teacher, diff)

    def rest(operands):
        shape = ((4, 4, 512, 128), BF)
        return tuple(blank(pos, shape, shape, ((32, 4096), F32)))

    def learn_back(operands):
        mine, other, pair, conv_rows, gate, spec_u, spec_h = operands
        d_conv, d_gate = gated_gradient(pos, mine, other, weights_out, conv_rows, gate)
        d_field, spec_d = convolve(exchanged(d_conv, "seq"), spec_h, tables, True)
        d_blocks = exchanged(d_field, "seq")
        d_taps = taps_gradient(spec_u, spec_d, tables, tap_scale)
        a, b = input_gradient(d_blocks, pair, d_gate, weights_in)
        return (a, b, d_taps)

    a, b, d_taps = lax.cond(
        teacher, rest, learn_back, (mine, other, pair, conv_rows, gate, spec_u, spec_h)
    )
    lower = swapped(d_taps[:, :2048].astype(BF)).astype(F32)
    sums = scatter_half(teacher, swapped(a), b)
    d_input = jnp.concatenate([swapped(sums), sums], axis=1)
    paired = jnp.where(teacher, y_own, d_input)[None]
    grad_filters = jnp.where(teacher, lower, d_taps[:, 2048:])
    return (paired, grad_filters)


def solution(mesh):
    fine = Mesh(mesh.devices.reshape(2, 4, 4, 8), ("grp", "hy", "hx", "seq"))
    return jax.shard_map(
        body,
        mesh=fine,
        in_specs=(
            P("seq", HEAD),
            P("grp", None, None, HEAD),
            P("grp", HEAD, None),
            P(HEAD + ("seq",), None),
        ),
        out_specs=(P("grp", "seq", HEAD), P(HEAD + ("seq",), "grp")),
        check_vma=False,
    )
```

```python
import functools
import math

import jax
import jax.numpy as jnp
import numpy as np
from jax import lax
from jax.experimental import pallas as pl
from jax.experimental.pallas import tpu as pltpu
from jax.sharding import Mesh
from jax.sharding import PartitionSpec as P

F32 = jnp.float32
BF = jnp.bfloat16
HX = ("grp", "hy", "hx")
GZ = ("grp", "seq")
HEAD = ("hy", "hx")
VM = pl.BlockSpec(memory_space=pltpu.VMEM)
SM = pl.BlockSpec(memory_space=pltpu.SMEM)
ANYWHERE = pl.BlockSpec(memory_space=pl.ANY)

ROOT_HALF = math.sqrt(0.5)

KEPT = [(k0, k1) for k0 in (1, 2, 3) for k1 in range(8)]
KEPT += [(0, k1) for k1 in range(5)] + [(4, k1) for k1 in range(4)]
NK = len(KEPT)


def dft_constants():
    m = np.arange(128)
    k = np.array([k0 + 8 * k1 for k0, k1 in KEPT])
    twist = np.exp(-2j * np.pi * np.outer(k, m) / 8192.0)
    weight = np.array([1.0 if kk in (0, 32) else 2.0 for kk in k]) / 8192.0
    back = np.conj(twist) * weight[:, None]
    inner = np.exp(-2j * np.pi * np.outer(m, m) / 128.0)
    c, s = inner.real, inner.imag
    forward = np.block([[c, s], [-s, c]])
    inverse = np.block([[c, -s], [s, c]])

    def split(mat):
        mat = jnp.asarray(mat, F32)
        hi = mat.astype(BF)
        lo = (mat - hi.astype(F32)).astype(BF)
        return jnp.stack([hi, lo])

    tw = np.stack([twist.real, twist.imag, back.real, back.imag]).astype(np.float32)
    return jnp.asarray(tw), split(forward), split(inverse)


def add_(a, b):
    if a is None:
        return b
    return a if b is None else a + b


def sub_(a, b):
    if b is None:
        return a
    return -b if a is None else a - b


def cadd(p, q):
    return (add_(p[0], q[0]), add_(p[1], q[1]))


def csub(p, q):
    return (sub_(p[0], q[0]), sub_(p[1], q[1]))


def scaled(a, by):
    if a is None or by == 0.0:
        return None
    return a if by == 1.0 else (-a if by == -1.0 else a * np.float32(by))


def turned(p, angle):
    eighth = angle / (math.pi / 4)
    near = round(eighth)
    re, im = p
    if abs(eighth - near) < 1e-9:
        near %= 8
        if near == 0:
            return p
        if near == 4:
            return (scaled(re, -1.0), scaled(im, -1.0))
        if near == 2:
            return (scaled(im, -1.0), re)
        if near == 6:
            return (im, scaled(re, -1.0))
        cc = ROOT_HALF if near in (1, 7) else -ROOT_HALF
        ss = ROOT_HALF if near in (1, 3) else -ROOT_HALF
        if re is not None and im is not None:
            if cc * ss > 0:
                return (scaled(re - im, cc), scaled(re + im, cc))
            return (scaled(re + im, cc), scaled(im - re, cc))
        return (sub_(scaled(re, cc), scaled(im, ss)), add_(scaled(re, ss), scaled(im, cc)))
    cc, ss = math.cos(angle), math.sin(angle)
    return (sub_(scaled(re, cc), scaled(im, ss)), add_(scaled(re, ss), scaled(im, cc)))


def dft_small(values, sign):
    count = len(values)
    if count == 1:
        return values
    even = dft_small(values[0::2], sign)
    odd = dft_small(values[1::2], sign)
    half = count // 2
    first, second = [], []
    for i in range(half):
        t = turned(odd[i], sign * 2 * math.pi * i / count)
        first.append(cadd(even[i], t))
        second.append(csub(even[i], t))
    return first + second


def outer_forward(x):
    c = np.float32(ROOT_HALF)
    cols = {k0: [] for k0 in range(5)}
    for b in range(8):
        x0, x1, x2, x3 = x[b], x[8 + b], x[16 + b], x[24 + b]
        e02, e13, d02 = x0 + x2, x1 + x3, x0 - x2
        cd, cs = c * (x1 - x3), c * e13
        part = {
            0: (e02 + e13, None),
            4: (e02 - e13, None),
            2: (d02, x3 - x1),
            1: (x0 + cd, -x2 - cs),
            3: (x0 - cd, x2 - cs),
        }
        for k0 in range(5):
            cols[k0].append(turned(part[k0], -2 * math.pi * b * k0 / 64))
    found = {k0: dft_small(cols[k0], -1) for k0 in range(5)}
    return [found[k0][k1] for k0, k1 in KEPT]


def outer_inverse(z):
    at = {kk: z[i] for i, kk in enumerate(KEPT)}
    zero = (None, None)
    grown = {}
    for k0 in (1, 2, 3):
        spread = dft_small([at[k0, k1] for k1 in range(8)], 1)
        grown[k0] = [turned(spread[b], 2 * math.pi * b * k0 / 64) for b in range(8)]
    real0 = dft_small([at[0, k1] if k1 < 5 else zero for k1 in range(8)], 1)
    spread4 = dft_small([at[4, k1] if k1 < 4 else zero for k1 in range(8)], 1)
    out = [None] * 32
    c = np.float32(ROOT_HALF)
    for b in range(8):
        r4 = turned(spread4[b], 2 * math.pi * b * 4 / 64)[0]
        g1, g2, g3 = grown[1][b], grown[2][b], grown[3][b]
        plus, minus = real0[b][0] + r4, real0[b][0] - r4
        out[b] = plus + g1[0] + g2[0] + g3[0]
        out[16 + b] = plus - g1[1] - g2[0] + g3[1]
        diag, anti = c * (g1[0] - g3[0]), c * (g1[1] + g3[1])
        out[8 + b] = minus + diag - anti - g2[1]
        out[24 + b] = minus - diag - anti + g2[1]
    return out


def store_split(hi_ref, lo_ref, k, rows, re, im):
    rh, ih = re.astype(BF), im.astype(BF)
    hi_ref[k, rows, 0:128] = rh
    hi_ref[k, rows, 128:256] = ih
    lo_ref[k, rows, 0:128] = (re - rh.astype(F32)).astype(BF)
    lo_ref[k, rows, 128:256] = (im - ih.astype(F32)).astype(BF)


def inner_product(hi_ref, lo_ref, mat_ref, out_ref):
    chans = hi_ref.shape[1]
    hi = hi_ref[...].reshape(NK * chans, 256)
    lo = lo_ref[...].reshape(NK * chans, 256)
    out = jnp.dot(hi, mat_ref[0], preferred_element_type=F32)
    out += jnp.dot(hi, mat_ref[1], preferred_element_type=F32)
    out += jnp.dot(lo, mat_ref[0], preferred_element_type=F32)
    out_ref[...] = out.reshape(NK, chans, 256)


def over_rows(chans, step):
    def one(part, carry):
        step(pl.ds(pl.multiple_of(part * 16, 16), 16))
        return carry

    lax.fori_loop(0, chans // 16, one, 0)


def forward_spectrum(read, tw_ref, fwd_ref, hi_ref, lo_ref, out_ref):
    def step(rows):
        outs = outer_forward([read(n, rows) for n in range(32)])
        for k in range(NK):
            re, im = outs[k]
            tr, ti = tw_ref[0, k : k + 1, :], tw_ref[1, k : k + 1, :]
            if im is None:
                store_split(hi_ref, lo_ref, k, rows, re * tr, re * ti)
            else:
                store_split(hi_ref, lo_ref, k, rows, re * tr - im * ti, re * ti + im * tr)

    over_rows(hi_ref.shape[1], step)
    inner_product(hi_ref, lo_ref, fwd_ref, out_ref)


def multiply_spectra(a_ref, b_ref, conj, hi_ref, lo_ref):
    chans = a_ref.shape[1]

    def one(k, carry):
        ar, ai = a_ref[k, :, 0:128], a_ref[k, :, 128:256]
        br, bi = b_ref[k, :, 0:128], b_ref[k, :, 128:256]
        if conj:
            re, im = ar * br + ai * bi, ar * bi - ai * br
        else:
            re, im = ar * br - ai * bi, ar * bi + ai * br
        store_split(hi_ref, lo_ref, k, slice(0, chans), re, im)
        return carry

    lax.fori_loop(0, NK, one, 0)


def inverse_field(hi_ref, lo_ref, inv_ref, tw_ref, mid_ref, write):
    inner_product(hi_ref, lo_ref, inv_ref, mid_ref)

    def step(rows):
        z = []
        for k in range(NK):
            re, im = mid_ref[k, rows, 0:128], mid_ref[k, rows, 128:256]
            tr, ti = tw_ref[2, k : k + 1, :], tw_ref[3, k : k + 1, :]
            z.append((re * tr - im * ti, re * ti + im * tr))
        out = outer_inverse(z)
        for n in range(32):
            write(n, rows, out[n])

    over_rows(hi_ref.shape[1], step)


def spec_scratch(chans):
    return [
        pltpu.VMEM((NK, chans, 256), BF),
        pltpu.VMEM((NK, chans, 256), BF),
        pltpu.VMEM((NK, chans, 256), F32),
    ]


def filter_kernel(scale, f_ref, tw_ref, fwd_ref, out_ref, hi, lo, mid):
    def read(n, rows):
        return f_ref[rows, n * 128 : n * 128 + 128] * np.float32(scale)

    forward_spectrum(read, tw_ref, fwd_ref, hi, lo, out_ref)


def filter_spectrum(filters, tables, scale):
    tw, fwd, _ = tables
    chans = filters.shape[0]
    return pl.pallas_call(
        functools.partial(filter_kernel, scale),
        out_shape=jax.ShapeDtypeStruct((NK, chans, 256), F32),
        in_specs=[VM] * 3,
        out_specs=VM,
        scratch_shapes=spec_scratch(chans),
        name="filter_spectrum",
    )(filters, tw, fwd)


def conv_kernel(conj, x_ref, h_ref, tw_ref, fwd_ref, inv_ref, out_ref, u_ref, hi, lo, mid):
    def read(n, rows):
        z, i = divmod(n, 4)
        return x_ref[z, i, rows, :].astype(F32)

    def write(n, rows, value):
        z, i = divmod(n, 4)
        out_ref[z, i, rows, :] = value.astype(BF)

    forward_spectrum(read, tw_ref, fwd_ref, hi, lo, u_ref)
    multiply_spectra(h_ref, u_ref, conj, hi, lo)
    inverse_field(hi, lo, inv_ref, tw_ref, mid, write)


def convolve(field, spec_h, tables, conj):
    tw, fwd, inv = tables
    chans = field.shape[2]
    return pl.pallas_call(
        functools.partial(conv_kernel, conj),
        out_shape=(
            jax.ShapeDtypeStruct((8, 4, chans, 128), BF),
            jax.ShapeDtypeStruct((NK, chans, 256), F32),
        ),
        in_specs=[VM] * 5,
        out_specs=(VM, VM),
        scratch_shapes=spec_scratch(chans),
        name="convolve_back" if conj else "convolve",
    )(field, spec_h, tw, fwd, inv)


def taps_kernel(scale, u_ref, d_ref, tw_ref, inv_ref, out_ref, hi, lo, mid):
    def write(n, rows, value):
        out_ref[rows, n * 128 : n * 128 + 128] = value * np.float32(scale)

    multiply_spectra(u_ref, d_ref, True, hi, lo)
    inverse_field(hi, lo, inv_ref, tw_ref, mid, write)


def taps_gradient(spec_u, spec_d, tables, scale):
    tw, _, inv = tables
    chans = spec_u.shape[1]
    return pl.pallas_call(
        functools.partial(taps_kernel, scale),
        out_shape=jax.ShapeDtypeStruct((chans, 4096), F32),
        in_specs=[VM] * 4,
        out_specs=VM,
        scratch_shapes=spec_scratch(chans),
        name="taps_gradient",
    )(spec_u, spec_d, tw, inv)


def to_blocks(rows, out_ref):
    for i in range(4):
        part = rows[i * 128 : i * 128 + 128, :].T.astype(BF)
        for z in range(8):
            out_ref[z, i] = part[z * 32 : z * 32 + 32, :]


def from_blocks(in_ref, t_ref):
    for z in range(8):
        for i in range(4):
            t_ref[z * 32 : z * 32 + 32, i * 128 : i * 128 + 128] = in_ref[z, i].astype(F32)
    return t_ref[...].T


def turned_place(y, x, dy, dx):
    return lax.rem(y + dy, 4) * 4 + lax.rem(x + dx, 4)


def feature_start(pos_ref, mine, k1, k2):
    g, y, x = pos_ref[0], pos_ref[1], pos_ref[2]
    owner = g if mine else 1 - g
    along_x = jnp.where(owner == 0, k1, k2)
    along_y = jnp.where(owner == 0, k2, k1)
    place = turned_place(y, x, 4 - along_y, 4 - along_x)
    return pl.multiple_of(place * 256 + owner * 128, 128)


def accumulate(pos_ref, blocks, marks, w_ref, acc_ref, transposed, buf_ref, sems):
    layers = 1 if transposed else 3

    def copies(k1):
        for i, (mine, k2) in enumerate(marks):
            start = feature_start(pos_ref, mine, k1, k2)
            part = pl.ds(i * 128, 128)
            for k in range(layers):
                if transposed:
                    src, dst = w_ref.at[:, pl.ds(start, 128)], buf_ref.at[k1, :, part]
                else:
                    src, dst = w_ref.at[k, pl.ds(start, 128), :], buf_ref.at[k1, k, part, :]
                yield pltpu.make_async_copy(src, dst, sems.at[k1, i * layers + k])

    def fetch(k1, carry):
        for copy in copies(k1):
            copy.start()
        return carry

    def one(k1, carry):
        left = jnp.concatenate([block[k1] for block in blocks], axis=1)
        for copy in copies(k1):
            copy.wait()
        if transposed:
            acc_ref[...] += lax.dot_general(
                left, buf_ref[k1], (((1,), (1,)), ((), ())), preferred_element_type=F32
            )
        else:
            for k in range(3):
                acc_ref[k] += jnp.dot(left, buf_ref[k1, k], preferred_element_type=F32)
        return carry

    lax.fori_loop(0, 4, fetch, 0)
    lax.fori_loop(0, 4, one, 0)


def project_kernel(marks, first, last, pos_ref, *refs):
    count = len(marks)
    blocks, refs = refs[:count], refs[count:]
    w_ref, refs = refs[0], refs[1:]
    if not first:
        before, refs = refs[0], refs[1:]
    buf_ref, sems = refs[-2:]
    acc_ref = refs[-3]
    acc_ref[...] = jnp.zeros_like(acc_ref) if first else before[...]
    accumulate(pos_ref, blocks, marks, w_ref, acc_ref, False, buf_ref, sems)
    if last:
        out_ref, car_ref = refs[0], refs[1]
        for k in range(3):
            out_ref[k] = acc_ref[k].astype(BF)

        @pl.when(pos_ref[0] == 1)
        def _():
            to_blocks(out_ref[0].astype(F32) * out_ref[1].astype(F32), car_ref)


def project_part(pos, blocks, marks, w, before, last):
    total = jax.ShapeDtypeStruct((3, 512, 256), F32)
    if last:
        shapes = (
            jax.ShapeDtypeStruct((3, 512, 256), BF),
            jax.ShapeDtypeStruct((8, 4, 32, 128), BF),
        )
    else:
        shapes = (total,)
    ins = [pos] + list(blocks) + [w] + ([] if before is None else [before])
    outs = pl.pallas_call(
        functools.partial(project_kernel, marks, before is None, last),
        out_shape=shapes,
        in_specs=[SM] + [VM] * len(blocks) + [ANYWHERE] + [VM] * (before is not None),
        out_specs=(VM,) * len(shapes),
        scratch_shapes=([pltpu.VMEM((3, 512, 256), F32)] if last else [])
        + [
            pltpu.VMEM((4, 3, 128 * len(marks), 256), BF),
            pltpu.SemaphoreType.DMA((4, 3 * len(marks))),
        ],
        cost_estimate=pl.CostEstimate(
            flops=2 * 512 * 512 * 768 * len(marks), bytes_accessed=3000000, transcendentals=0
        ),
        name="project_part",
    )(*ins)
    return outs if last else outs[0]


def gated_kernel(marks, first, last, pos_ref, *refs):
    @pl.when(pos_ref[0] == 1)
    def _():
        rest = refs
        blocks, rest = rest[: len(marks)], rest[len(marks) :]
        w_ref, rest = rest[0], rest[1:]
        if not first:
            before, rest = rest[0], rest[1:]
        buf_ref, sems = rest[-2:]
        acc_ref = rest[-3]
        acc_ref[...] = jnp.zeros_like(acc_ref) if first else before[...]
        accumulate(pos_ref, blocks, marks, w_ref, acc_ref, True, buf_ref, sems)
        if last:
            conv_ref, gate_ref, dconv_ref, dgate_ref = rest[:4]
            grad = acc_ref[...].astype(BF).astype(F32)
            dgate_ref[...] = (conv_ref[...].astype(F32) * grad).astype(BF)
            to_blocks(gate_ref[...].astype(F32) * grad, dconv_ref)


def gated_part(pos, blocks, marks, w, before, rows):
    last = rows is not None
    if last:
        shapes = (
            jax.ShapeDtypeStruct((8, 4, 32, 128), BF),
            jax.ShapeDtypeStruct((512, 256), BF),
        )
    else:
        shapes = (jax.ShapeDtypeStruct((512, 256), F32),)
    ins = [pos] + list(blocks) + [w] + ([] if before is None else [before])
    ins += list(rows) if last else []
    outs = pl.pallas_call(
        functools.partial(gated_kernel, marks, before is None, last),
        out_shape=shapes,
        in_specs=[SM]
        + [VM] * len(blocks)
        + [ANYWHERE]
        + [VM] * (len(ins) - len(blocks) - 2),
        out_specs=(VM,) * len(shapes),
        scratch_shapes=([pltpu.VMEM((512, 256), F32)] if last else [])
        + [
            pltpu.VMEM((4, 256, 128 * len(marks)), BF),
            pltpu.SemaphoreType.DMA((4, len(marks))),
        ],
        cost_estimate=pl.CostEstimate(
            flops=2 * 512 * 512 * 256 * len(marks), bytes_accessed=2000000, transcendentals=0
        ),
        name="gated_part",
    )(*ins)
    return outs if last else outs[0]


SCORE = 128 ** (-0.5) * math.log2(math.e)


def attend_kernel(first, last, steps, pos_ref, q_ref, *refs):
    kv = refs[: len(steps)]
    refs = refs[len(steps) :]
    if not first:
        m_in, l_in, a_in = refs[:3]
        refs = refs[3:]
    if last:
        out_ref, m_ref, l_ref, a_ref = refs
    else:
        m_ref, l_ref, a_ref = refs
    z = pos_ref[3]
    if not first:
        m_ref[...] = m_in[...]
        l_ref[...] = l_in[...]
        a_ref[...] = a_in[...]

    def block(kv_ref):
        def one(i, carry):
            h, part = i // 2, i % 2
            cols = pl.ds(pl.multiple_of(h * 128, 128), 128)
            rows = pl.ds(pl.multiple_of(part * 256, 256), 256)
            s = lax.dot_general(
                kv_ref[0, :, cols],
                q_ref[rows, cols],
                (((1,), (1,)), ((), ())),
                preferred_element_type=F32,
            ) * np.float32(SCORE)
            if first:
                key = lax.broadcasted_iota(jnp.int32, s.shape, 0)
                qry = lax.broadcasted_iota(jnp.int32, s.shape, 1) + part * 256
                s = jnp.where(key <= qry, s, np.float32(-1e30))
                top = jnp.max(s, axis=0, keepdims=True)
            else:
                old = m_ref[h, 0:1, rows]
                top = jnp.maximum(old, jnp.max(s, axis=0, keepdims=True))
            p = jnp.exp2(s - top)
            total = jnp.sum(p, axis=0, keepdims=True)
            prod = lax.dot_general(
                kv_ref[1, :, cols],
                p.astype(BF),
                (((0,), (0,)), ((), ())),
                preferred_element_type=F32,
            )
            if not first:
                fade = jnp.exp2(old - top)
                total += l_ref[h, 0:1, rows] * fade
                prod += a_ref[h, :, rows] * fade
            m_ref[h, 0:1, rows] = top
            l_ref[h, 0:1, rows] = total
            a_ref[h, :, rows] = prod
            return carry

        lax.fori_loop(0, 4, one, 0)

    for i, (step, forward) in enumerate(steps):
        if first:
            block(kv[i])
        else:
            pl.when(z >= step if forward else z + step >= 8)(functools.partial(block, kv[i]))

    if last:
        for h in range(2):
            done = a_ref[h] / l_ref[h, 0:1, :]
            out_ref[:, h * 128 : h * 128 + 128] = done.T.astype(BF)


def attend(pos, q, blocks, state, steps, last):
    first = state is None
    shapes = [
        jax.ShapeDtypeStruct((2, 8, 512), F32),
        jax.ShapeDtypeStruct((2, 8, 512), F32),
        jax.ShapeDtypeStruct((2, 128, 512), F32),
    ]
    scratch = []
    if last:
        scratch = [pltpu.VMEM(s.shape, s.dtype) for s in shapes]
        shapes = [jax.ShapeDtypeStruct((512, 256), BF)]
    ins = [pos, q] + list(blocks) + ([] if first else list(state))
    return pl.pallas_call(
        functools.partial(attend_kernel, first, last, steps),
        out_shape=tuple(shapes),
        in_specs=[SM] + [VM] * (len(ins) - 1),
        out_specs=tuple([VM] * len(shapes)),
        scratch_shapes=scratch,
        cost_estimate=pl.CostEstimate(
            flops=1000000000 * len(steps), bytes_accessed=1000000, transcendentals=500000
        ),
        name="attend",
    )(*ins)


def gate_kernel(in_ref, gate_ref, mixed_ref, conv_ref, t_ref):
    conv = from_blocks(in_ref, t_ref)
    conv_ref[...] = conv.astype(BF)
    mixed_ref[...] = (gate_ref[...].astype(F32) * conv).astype(BF)


def gate_rows(blocks, gate):
    shape = jax.ShapeDtypeStruct((512, 256), BF)
    return pl.pallas_call(
        gate_kernel,
        out_shape=(shape, shape),
        in_specs=[VM, VM],
        out_specs=(VM, VM),
        scratch_shapes=[pltpu.VMEM((256, 512), F32)],
        name="gate_rows",
    )(blocks, gate)


def spread_kernel(pos_ref, x_ref, w_ref, *outs):
    y, x = pos_ref[1], pos_ref[2]
    for d in (1, 3, 2, 0):
        for half in range(2):
            out_ref = outs[half * 4 + d]

            def two(i, carry, half=half, d=d, out_ref=out_ref):
                right = []
                for e in (2 * i, 2 * i + 1):
                    place = turned_place(y, x, *((e, d) if half == 0 else (d, e)))
                    start = pl.multiple_of(place * 256 + half * 128, 128)
                    right.append(w_ref[:, pl.ds(start, 128)])
                part = jnp.dot(
                    x_ref[...], jnp.concatenate(right, axis=1), preferred_element_type=F32
                ).astype(BF)
                out_ref[2 * i] = part[:, :128]
                out_ref[2 * i + 1] = part[:, 128:]
                return carry

            lax.fori_loop(0, 2, two, 0)


def spread_out(pos, mixed, w):
    shape = jax.ShapeDtypeStruct((4, 512, 128), BF)
    outs = pl.pallas_call(
        spread_kernel,
        out_shape=(shape,) * 8,
        in_specs=[SM, VM, VM],
        out_specs=(VM,) * 8,
        name="spread_out",
    )(pos, mixed, w)
    return outs[:4], outs[4:]


def rows_kernel(d_ref, rows_ref, dgate_ref, l_ref, t_ref):
    carried = from_blocks(d_ref, t_ref)
    l_ref[:, 0:256] = (carried * rows_ref[1].astype(F32)).astype(BF)
    l_ref[:, 256:512] = (carried * rows_ref[0].astype(F32)).astype(BF)
    l_ref[:, 512:768] = dgate_ref[...]


def gradient_rows(d_blocks, rows, d_gate):
    return pl.pallas_call(
        rows_kernel,
        out_shape=jax.ShapeDtypeStruct((512, 768), BF),
        in_specs=[VM] * 3,
        out_specs=VM,
        scratch_shapes=[pltpu.VMEM((256, 512), F32)],
        name="gradient_rows",
    )(d_blocks, rows, d_gate)


def piece_kernel(half, d, pos_ref, l_ref, w_ref, *refs):
    out_ref, buf_ref, sems = refs[-3:]
    y, x = pos_ref[1], pos_ref[2]

    if half == 1:

        @pl.when(pos_ref[0] == 0)
        def _():
            out_ref[...] = refs[0][...]

    def copies(e):
        place = turned_place(y, x, *((e, d) if half == 0 else (d, e)))
        start = pl.multiple_of(place * 256 + half * 128, 128)
        for k in range(3):
            yield pltpu.make_async_copy(
                w_ref.at[k, pl.ds(start, 128), :],
                buf_ref.at[pl.ds(e * 128, 128), pl.ds(k * 256, 256)],
                sems.at[e, k],
            )

    @pl.when(pos_ref[0] == 1)
    def _():
        for e in range(4):
            for copy in copies(e):
                copy.start()

        def two(i, carry):
            for e in (2 * i, 2 * i + 1):
                for copy in copies(e):
                    copy.wait()
            part = lax.dot_general(
                l_ref[...],
                buf_ref[pl.ds(pl.multiple_of(i * 256, 256), 256), :],
                (((1,), (1,)), ((), ())),
                preferred_element_type=F32,
            ).astype(BF)
            out_ref[2 * i] = part[:, :128]
            out_ref[2 * i + 1] = part[:, 128:]
            return carry

        lax.fori_loop(0, 2, two, 0)


def input_piece(pos, rows, w, half, d, under=None):
    ins = [pos, rows, w] + ([] if under is None else [under])
    return pl.pallas_call(
        functools.partial(piece_kernel, half, d),
        out_shape=jax.ShapeDtypeStruct((4, 512, 128), BF),
        in_specs=[SM, VM, ANYWHERE] + ([] if under is None else [VM]),
        out_specs=VM,
        scratch_shapes=[pltpu.VMEM((512, 768), BF), pltpu.SemaphoreType.DMA((4, 3))],
        cost_estimate=pl.CostEstimate(
            flops=2 * 512 * 768 * 512, bytes_accessed=2000000, transcendentals=0
        ),
        name="input_piece",
    )(*ins)


def blank_kernel(*refs):
    pass


def blank(pos, *shapes):
    return pl.pallas_call(
        blank_kernel,
        out_shape=tuple(jax.ShapeDtypeStruct(shape, kind) for shape, kind in shapes),
        in_specs=[SM],
        out_specs=(ANYWHERE,) * len(shapes),
        name="blank",
    )(pos)


def plane_pairs(axes, by):
    pairs = []
    for g in range(2):
        for y in range(4):
            for x in range(4):
                ty, tx = (y, (x + by) % 4) if axes[g] == "x" else ((y + by) % 4, x)
                pairs.append((g * 16 + y * 4 + x, g * 16 + ty * 4 + tx))
    return pairs


def along(value, axes, by):
    return lax.ppermute(value, HX, plane_pairs(axes, by))


def ring(value, by):
    return lax.ppermute(value, "seq", [(i, (i + by) % 8) for i in range(8)])


def swapped(value):
    return lax.ppermute(value, "grp", [(0, 1), (1, 0)])


def exchanged(value, axis):
    return lax.all_to_all(value, axis, 0, 0, tiled=True)


ORDER = (1, 3, 2)


def gather_product(half, step):
    near = {d: along(half, "xy", d) for d in ORDER}
    stack = jnp.stack([half] + [near[d] for d in (1, 2, 3)])
    mine = {d: along(stack, "yx", d) for d in ORDER}
    total = step((stack, swapped(stack)), ((True, 0), (False, 0)), None, False)
    for d in ORDER:
        mine[d], total = lax.optimization_barrier((mine[d], total))
    other = [swapped(mine[d]) for d in ORDER]
    total = step([mine[d] for d in ORDER], [(True, d) for d in ORDER], total, False)
    return step(other, [(False, d) for d in ORDER], total, True)


def added(first, others):
    total = first.astype(F32)
    for other in others:
        total += other.astype(F32)
    return total.astype(BF)


def scatter_features(a, b):
    ra = [along(a[d], "xx", d) for d in ORDER]
    rb = [along(b[d], "yy", d) for d in ORDER]
    sa, sb = added(a[0], ra), added(b[0], rb)
    ta = [along(sa[d], "yy", d) for d in ORDER]
    tb = [along(sb[d], "xx", d) for d in ORDER]
    return jnp.concatenate([added(sa[0], ta), added(sb[0], tb)], axis=1)


def scatter_input(pos, rows, w):
    pieces = {}
    for d in ORDER + (0,):
        pieces[d] = swapped(input_piece(pos, rows, w, 0, d))
    for d in ORDER + (0,):
        pieces[d] = input_piece(pos, rows, w, 1, d, pieces[d])
    row = added(pieces[0], [along(pieces[d], "xy", d) for d in ORDER])
    return added(row[0], [along(row[d], "yx", d) for d in ORDER])


def body(seq_in, w_proj, w_out, filters):
    g, y, x, z = (lax.axis_index(name) for name in ("grp", "hy", "hx", "seq"))
    teacher = g == 0
    pos = jnp.stack([g, y, x, z]).astype(jnp.int32)
    weights_in, weights_out = w_proj[0], w_out[0]
    length = 4096
    tap_scale = length ** (-0.5)
    tables = dft_constants()
    spec_shape = ((NK, 32, 256), F32)
    row_shape = ((512, 256), BF)

    half = lax.dynamic_slice_in_dim(seq_in, g * 128, 128, 1)

    def project(blocks, marks, before, last):
        return project_part(pos, blocks, marks, weights_in, before, last)

    rows, carried = gather_product(half, project)

    def teach(operands):
        rows, carried = operands
        q, pair = rows[0], rows[1:]
        moved = (ring(pair, 1), ring(pair, -1))
        state = attend(pos, q, [pair], None, [(0, True)], False)
        for step in range(1, 5):
            moved, state = lax.optimization_barrier((moved, state))
            blocks, steps = moved, [(step, True), (step, False)]
            if step < 3:
                moved = (ring(blocks[0], 1), ring(blocks[1], -1))
            elif step == 3:
                moved = (ring(blocks[0], 1),)
            else:
                steps = steps[:1]
            state = attend(pos, q, blocks, state, steps, step == 4)
        return (state[0],) + tuple(blank(pos, row_shape, spec_shape, spec_shape))

    def learn(operands):
        rows, carried = operands
        field = exchanged(carried, "seq")
        spec_h = filter_spectrum(filters, tables, tap_scale)
        conv, spec_u = convolve(field, spec_h, tables, False)
        mixed, conv_rows = gate_rows(exchanged(conv, "seq"), rows[2])
        return (mixed, conv_rows, spec_u, spec_h)

    mixed, conv_rows, spec_u, spec_h = lax.cond(teacher, teach, learn, (rows, carried))
    y_own = scatter_features(*spread_out(pos, mixed, weights_out))
    sent = jnp.where(teacher, y_own[:, 128:], y_own[:, :128])
    kept = jnp.where(teacher, y_own[:, :128], y_own[:, 128:])
    got = swapped(sent)
    low, high = kept.astype(F32), got.astype(F32)
    diff = jnp.where(teacher, high - low, low - high).astype(BF)

    def gated(blocks, marks, before, last):
        extra = (conv_rows, rows[2]) if last else None
        return gated_part(pos, blocks, marks, weights_out, before, extra)

    d_conv, d_gate = gather_product(diff, gated)

    def rest(operands):
        return tuple(blank(pos, ((512, 768), BF), ((32, 4096), F32)))

    def learn_back(operands):
        d_conv, d_gate, rows, spec_u, spec_h = operands
        d_field, spec_d = convolve(exchanged(d_conv, "seq"), spec_h, tables, True)
        d_blocks = exchanged(d_field, "seq")
        d_taps = taps_gradient(spec_u, spec_d, tables, tap_scale)
        return (gradient_rows(d_blocks, rows, d_gate), d_taps)

    d_rows, d_taps = lax.cond(
        teacher, rest, learn_back, (d_conv, d_gate, rows, spec_u, spec_h)
    )
    lower = swapped(d_taps[:, :2048].astype(BF)).astype(F32)
    sums = scatter_input(pos, d_rows, weights_in)
    d_input = jnp.concatenate([swapped(sums), sums], axis=1)
    paired = jnp.where(teacher, y_own, d_input)[None]
    grad_filters = jnp.where(teacher, lower, d_taps[:, 2048:])
    return (paired, grad_filters)


def solution(mesh):
    fine = Mesh(mesh.devices.reshape(2, 4, 4, 8), ("grp", "hy", "hx", "seq"))
    return jax.shard_map(
        body,
        mesh=fine,
        in_specs=(
            P("seq", HEAD),
            P("grp", None, None, HEAD),
            P("grp", HEAD, None),
            P(HEAD + ("seq",), None),
        ),
        out_specs=(P("grp", "seq", HEAD), P(HEAD + ("seq",), "grp")),
        check_vma=False,
    )
```

```python
import functools
import math

import jax
import jax.numpy as jnp
import numpy as np
from jax import lax
from jax.experimental import pallas as pl
from jax.experimental.pallas import tpu as pltpu
from jax.sharding import Mesh
from jax.sharding import PartitionSpec as P

F32 = jnp.float32
BF = jnp.bfloat16
HX = ("grp", "hy", "hx")
GZ = ("grp", "seq")
HEAD = ("hy", "hx")
VM = pl.BlockSpec(memory_space=pltpu.VMEM)
SM = pl.BlockSpec(memory_space=pltpu.SMEM)
ANYWHERE = pl.BlockSpec(memory_space=pl.ANY)

ROOT_HALF = math.sqrt(0.5)
MIB = 1 << 20


def grant(mib):
    return pltpu.CompilerParams(vmem_limit_bytes=mib * MIB)

KEPT = [(k0, k1) for k0 in (1, 2, 3) for k1 in range(8)]
KEPT += [(0, k1) for k1 in range(5)] + [(4, k1) for k1 in range(4)]
NK = len(KEPT)


def dft_constants():
    m = np.arange(128)
    k = np.array([k0 + 8 * k1 for k0, k1 in KEPT])
    twist = np.exp(-2j * np.pi * np.outer(k, m) / 8192.0)
    weight = np.array([1.0 if kk in (0, 32) else 2.0 for kk in k]) / 8192.0
    back = np.conj(twist) * weight[:, None]
    inner = np.exp(-2j * np.pi * np.outer(m, m) / 128.0)
    c, s = inner.real, inner.imag
    forward = np.block([[c, s], [-s, c]])
    inverse = np.block([[c, -s], [s, c]])

    def split(mat):
        mat = jnp.asarray(mat, F32)
        hi = mat.astype(BF)
        lo = (mat - hi.astype(F32)).astype(BF)
        return jnp.stack([hi, lo])

    tw = np.stack([twist.real, twist.imag, back.real, back.imag]).astype(np.float32)
    return jnp.asarray(tw), split(forward), split(inverse)


def add_(a, b):
    if a is None:
        return b
    return a if b is None else a + b


def sub_(a, b):
    if b is None:
        return a
    return -b if a is None else a - b


def cadd(p, q):
    return (add_(p[0], q[0]), add_(p[1], q[1]))


def csub(p, q):
    return (sub_(p[0], q[0]), sub_(p[1], q[1]))


def scaled(a, by):
    if a is None or by == 0.0:
        return None
    return a if by == 1.0 else (-a if by == -1.0 else a * np.float32(by))


def turned(p, angle):
    eighth = angle / (math.pi / 4)
    near = round(eighth)
    re, im = p
    if abs(eighth - near) < 1e-9:
        near %= 8
        if near == 0:
            return p
        if near == 4:
            return (scaled(re, -1.0), scaled(im, -1.0))
        if near == 2:
            return (scaled(im, -1.0), re)
        if near == 6:
            return (im, scaled(re, -1.0))
        cc = ROOT_HALF if near in (1, 7) else -ROOT_HALF
        ss = ROOT_HALF if near in (1, 3) else -ROOT_HALF
        if re is not None and im is not None:
            if cc * ss > 0:
                return (scaled(re - im, cc), scaled(re + im, cc))
            return (scaled(re + im, cc), scaled(im - re, cc))
        return (sub_(scaled(re, cc), scaled(im, ss)), add_(scaled(re, ss), scaled(im, cc)))
    cc, ss = math.cos(angle), math.sin(angle)
    return (sub_(scaled(re, cc), scaled(im, ss)), add_(scaled(re, ss), scaled(im, cc)))


def dft_small(values, sign):
    count = len(values)
    if count == 1:
        return values
    even = dft_small(values[0::2], sign)
    odd = dft_small(values[1::2], sign)
    half = count // 2
    first, second = [], []
    for i in range(half):
        t = turned(odd[i], sign * 2 * math.pi * i / count)
        first.append(cadd(even[i], t))
        second.append(csub(even[i], t))
    return first + second


def outer_forward(x):
    c = np.float32(ROOT_HALF)
    cols = {k0: [] for k0 in range(5)}
    for b in range(8):
        x0, x1, x2, x3 = x[b], x[8 + b], x[16 + b], x[24 + b]
        e02, e13, d02 = x0 + x2, x1 + x3, x0 - x2
        cd, cs = c * (x1 - x3), c * e13
        part = {
            0: (e02 + e13, None),
            4: (e02 - e13, None),
            2: (d02, x3 - x1),
            1: (x0 + cd, -x2 - cs),
            3: (x0 - cd, x2 - cs),
        }
        for k0 in range(5):
            cols[k0].append(turned(part[k0], -2 * math.pi * b * k0 / 64))
    found = {k0: dft_small(cols[k0], -1) for k0 in range(5)}
    return [found[k0][k1] for k0, k1 in KEPT]


def outer_inverse(z):
    at = {kk: z[i] for i, kk in enumerate(KEPT)}
    zero = (None, None)
    grown = {}
    for k0 in (1, 2, 3):
        spread = dft_small([at[k0, k1] for k1 in range(8)], 1)
        grown[k0] = [turned(spread[b], 2 * math.pi * b * k0 / 64) for b in range(8)]
    real0 = dft_small([at[0, k1] if k1 < 5 else zero for k1 in range(8)], 1)
    spread4 = dft_small([at[4, k1] if k1 < 4 else zero for k1 in range(8)], 1)
    out = [None] * 32
    c = np.float32(ROOT_HALF)
    for b in range(8):
        r4 = turned(spread4[b], 2 * math.pi * b * 4 / 64)[0]
        g1, g2, g3 = grown[1][b], grown[2][b], grown[3][b]
        plus, minus = real0[b][0] + r4, real0[b][0] - r4
        out[b] = plus + g1[0] + g2[0] + g3[0]
        out[16 + b] = plus - g1[1] - g2[0] + g3[1]
        diag, anti = c * (g1[0] - g3[0]), c * (g1[1] + g3[1])
        out[8 + b] = minus + diag - anti - g2[1]
        out[24 + b] = minus - diag - anti + g2[1]
    return out


def store_split(hi_ref, lo_ref, k, rows, re, im):
    rh, ih = re.astype(BF), im.astype(BF)
    hi_ref[k, rows, 0:128] = rh
    hi_ref[k, rows, 128:256] = ih
    lo_ref[k, rows, 0:128] = (re - rh.astype(F32)).astype(BF)
    lo_ref[k, rows, 128:256] = (im - ih.astype(F32)).astype(BF)


def inner_product(hi_ref, lo_ref, mat_ref, out_ref):
    chans = hi_ref.shape[1]
    hi = hi_ref[...].reshape(NK * chans, 256)
    lo = lo_ref[...].reshape(NK * chans, 256)
    out = jnp.dot(hi, mat_ref[0], preferred_element_type=F32)
    out += jnp.dot(hi, mat_ref[1], preferred_element_type=F32)
    out += jnp.dot(lo, mat_ref[0], preferred_element_type=F32)
    out_ref[...] = out.reshape(NK, chans, 256)


def over_rows(chans, step):
    def one(part, carry):
        step(pl.ds(pl.multiple_of(part * 16, 16), 16))
        return carry

    lax.fori_loop(0, chans // 16, one, 0)


def forward_spectrum(read, tw_ref, fwd_ref, hi_ref, lo_ref, out_ref):
    def step(rows):
        outs = outer_forward([read(n, rows) for n in range(32)])
        for k in range(NK):
            re, im = outs[k]
            tr, ti = tw_ref[0, k : k + 1, :], tw_ref[1, k : k + 1, :]
            if im is None:
                store_split(hi_ref, lo_ref, k, rows, re * tr, re * ti)
            else:
                store_split(hi_ref, lo_ref, k, rows, re * tr - im * ti, re * ti + im * tr)

    over_rows(hi_ref.shape[1], step)
    inner_product(hi_ref, lo_ref, fwd_ref, out_ref)


def multiply_spectra(a_ref, b_ref, conj, hi_ref, lo_ref):
    chans = a_ref.shape[1]

    def one(k, carry):
        ar, ai = a_ref[k, :, 0:128], a_ref[k, :, 128:256]
        br, bi = b_ref[k, :, 0:128], b_ref[k, :, 128:256]
        if conj:
            re, im = ar * br + ai * bi, ar * bi - ai * br
        else:
            re, im = ar * br - ai * bi, ar * bi + ai * br
        store_split(hi_ref, lo_ref, k, slice(0, chans), re, im)
        return carry

    lax.fori_loop(0, NK, one, 0)


def inverse_field(hi_ref, lo_ref, inv_ref, tw_ref, mid_ref, write):
    inner_product(hi_ref, lo_ref, inv_ref, mid_ref)

    def step(rows):
        z = []
        for k in range(NK):
            re, im = mid_ref[k, rows, 0:128], mid_ref[k, rows, 128:256]
            tr, ti = tw_ref[2, k : k + 1, :], tw_ref[3, k : k + 1, :]
            z.append((re * tr - im * ti, re * ti + im * tr))
        out = outer_inverse(z)
        for n in range(32):
            write(n, rows, out[n])

    over_rows(hi_ref.shape[1], step)


def spec_scratch(chans):
    return [
        pltpu.VMEM((NK, chans, 256), BF),
        pltpu.VMEM((NK, chans, 256), BF),
        pltpu.VMEM((NK, chans, 256), F32),
    ]


def filter_kernel(scale, f_ref, tw_ref, fwd_ref, out_ref, hi, lo, mid):
    def read(n, rows):
        return f_ref[rows, n * 128 : n * 128 + 128] * np.float32(scale)

    forward_spectrum(read, tw_ref, fwd_ref, hi, lo, out_ref)


def filter_spectrum(filters, tables, scale):
    tw, fwd, _ = tables
    chans = filters.shape[0]
    return pl.pallas_call(
        functools.partial(filter_kernel, scale),
        out_shape=jax.ShapeDtypeStruct((NK, chans, 256), F32),
        in_specs=[VM] * 3,
        out_specs=VM,
        scratch_shapes=spec_scratch(chans),
        compiler_params=grant(10),
        name="filter_spectrum",
    )(filters, tw, fwd)


def conv_kernel(conj, x_ref, h_ref, tw_ref, fwd_ref, inv_ref, out_ref, u_ref, hi, lo, mid):
    def read(n, rows):
        z, i = divmod(n, 4)
        return x_ref[z, i, rows, :].astype(F32)

    def write(n, rows, value):
        z, i = divmod(n, 4)
        out_ref[z, i, rows, :] = value.astype(BF)

    forward_spectrum(read, tw_ref, fwd_ref, hi, lo, u_ref)
    multiply_spectra(h_ref, u_ref, conj, hi, lo)
    inverse_field(hi, lo, inv_ref, tw_ref, mid, write)


def convolve(field, spec_h, tables, conj):
    tw, fwd, inv = tables
    chans = field.shape[2]
    return pl.pallas_call(
        functools.partial(conv_kernel, conj),
        out_shape=(
            jax.ShapeDtypeStruct((8, 4, chans, 128), BF),
            jax.ShapeDtypeStruct((NK, chans, 256), F32),
        ),
        in_specs=[VM] * 5,
        out_specs=(VM, VM),
        scratch_shapes=spec_scratch(chans),
        compiler_params=grant(12),
        name="convolve_back" if conj else "convolve",
    )(field, spec_h, tw, fwd, inv)


def taps_kernel(scale, u_ref, d_ref, tw_ref, inv_ref, out_ref, hi, lo, mid):
    def write(n, rows, value):
        out_ref[rows, n * 128 : n * 128 + 128] = value * np.float32(scale)

    multiply_spectra(u_ref, d_ref, True, hi, lo)
    inverse_field(hi, lo, inv_ref, tw_ref, mid, write)


def taps_gradient(spec_u, spec_d, tables, scale):
    tw, _, inv = tables
    chans = spec_u.shape[1]
    return pl.pallas_call(
        functools.partial(taps_kernel, scale),
        out_shape=jax.ShapeDtypeStruct((chans, 4096), F32),
        in_specs=[VM] * 4,
        out_specs=VM,
        scratch_shapes=spec_scratch(chans),
        compiler_params=grant(10),
        name="taps_gradient",
    )(spec_u, spec_d, tw, inv)


def to_blocks(rows, out_ref):
    for i in range(4):
        part = rows[i * 128 : i * 128 + 128, :].T.astype(BF)
        for z in range(8):
            out_ref[z, i] = part[z * 32 : z * 32 + 32, :]


def from_blocks(in_ref, t_ref):
    for z in range(8):
        for i in range(4):
            t_ref[z * 32 : z * 32 + 32, i * 128 : i * 128 + 128] = in_ref[z, i].astype(F32)
    return t_ref[...].T


def turned_place(y, x, dy, dx):
    return lax.rem(y + dy, 4) * 4 + lax.rem(x + dx, 4)


def feature_start(pos_ref, mine, k1, k2):
    g, y, x = pos_ref[0], pos_ref[1], pos_ref[2]
    owner = g if mine else 1 - g
    along_x = jnp.where(owner == 0, k1, k2)
    along_y = jnp.where(owner == 0, k2, k1)
    place = turned_place(y, x, 4 - along_y, 4 - along_x)
    return pl.multiple_of(place * 256 + owner * 128, 128)


def accumulate(pos_ref, blocks, marks, w_ref, acc_ref, transposed, buf_ref, sems):
    layers = 1 if transposed else 3

    def copies(k1):
        for i, (mine, k2) in enumerate(marks):
            start = feature_start(pos_ref, mine, k1, k2)
            part = pl.ds(i * 128, 128)
            for k in range(layers):
                if transposed:
                    src, dst = w_ref.at[:, pl.ds(start, 128)], buf_ref.at[k1, :, part]
                else:
                    src, dst = w_ref.at[k, pl.ds(start, 128), :], buf_ref.at[k1, k, part, :]
                yield pltpu.make_async_copy(src, dst, sems.at[k1, i * layers + k])

    def fetch(k1, carry):
        for copy in copies(k1):
            copy.start()
        return carry

    def one(k1, carry):
        left = jnp.concatenate([block[k1] for block in blocks], axis=1)
        for copy in copies(k1):
            copy.wait()
        if transposed:
            acc_ref[...] += lax.dot_general(
                left, buf_ref[k1], (((1,), (1,)), ((), ())), preferred_element_type=F32
            )
        else:
            for k in range(3):
                acc_ref[k] += jnp.dot(left, buf_ref[k1, k], preferred_element_type=F32)
        return carry

    lax.fori_loop(0, 4, fetch, 0)
    lax.fori_loop(0, 4, one, 0)


def project_kernel(marks, first, last, pos_ref, *refs):
    count = len(marks)
    blocks, refs = refs[:count], refs[count:]
    w_ref, refs = refs[0], refs[1:]
    if not first:
        before, refs = refs[0], refs[1:]
    buf_ref, sems = refs[-2:]
    acc_ref = refs[-3]
    acc_ref[...] = jnp.zeros_like(acc_ref) if first else before[...]
    accumulate(pos_ref, blocks, marks, w_ref, acc_ref, False, buf_ref, sems)
    if last:
        out_ref, car_ref = refs[0], refs[1]
        for k in range(3):
            out_ref[k] = acc_ref[k].astype(BF)

        @pl.when(pos_ref[0] == 1)
        def _():
            to_blocks(out_ref[0].astype(F32) * out_ref[1].astype(F32), car_ref)


def project_part(pos, blocks, marks, w, before, last):
    total = jax.ShapeDtypeStruct((3, 512, 256), F32)
    if last:
        shapes = (
            jax.ShapeDtypeStruct((3, 512, 256), BF),
            jax.ShapeDtypeStruct((8, 4, 32, 128), BF),
        )
    else:
        shapes = (total,)
    ins = [pos] + list(blocks) + [w] + ([] if before is None else [before])
    outs = pl.pallas_call(
        functools.partial(project_kernel, marks, before is None, last),
        out_shape=shapes,
        in_specs=[SM] + [VM] * len(blocks) + [ANYWHERE] + [VM] * (before is not None),
        out_specs=(VM,) * len(shapes),
        scratch_shapes=([pltpu.VMEM((3, 512, 256), F32)] if last else [])
        + [
            pltpu.VMEM((4, 3, 128 * len(marks), 256), BF),
            pltpu.SemaphoreType.DMA((4, 3 * len(marks))),
        ],
        cost_estimate=pl.CostEstimate(
            flops=2 * 512 * 512 * 768 * len(marks), bytes_accessed=3000000, transcendentals=0
        ),
        compiler_params=grant(24),
        name="project_part",
    )(*ins)
    return outs if last else outs[0]


def gated_kernel(marks, first, last, pos_ref, *refs):
    @pl.when(pos_ref[0] == 1)
    def _():
        rest = refs
        blocks, rest = rest[: len(marks)], rest[len(marks) :]
        w_ref, rest = rest[0], rest[1:]
        if not first:
            before, rest = rest[0], rest[1:]
        buf_ref, sems = rest[-2:]
        acc_ref = rest[-3]
        acc_ref[...] = jnp.zeros_like(acc_ref) if first else before[...]
        accumulate(pos_ref, blocks, marks, w_ref, acc_ref, True, buf_ref, sems)
        if last:
            conv_ref, gate_ref, dconv_ref, dgate_ref = rest[:4]
            grad = acc_ref[...].astype(BF).astype(F32)
            dgate_ref[...] = (conv_ref[...].astype(F32) * grad).astype(BF)
            to_blocks(gate_ref[...].astype(F32) * grad, dconv_ref)


def gated_part(pos, blocks, marks, w, before, rows):
    last = rows is not None
    if last:
        shapes = (
            jax.ShapeDtypeStruct((8, 4, 32, 128), BF),
            jax.ShapeDtypeStruct((512, 256), BF),
        )
    else:
        shapes = (jax.ShapeDtypeStruct((512, 256), F32),)
    ins = [pos] + list(blocks) + [w] + ([] if before is None else [before])
    ins += list(rows) if last else []
    outs = pl.pallas_call(
        functools.partial(gated_kernel, marks, before is None, last),
        out_shape=shapes,
        in_specs=[SM]
        + [VM] * len(blocks)
        + [ANYWHERE]
        + [VM] * (len(ins) - len(blocks) - 2),
        out_specs=(VM,) * len(shapes),
        scratch_shapes=([pltpu.VMEM((512, 256), F32)] if last else [])
        + [
            pltpu.VMEM((4, 256, 128 * len(marks)), BF),
            pltpu.SemaphoreType.DMA((4, len(marks))),
        ],
        cost_estimate=pl.CostEstimate(
            flops=2 * 512 * 512 * 256 * len(marks), bytes_accessed=2000000, transcendentals=0
        ),
        compiler_params=grant(12),
        name="gated_part",
    )(*ins)
    return outs if last else outs[0]


SCORE = 128 ** (-0.5) * math.log2(math.e)


def attend_kernel(first, last, steps, pos_ref, q_ref, *refs):
    kv = refs[: len(steps)]
    refs = refs[len(steps) :]
    if not first:
        m_in, l_in, a_in = refs[:3]
        refs = refs[3:]
    if last:
        out_ref, m_ref, l_ref, a_ref = refs
    else:
        m_ref, l_ref, a_ref = refs
    z = pos_ref[3]
    if not first:
        m_ref[...] = m_in[...]
        l_ref[...] = l_in[...]
        a_ref[...] = a_in[...]

    def block(kv_ref):
        def one(i, carry):
            h, part = i // 2, i % 2
            cols = pl.ds(pl.multiple_of(h * 128, 128), 128)
            rows = pl.ds(pl.multiple_of(part * 256, 256), 256)
            s = lax.dot_general(
                kv_ref[0, :, cols],
                q_ref[rows, cols],
                (((1,), (1,)), ((), ())),
                preferred_element_type=F32,
            ) * np.float32(SCORE)
            if first:
                key = lax.broadcasted_iota(jnp.int32, s.shape, 0)
                qry = lax.broadcasted_iota(jnp.int32, s.shape, 1) + part * 256
                s = jnp.where(key <= qry, s, np.float32(-1e30))
                top = jnp.max(s, axis=0, keepdims=True)
            else:
                old = m_ref[h, 0:1, rows]
                top = jnp.maximum(old, jnp.max(s, axis=0, keepdims=True))
            p = jnp.exp2(s - top)
            total = jnp.sum(p, axis=0, keepdims=True)
            prod = lax.dot_general(
                kv_ref[1, :, cols],
                p.astype(BF),
                (((0,), (0,)), ((), ())),
                preferred_element_type=F32,
            )
            if not first:
                fade = jnp.exp2(old - top)
                total += l_ref[h, 0:1, rows] * fade
                prod += a_ref[h, :, rows] * fade
            m_ref[h, 0:1, rows] = top
            l_ref[h, 0:1, rows] = total
            a_ref[h, :, rows] = prod
            return carry

        lax.fori_loop(0, 4, one, 0)

    for i, (step, forward) in enumerate(steps):
        if first:
            block(kv[i])
        else:
            pl.when(z >= step if forward else z + step >= 8)(functools.partial(block, kv[i]))

    if last:
        for h in range(2):
            done = a_ref[h] / l_ref[h, 0:1, :]
            out_ref[:, h * 128 : h * 128 + 128] = done.T.astype(BF)


def attend(pos, q, blocks, state, steps, last):
    first = state is None
    shapes = [
        jax.ShapeDtypeStruct((2, 8, 512), F32),
        jax.ShapeDtypeStruct((2, 8, 512), F32),
        jax.ShapeDtypeStruct((2, 128, 512), F32),
    ]
    scratch = []
    if last:
        scratch = [pltpu.VMEM(s.shape, s.dtype) for s in shapes]
        shapes = [jax.ShapeDtypeStruct((512, 256), BF)]
    ins = [pos, q] + list(blocks) + ([] if first else list(state))
    return pl.pallas_call(
        functools.partial(attend_kernel, first, last, steps),
        out_shape=tuple(shapes),
        in_specs=[SM] + [VM] * (len(ins) - 1),
        out_specs=tuple([VM] * len(shapes)),
        scratch_shapes=scratch,
        cost_estimate=pl.CostEstimate(
            flops=1000000000 * len(steps), bytes_accessed=1000000, transcendentals=500000
        ),
        compiler_params=grant(14),
        name="attend",
    )(*ins)


def gate_kernel(in_ref, gate_ref, mixed_ref, conv_ref, t_ref):
    conv = from_blocks(in_ref, t_ref)
    conv_ref[...] = conv.astype(BF)
    mixed_ref[...] = (gate_ref[...].astype(F32) * conv).astype(BF)


def gate_rows(blocks, gate):
    shape = jax.ShapeDtypeStruct((512, 256), BF)
    return pl.pallas_call(
        gate_kernel,
        out_shape=(shape, shape),
        in_specs=[VM, VM],
        out_specs=(VM, VM),
        scratch_shapes=[pltpu.VMEM((256, 512), F32)],
        compiler_params=grant(4),
        name="gate_rows",
    )(blocks, gate)


def spread_kernel(pos_ref, x_ref, w_ref, *outs):
    y, x = pos_ref[1], pos_ref[2]
    a_refs, b_refs = outs[:4], outs[4:]
    for dx in range(4):
        for dy in range(4):
            cols = pl.ds(pl.multiple_of(turned_place(y, x, dy, dx) * 256, 256), 256)
            part = jnp.dot(x_ref[...], w_ref[:, cols], preferred_element_type=F32).astype(BF)
            a_refs[dx][dy] = part[:, :128]
            b_refs[dy][dx] = part[:, 128:]


def spread_out(pos, mixed, w):
    shape = jax.ShapeDtypeStruct((4, 512, 128), BF)
    outs = pl.pallas_call(
        spread_kernel,
        out_shape=(shape,) * 8,
        in_specs=[SM, VM, VM],
        out_specs=(VM,) * 8,
        compiler_params=grant(10),
        name="spread_out",
    )(pos, mixed, w)
    return outs[:4], outs[4:]


def rows_kernel(d_ref, rows_ref, dgate_ref, l_ref, t_ref):
    carried = from_blocks(d_ref, t_ref)
    l_ref[:, 0:256] = (carried * rows_ref[1].astype(F32)).astype(BF)
    l_ref[:, 256:512] = (carried * rows_ref[0].astype(F32)).astype(BF)
    l_ref[:, 512:768] = dgate_ref[...]


def gradient_rows(d_blocks, rows, d_gate):
    return pl.pallas_call(
        rows_kernel,
        out_shape=jax.ShapeDtypeStruct((512, 768), BF),
        in_specs=[VM] * 3,
        out_specs=VM,
        scratch_shapes=[pltpu.VMEM((256, 512), F32)],
        compiler_params=grant(5),
        name="gradient_rows",
    )(d_blocks, rows, d_gate)


def piece_kernel(half, d, pos_ref, l_ref, w_ref, *refs):
    out_ref, buf_ref, sems = refs[-3:]
    y, x = pos_ref[1], pos_ref[2]

    if half == 1:

        @pl.when(pos_ref[0] == 0)
        def _():
            out_ref[...] = refs[0][...]

    def copies(e):
        place = turned_place(y, x, *((e, d) if half == 0 else (d, e)))
        start = pl.multiple_of(place * 256 + half * 128, 128)
        for k in range(3):
            yield pltpu.make_async_copy(
                w_ref.at[k, pl.ds(start, 128), :],
                buf_ref.at[pl.ds(e * 128, 128), pl.ds(k * 256, 256)],
                sems.at[e, k],
            )

    @pl.when(pos_ref[0] == 1)
    def _():
        for e in range(4):
            for copy in copies(e):
                copy.start()

        def two(i, carry):
            for e in (2 * i, 2 * i + 1):
                for copy in copies(e):
                    copy.wait()
            part = lax.dot_general(
                l_ref[...],
                buf_ref[pl.ds(pl.multiple_of(i * 256, 256), 256), :],
                (((1,), (1,)), ((), ())),
                preferred_element_type=F32,
            ).astype(BF)
            out_ref[2 * i] = part[:, :128]
            out_ref[2 * i + 1] = part[:, 128:]
            return carry

        lax.fori_loop(0, 2, two, 0)


def input_piece(pos, rows, w, half, d, under=None):
    ins = [pos, rows, w] + ([] if under is None else [under])
    return pl.pallas_call(
        functools.partial(piece_kernel, half, d),
        out_shape=jax.ShapeDtypeStruct((4, 512, 128), BF),
        in_specs=[SM, VM, ANYWHERE] + ([] if under is None else [VM]),
        out_specs=VM,
        scratch_shapes=[pltpu.VMEM((512, 768), BF), pltpu.SemaphoreType.DMA((4, 3))],
        cost_estimate=pl.CostEstimate(
            flops=2 * 512 * 768 * 512, bytes_accessed=2000000, transcendentals=0
        ),
        compiler_params=grant(8),
        name="input_piece",
    )(*ins)


def blank_kernel(*refs):
    pass


def blank(pos, *shapes):
    return pl.pallas_call(
        blank_kernel,
        out_shape=tuple(jax.ShapeDtypeStruct(shape, kind) for shape, kind in shapes),
        in_specs=[SM],
        out_specs=(ANYWHERE,) * len(shapes),
        compiler_params=grant(1),
        name="blank",
    )(pos)


def plane_pairs(axes, by):
    pairs = []
    for g in range(2):
        for y in range(4):
            for x in range(4):
                ty, tx = (y, (x + by) % 4) if axes[g] == "x" else ((y + by) % 4, x)
                pairs.append((g * 16 + y * 4 + x, g * 16 + ty * 4 + tx))
    return pairs


def along(value, axes, by):
    return lax.ppermute(value, HX, plane_pairs(axes, by))


def ring(value, by):
    return lax.ppermute(value, "seq", [(i, (i + by) % 8) for i in range(8)])


def swapped(value):
    return lax.ppermute(value, "grp", [(0, 1), (1, 0)])


def exchanged(value, axis):
    return lax.all_to_all(value, axis, 0, 0, tiled=True)


ORDER = (1, 3, 2)


def gather_product(half, step):
    near = {d: along(half, "xy", d) for d in ORDER}
    stack = jnp.stack([half] + [near[d] for d in (1, 2, 3)])
    mine = {d: along(stack, "yx", d) for d in ORDER}
    total = step((stack, swapped(stack)), ((True, 0), (False, 0)), None, False)
    for d in ORDER:
        mine[d], total = lax.optimization_barrier((mine[d], total))
    other = [swapped(mine[d]) for d in ORDER]
    total = step([mine[d] for d in ORDER], [(True, d) for d in ORDER], total, False)
    return step(other, [(False, d) for d in ORDER], total, True)


def added(first, others):
    total = first.astype(F32)
    for other in others:
        total += other.astype(F32)
    return total.astype(BF)


def scatter_features(a, b):
    ra = [along(a[d], "xx", d) for d in ORDER]
    rb = [along(b[d], "yy", d) for d in ORDER]
    sa, sb = added(a[0], ra), added(b[0], rb)
    ta = [along(sa[d], "yy", d) for d in ORDER]
    tb = [along(sb[d], "xx", d) for d in ORDER]
    return jnp.concatenate([added(sa[0], ta), added(sb[0], tb)], axis=1)


def scatter_input(pos, rows, w):
    pieces = {}
    for d in ORDER + (0,):
        pieces[d] = swapped(input_piece(pos, rows, w, 0, d))
    for d in ORDER + (0,):
        pieces[d] = input_piece(pos, rows, w, 1, d, pieces[d])
    row = added(pieces[0], [along(pieces[d], "xy", d) for d in ORDER])
    return added(row[0], [along(row[d], "yx", d) for d in ORDER])


def body(seq_in, w_proj, w_out, filters):
    g, y, x, z = (lax.axis_index(name) for name in ("grp", "hy", "hx", "seq"))
    teacher = g == 0
    pos = jnp.stack([g, y, x, z]).astype(jnp.int32)
    weights_in, weights_out = w_proj[0], w_out[0]
    length = 4096
    tap_scale = length ** (-0.5)
    tables = dft_constants()
    spec_shape = ((NK, 32, 256), F32)
    row_shape = ((512, 256), BF)

    half = lax.dynamic_slice_in_dim(seq_in, g * 128, 128, 1)

    def project(blocks, marks, before, last):
        return project_part(pos, blocks, marks, weights_in, before, last)

    rows, carried = gather_product(half, project)

    def teach(operands):
        rows, carried = operands
        q, pair = rows[0], rows[1:]
        moved = (ring(pair, 1), ring(pair, -1))
        state = attend(pos, q, [pair], None, [(0, True)], False)
        for step in range(1, 5):
            moved, state = lax.optimization_barrier((moved, state))
            blocks, steps = moved, [(step, True), (step, False)]
            if step < 3:
                moved = (ring(blocks[0], 1), ring(blocks[1], -1))
            elif step == 3:
                moved = (ring(blocks[0], 1),)
            else:
                steps = steps[:1]
            state = attend(pos, q, blocks, state, steps, step == 4)
        return (state[0],) + tuple(blank(pos, row_shape, spec_shape, spec_shape))

    def learn(operands):
        rows, carried = operands
        field = exchanged(carried, "seq")
        spec_h = filter_spectrum(filters, tables, tap_scale)
        conv, spec_u = convolve(field, spec_h, tables, False)
        mixed, conv_rows = gate_rows(exchanged(conv, "seq"), rows[2])
        return (mixed, conv_rows, spec_u, spec_h)

    mixed, conv_rows, spec_u, spec_h = lax.cond(teacher, teach, learn, (rows, carried))
    y_own = scatter_features(*spread_out(pos, mixed, weights_out))
    sent = jnp.where(teacher, y_own[:, 128:], y_own[:, :128])
    kept = jnp.where(teacher, y_own[:, :128], y_own[:, 128:])
    got = swapped(sent)
    low, high = kept.astype(F32), got.astype(F32)
    diff = jnp.where(teacher, high - low, low - high).astype(BF)

    def gated(blocks, marks, before, last):
        extra = (conv_rows, rows[2]) if last else None
        return gated_part(pos, blocks, marks, weights_out, before, extra)

    d_conv, d_gate = gather_product(diff, gated)

    def rest(operands):
        return tuple(blank(pos, ((512, 768), BF), ((32, 4096), F32)))

    def learn_back(operands):
        d_conv, d_gate, rows, spec_u, spec_h = operands
        d_field, spec_d = convolve(exchanged(d_conv, "seq"), spec_h, tables, True)
        d_blocks = exchanged(d_field, "seq")
        d_taps = taps_gradient(spec_u, spec_d, tables, tap_scale)
        return (gradient_rows(d_blocks, rows, d_gate), d_taps)

    d_rows, d_taps = lax.cond(
        teacher, rest, learn_back, (d_conv, d_gate, rows, spec_u, spec_h)
    )
    lower = swapped(d_taps[:, :2048].astype(BF)).astype(F32)
    sums = scatter_input(pos, d_rows, weights_in)
    d_input = jnp.concatenate([swapped(sums), sums], axis=1)
    paired = jnp.where(teacher, y_own, d_input)[None]
    grad_filters = jnp.where(teacher, lower, d_taps[:, 2048:])
    return (paired, grad_filters)


def solution(mesh):
    fine = Mesh(mesh.devices.reshape(2, 4, 4, 8), ("grp", "hy", "hx", "seq"))
    return jax.shard_map(
        body,
        mesh=fine,
        in_specs=(
            P("seq", HEAD),
            P("grp", None, None, HEAD),
            P("grp", HEAD, None),
            P(HEAD + ("seq",), None),
        ),
        out_specs=(P("grp", "seq", HEAD), P(HEAD + ("seq",), "grp")),
        check_vma=False,
    )
```

```python
import functools
import math

import jax
import jax.numpy as jnp
import numpy as np
from jax import lax
from jax.experimental import pallas as pl
from jax.experimental.pallas import tpu as pltpu
from jax.sharding import Mesh
from jax.sharding import PartitionSpec as P

F32 = jnp.float32
BF = jnp.bfloat16
HX = ("grp", "hy", "hx")
GZ = ("grp", "seq")
HEAD = ("hy", "hx")
VM = pl.BlockSpec(memory_space=pltpu.VMEM)
SM = pl.BlockSpec(memory_space=pltpu.SMEM)
ANYWHERE = pl.BlockSpec(memory_space=pl.ANY)
IN_HBM = pl.BlockSpec(memory_space=pltpu.HBM)

ROOT_HALF = math.sqrt(0.5)
MIB = 1 << 20


def grant(mib):
    return pltpu.CompilerParams(vmem_limit_bytes=mib * MIB)

KEPT = [(k0, k1) for k0 in (1, 2, 3) for k1 in range(8)]
KEPT += [(0, k1) for k1 in range(5)] + [(4, k1) for k1 in range(4)]
NK = len(KEPT)


def dft_constants():
    m = np.arange(128)
    k = np.array([k0 + 8 * k1 for k0, k1 in KEPT])
    twist = np.exp(-2j * np.pi * np.outer(k, m) / 8192.0)
    weight = np.array([1.0 if kk in (0, 32) else 2.0 for kk in k]) / 8192.0
    back = np.conj(twist) * weight[:, None]
    inner = np.exp(-2j * np.pi * np.outer(m, m) / 128.0)
    c, s = inner.real, inner.imag
    forward = np.block([[c, s], [-s, c]])
    inverse = np.block([[c, -s], [s, c]])

    def split(mat):
        mat = jnp.asarray(mat, F32)
        hi = mat.astype(BF)
        lo = (mat - hi.astype(F32)).astype(BF)
        return jnp.stack([hi, lo])

    tw = np.stack([twist.real, twist.imag, back.real, back.imag]).astype(np.float32)
    return jnp.asarray(tw), split(forward), split(inverse)


def add_(a, b):
    if a is None:
        return b
    return a if b is None else a + b


def sub_(a, b):
    if b is None:
        return a
    return -b if a is None else a - b


def cadd(p, q):
    return (add_(p[0], q[0]), add_(p[1], q[1]))


def csub(p, q):
    return (sub_(p[0], q[0]), sub_(p[1], q[1]))


def scaled(a, by):
    if a is None or by == 0.0:
        return None
    return a if by == 1.0 else (-a if by == -1.0 else a * np.float32(by))


def turned(p, angle):
    eighth = angle / (math.pi / 4)
    near = round(eighth)
    re, im = p
    if abs(eighth - near) < 1e-9:
        near %= 8
        if near == 0:
            return p
        if near == 4:
            return (scaled(re, -1.0), scaled(im, -1.0))
        if near == 2:
            return (scaled(im, -1.0), re)
        if near == 6:
            return (im, scaled(re, -1.0))
        cc = ROOT_HALF if near in (1, 7) else -ROOT_HALF
        ss = ROOT_HALF if near in (1, 3) else -ROOT_HALF
        if re is not None and im is not None:
            if cc * ss > 0:
                return (scaled(re - im, cc), scaled(re + im, cc))
            return (scaled(re + im, cc), scaled(im - re, cc))
        return (sub_(scaled(re, cc), scaled(im, ss)), add_(scaled(re, ss), scaled(im, cc)))
    cc, ss = math.cos(angle), math.sin(angle)
    return (sub_(scaled(re, cc), scaled(im, ss)), add_(scaled(re, ss), scaled(im, cc)))


def dft_small(values, sign):
    count = len(values)
    if count == 1:
        return values
    even = dft_small(values[0::2], sign)
    odd = dft_small(values[1::2], sign)
    half = count // 2
    first, second = [], []
    for i in range(half):
        t = turned(odd[i], sign * 2 * math.pi * i / count)
        first.append(cadd(even[i], t))
        second.append(csub(even[i], t))
    return first + second


def outer_forward(x):
    c = np.float32(ROOT_HALF)
    cols = {k0: [] for k0 in range(5)}
    for b in range(8):
        x0, x1, x2, x3 = x[b], x[8 + b], x[16 + b], x[24 + b]
        e02, e13, d02 = x0 + x2, x1 + x3, x0 - x2
        cd, cs = c * (x1 - x3), c * e13
        part = {
            0: (e02 + e13, None),
            4: (e02 - e13, None),
            2: (d02, x3 - x1),
            1: (x0 + cd, -x2 - cs),
            3: (x0 - cd, x2 - cs),
        }
        for k0 in range(5):
            cols[k0].append(turned(part[k0], -2 * math.pi * b * k0 / 64))
    found = {k0: dft_small(cols[k0], -1) for k0 in range(5)}
    return [found[k0][k1] for k0, k1 in KEPT]


def outer_inverse(z):
    at = {kk: z[i] for i, kk in enumerate(KEPT)}
    zero = (None, None)
    grown = {}
    for k0 in (1, 2, 3):
        spread = dft_small([at[k0, k1] for k1 in range(8)], 1)
        grown[k0] = [turned(spread[b], 2 * math.pi * b * k0 / 64) for b in range(8)]
    real0 = dft_small([at[0, k1] if k1 < 5 else zero for k1 in range(8)], 1)
    spread4 = dft_small([at[4, k1] if k1 < 4 else zero for k1 in range(8)], 1)
    out = [None] * 32
    c = np.float32(ROOT_HALF)
    for b in range(8):
        r4 = turned(spread4[b], 2 * math.pi * b * 4 / 64)[0]
        g1, g2, g3 = grown[1][b], grown[2][b], grown[3][b]
        plus, minus = real0[b][0] + r4, real0[b][0] - r4
        out[b] = plus + g1[0] + g2[0] + g3[0]
        out[16 + b] = plus - g1[1] - g2[0] + g3[1]
        diag, anti = c * (g1[0] - g3[0]), c * (g1[1] + g3[1])
        out[8 + b] = minus + diag - anti - g2[1]
        out[24 + b] = minus - diag - anti + g2[1]
    return out


def store_split(hi_ref, lo_ref, k, rows, re, im):
    rh, ih = re.astype(BF), im.astype(BF)
    hi_ref[k, rows, 0:128] = rh
    hi_ref[k, rows, 128:256] = ih
    lo_ref[k, rows, 0:128] = (re - rh.astype(F32)).astype(BF)
    lo_ref[k, rows, 128:256] = (im - ih.astype(F32)).astype(BF)


def inner_product(hi_ref, lo_ref, mat_ref, out_ref):
    chans = hi_ref.shape[1]
    hi = hi_ref[...].reshape(NK * chans, 256)
    lo = lo_ref[...].reshape(NK * chans, 256)
    out = jnp.dot(hi, mat_ref[0], preferred_element_type=F32)
    out += jnp.dot(hi, mat_ref[1], preferred_element_type=F32)
    out += jnp.dot(lo, mat_ref[0], preferred_element_type=F32)
    out_ref[...] = out.reshape(NK, chans, 256)


def over_rows(chans, step):
    def one(part, carry):
        step(pl.ds(pl.multiple_of(part * 16, 16), 16))
        return carry

    lax.fori_loop(0, chans // 16, one, 0)


def forward_spectrum(read, tw_ref, fwd_ref, hi_ref, lo_ref, out_ref):
    def step(rows):
        outs = outer_forward([read(n, rows) for n in range(32)])
        for k in range(NK):
            re, im = outs[k]
            tr, ti = tw_ref[0, k : k + 1, :], tw_ref[1, k : k + 1, :]
            if im is None:
                store_split(hi_ref, lo_ref, k, rows, re * tr, re * ti)
            else:
                store_split(hi_ref, lo_ref, k, rows, re * tr - im * ti, re * ti + im * tr)

    over_rows(hi_ref.shape[1], step)
    inner_product(hi_ref, lo_ref, fwd_ref, out_ref)


def multiply_spectra(a_ref, b_ref, conj, hi_ref, lo_ref):
    chans = a_ref.shape[1]

    def one(k, carry):
        ar, ai = a_ref[k, :, 0:128], a_ref[k, :, 128:256]
        br, bi = b_ref[k, :, 0:128], b_ref[k, :, 128:256]
        if conj:
            re, im = ar * br + ai * bi, ar * bi - ai * br
        else:
            re, im = ar * br - ai * bi, ar * bi + ai * br
        store_split(hi_ref, lo_ref, k, slice(0, chans), re, im)
        return carry

    lax.fori_loop(0, NK, one, 0)


def inverse_field(hi_ref, lo_ref, inv_ref, tw_ref, mid_ref, write):
    inner_product(hi_ref, lo_ref, inv_ref, mid_ref)

    def step(rows):
        z = []
        for k in range(NK):
            re, im = mid_ref[k, rows, 0:128], mid_ref[k, rows, 128:256]
            tr, ti = tw_ref[2, k : k + 1, :], tw_ref[3, k : k + 1, :]
            z.append((re * tr - im * ti, re * ti + im * tr))
        out = outer_inverse(z)
        for n in range(32):
            write(n, rows, out[n])

    over_rows(hi_ref.shape[1], step)


def spec_scratch(chans):
    return [
        pltpu.VMEM((NK, chans, 256), BF),
        pltpu.VMEM((NK, chans, 256), BF),
        pltpu.VMEM((NK, chans, 256), F32),
    ]


def filter_kernel(scale, f_ref, tw_ref, fwd_ref, out_ref, hi, lo, mid):
    def read(n, rows):
        return f_ref[rows, n * 128 : n * 128 + 128] * np.float32(scale)

    forward_spectrum(read, tw_ref, fwd_ref, hi, lo, out_ref)


def filter_spectrum(filters, tables, scale):
    tw, fwd, _ = tables
    chans = filters.shape[0]
    return pl.pallas_call(
        functools.partial(filter_kernel, scale),
        out_shape=jax.ShapeDtypeStruct((NK, chans, 256), F32),
        in_specs=[VM] * 3,
        out_specs=VM,
        scratch_shapes=spec_scratch(chans),
        compiler_params=grant(10),
        name="filter_spectrum",
    )(filters, tw, fwd)


def conv_kernel(conj, x_ref, h_ref, tw_ref, fwd_ref, inv_ref, out_ref, u_ref, hi, lo, mid):
    def read(n, rows):
        z, i = divmod(n, 4)
        return x_ref[z, i, rows, :].astype(F32)

    def write(n, rows, value):
        z, i = divmod(n, 4)
        out_ref[z, i, rows, :] = value.astype(BF)

    forward_spectrum(read, tw_ref, fwd_ref, hi, lo, u_ref)
    multiply_spectra(h_ref, u_ref, conj, hi, lo)
    inverse_field(hi, lo, inv_ref, tw_ref, mid, write)


def convolve(field, spec_h, tables, conj):
    tw, fwd, inv = tables
    chans = field.shape[2]
    return pl.pallas_call(
        functools.partial(conv_kernel, conj),
        out_shape=(
            jax.ShapeDtypeStruct((8, 4, chans, 128), BF),
            jax.ShapeDtypeStruct((NK, chans, 256), F32),
        ),
        in_specs=[VM] * 5,
        out_specs=(VM, VM),
        scratch_shapes=spec_scratch(chans),
        compiler_params=grant(12),
        name="convolve_back" if conj else "convolve",
    )(field, spec_h, tw, fwd, inv)


def taps_kernel(scale, u_ref, d_ref, tw_ref, inv_ref, out_ref, hi, lo, mid):
    def write(n, rows, value):
        out_ref[rows, n * 128 : n * 128 + 128] = value * np.float32(scale)

    multiply_spectra(u_ref, d_ref, True, hi, lo)
    inverse_field(hi, lo, inv_ref, tw_ref, mid, write)


def taps_gradient(spec_u, spec_d, tables, scale):
    tw, _, inv = tables
    chans = spec_u.shape[1]
    return pl.pallas_call(
        functools.partial(taps_kernel, scale),
        out_shape=jax.ShapeDtypeStruct((chans, 4096), F32),
        in_specs=[VM] * 4,
        out_specs=VM,
        scratch_shapes=spec_scratch(chans),
        compiler_params=grant(10),
        name="taps_gradient",
    )(spec_u, spec_d, tw, inv)


def to_blocks(rows, out_ref):
    for i in range(4):
        part = rows[i * 128 : i * 128 + 128, :].T.astype(BF)
        for z in range(8):
            out_ref[z, i] = part[z * 32 : z * 32 + 32, :]


def from_blocks(in_ref, t_ref):
    for z in range(8):
        for i in range(4):
            t_ref[z * 32 : z * 32 + 32, i * 128 : i * 128 + 128] = in_ref[z, i].astype(F32)
    return t_ref[...].T


def turned_place(y, x, dy, dx):
    return lax.rem(y + dy, 4) * 4 + lax.rem(x + dx, 4)


def feature_start(pos_ref, mine, k1, k2):
    g, y, x = pos_ref[0], pos_ref[1], pos_ref[2]
    owner = g if mine else 1 - g
    along_x = jnp.where(owner == 0, k1, k2)
    along_y = jnp.where(owner == 0, k2, k1)
    place = turned_place(y, x, 4 - along_y, 4 - along_x)
    return pl.multiple_of(place * 256 + owner * 128, 128)


def fetch_parts(pos_ref, blocks, marks, w_ref, transposed, x_ref, buf_ref, sems):
    count = len(marks)
    layers = 1 if transposed else 3
    copies = []
    for k1 in range(4):
        for i, (mine, k2) in enumerate(marks):
            start = feature_start(pos_ref, mine, k1, k2)
            part = pl.ds((k1 * count + i) * 128, 128)
            for k in range(layers):
                if transposed:
                    src, dst = w_ref.at[:, pl.ds(start, 128)], buf_ref.at[:, part]
                else:
                    src, dst = w_ref.at[k, pl.ds(start, 128), :], buf_ref.at[k, part, :]
                copies.append(pltpu.make_async_copy(src, dst, sems.at[k1, i * layers + k]))
                copies[-1].start()
    for k1 in range(4):
        for i in range(count):
            x_ref[:, (k1 * count + i) * 128 : (k1 * count + i + 1) * 128] = blocks[i][k1]
    for copy in copies:
        copy.wait()


def project_kernel(marks, first, last, pos_ref, *refs):
    count = len(marks)
    blocks, refs = refs[:count], refs[count:]
    w_ref, refs = refs[0], refs[1:]
    if not first:
        before, refs = refs[0], refs[1:]
    x_ref, buf_ref, sems = refs[-3:]
    fetch_parts(pos_ref, blocks, marks, w_ref, False, x_ref, buf_ref, sems)
    g = pos_ref[0]
    for k in range(3):
        total = jnp.dot(x_ref[...], buf_ref[k], preferred_element_type=F32)
        if not first:
            total += before[k]
        if not last:
            refs[0][k] = total
            continue
        pair_ref, single_ref = refs[:2]
        low = total.astype(BF)
        if k == 0:

            @pl.when(g == 0)
            def _(low=low):
                single_ref[...] = low

            @pl.when(g == 1)
            def _(low=low):
                pair_ref[0] = low

        elif k == 1:
            pair_ref[g] = low
        else:

            @pl.when(g == 0)
            def _(low=low):
                pair_ref[1] = low

            @pl.when(g == 1)
            def _(low=low):
                single_ref[...] = low

    if last:

        @pl.when(g == 1)
        def _():
            to_blocks(refs[0][0].astype(F32) * refs[0][1].astype(F32), refs[2])


def project_part(pos, blocks, marks, w, before, last):
    total = jax.ShapeDtypeStruct((3, 512, 256), F32)
    if last:
        shapes = (
            jax.ShapeDtypeStruct((2, 512, 256), BF),
            jax.ShapeDtypeStruct((512, 256), BF),
            jax.ShapeDtypeStruct((8, 4, 32, 128), BF),
        )
    else:
        shapes = (total,)
    ins = [pos] + list(blocks) + [w] + ([] if before is None else [before])
    outs = pl.pallas_call(
        functools.partial(project_kernel, marks, before is None, last),
        out_shape=shapes,
        in_specs=[SM] + [VM] * len(blocks) + [IN_HBM] + [VM] * (before is not None),
        out_specs=(VM,) * len(shapes),
        scratch_shapes=[
            pltpu.VMEM((512, 512 * len(marks)), BF),
            pltpu.VMEM((3, 512 * len(marks), 256), BF),
            pltpu.SemaphoreType.DMA((4, 3 * len(marks))),
        ],
        cost_estimate=pl.CostEstimate(
            flops=2 * 512 * 512 * 768 * len(marks), bytes_accessed=3000000, transcendentals=0
        ),
        compiler_params=grant(24),
        name="project_part",
    )(*ins)
    return outs if last else outs[0]


def gated_kernel(marks, first, last, pos_ref, *refs):
    @pl.when(pos_ref[0] == 1)
    def _():
        rest = refs
        blocks, rest = rest[: len(marks)], rest[len(marks) :]
        w_ref, rest = rest[0], rest[1:]
        if not first:
            before, rest = rest[0], rest[1:]
        x_ref, buf_ref, sems = rest[-3:]
        fetch_parts(pos_ref, blocks, marks, w_ref, True, x_ref, buf_ref, sems)
        total = lax.dot_general(
            x_ref[...], buf_ref[...], (((1,), (1,)), ((), ())), preferred_element_type=F32
        )
        if not first:
            total += before[...]
        if not last:
            rest[0][...] = total
        else:
            conv_ref, gate_ref, dconv_ref, dgate_ref = rest[:4]
            grad = total.astype(BF).astype(F32)
            dgate_ref[...] = (conv_ref[...].astype(F32) * grad).astype(BF)
            to_blocks(gate_ref[...].astype(F32) * grad, dconv_ref)


def gated_part(pos, blocks, marks, w, before, rows):
    last = rows is not None
    if last:
        shapes = (
            jax.ShapeDtypeStruct((8, 4, 32, 128), BF),
            jax.ShapeDtypeStruct((512, 256), BF),
        )
    else:
        shapes = (jax.ShapeDtypeStruct((512, 256), F32),)
    ins = [pos] + list(blocks) + [w] + ([] if before is None else [before])
    ins += list(rows) if last else []
    outs = pl.pallas_call(
        functools.partial(gated_kernel, marks, before is None, last),
        out_shape=shapes,
        in_specs=[SM]
        + [VM] * len(blocks)
        + [ANYWHERE]
        + [VM] * (len(ins) - len(blocks) - 2),
        out_specs=(VM,) * len(shapes),
        scratch_shapes=[
            pltpu.VMEM((512, 512 * len(marks)), BF),
            pltpu.VMEM((256, 512 * len(marks)), BF),
            pltpu.SemaphoreType.DMA((4, len(marks))),
        ],
        cost_estimate=pl.CostEstimate(
            flops=2 * 512 * 512 * 256 * len(marks), bytes_accessed=2000000, transcendentals=0
        ),
        compiler_params=grant(12),
        name="gated_part",
    )(*ins)
    return outs if last else outs[0]


SCORE = 128 ** (-0.5) * math.log2(math.e)


def attend_kernel(first, last, steps, pos_ref, q_ref, *refs):
    kv = refs[: len(steps)]
    refs = refs[len(steps) :]
    if not first:
        m_in, l_in, a_in = refs[:3]
        refs = refs[3:]
    if last:
        out_ref, m_ref, l_ref, a_ref = refs
    else:
        m_ref, l_ref, a_ref = refs
    z = pos_ref[3]
    if not first:
        m_ref[...] = m_in[...]
        l_ref[...] = l_in[...]
        a_ref[...] = a_in[...]

    def block(kv_ref):
        def one(i, carry):
            h, part = i // 2, i % 2
            cols = pl.ds(pl.multiple_of(h * 128, 128), 128)
            rows = pl.ds(pl.multiple_of(part * 256, 256), 256)
            s = lax.dot_general(
                kv_ref[0, :, cols],
                q_ref[rows, cols],
                (((1,), (1,)), ((), ())),
                preferred_element_type=F32,
            ) * np.float32(SCORE)
            if first:
                key = lax.broadcasted_iota(jnp.int32, s.shape, 0)
                qry = lax.broadcasted_iota(jnp.int32, s.shape, 1) + part * 256
                s = jnp.where(key <= qry, s, np.float32(-1e30))
                top = jnp.max(s, axis=0, keepdims=True)
            else:
                old = m_ref[h, 0:1, rows]
                top = jnp.maximum(old, jnp.max(s, axis=0, keepdims=True))
            p = jnp.exp2(s - top)
            total = jnp.sum(p, axis=0, keepdims=True)
            prod = lax.dot_general(
                kv_ref[1, :, cols],
                p.astype(BF),
                (((0,), (0,)), ((), ())),
                preferred_element_type=F32,
            )
            if not first:
                fade = jnp.exp2(old - top)
                total += l_ref[h, 0:1, rows] * fade
                prod += a_ref[h, :, rows] * fade
            m_ref[h, 0:1, rows] = top
            l_ref[h, 0:1, rows] = total
            a_ref[h, :, rows] = prod
            return carry

        lax.fori_loop(0, 4, one, 0)

    for i, (step, forward) in enumerate(steps):
        if first:
            block(kv[i])
        else:
            pl.when(z >= step if forward else z + step >= 8)(functools.partial(block, kv[i]))

    if last:
        for h in range(2):
            done = a_ref[h] / l_ref[h, 0:1, :]
            out_ref[:, h * 128 : h * 128 + 128] = done.T.astype(BF)


def attend(pos, q, blocks, state, steps, last):
    first = state is None
    shapes = [
        jax.ShapeDtypeStruct((2, 8, 512), F32),
        jax.ShapeDtypeStruct((2, 8, 512), F32),
        jax.ShapeDtypeStruct((2, 128, 512), F32),
    ]
    scratch = []
    if last:
        scratch = [pltpu.VMEM(s.shape, s.dtype) for s in shapes]
        shapes = [jax.ShapeDtypeStruct((512, 256), BF)]
    ins = [pos, q] + list(blocks) + ([] if first else list(state))
    return pl.pallas_call(
        functools.partial(attend_kernel, first, last, steps),
        out_shape=tuple(shapes),
        in_specs=[SM] + [VM] * (len(ins) - 1),
        out_specs=tuple([VM] * len(shapes)),
        scratch_shapes=scratch,
        cost_estimate=pl.CostEstimate(
            flops=1000000000 * len(steps), bytes_accessed=1000000, transcendentals=500000
        ),
        compiler_params=grant(14),
        name="attend",
    )(*ins)


def gate_kernel(in_ref, gate_ref, mixed_ref, conv_ref, t_ref):
    conv = from_blocks(in_ref, t_ref)
    conv_ref[...] = conv.astype(BF)
    mixed_ref[...] = (gate_ref[...].astype(F32) * conv).astype(BF)


def gate_rows(blocks, gate):
    shape = jax.ShapeDtypeStruct((512, 256), BF)
    return pl.pallas_call(
        gate_kernel,
        out_shape=(shape, shape),
        in_specs=[VM, VM],
        out_specs=(VM, VM),
        scratch_shapes=[pltpu.VMEM((256, 512), F32)],
        compiler_params=grant(4),
        name="gate_rows",
    )(blocks, gate)


def spread_kernel(pos_ref, x_ref, w_ref, *outs):
    y, x = pos_ref[1], pos_ref[2]
    a_refs, b_refs = outs[:4], outs[4:]
    for dx in range(4):
        for dy in range(4):
            cols = pl.ds(pl.multiple_of(turned_place(y, x, dy, dx) * 256, 256), 256)
            part = jnp.dot(x_ref[...], w_ref[:, cols], preferred_element_type=F32).astype(BF)
            a_refs[dx][dy] = part[:, :128]
            b_refs[dy][dx] = part[:, 128:]


def spread_out(pos, mixed, w):
    shape = jax.ShapeDtypeStruct((4, 512, 128), BF)
    outs = pl.pallas_call(
        spread_kernel,
        out_shape=(shape,) * 8,
        in_specs=[SM, VM, VM],
        out_specs=(VM,) * 8,
        compiler_params=grant(10),
        name="spread_out",
    )(pos, mixed, w)
    return outs[:4], outs[4:]


def rows_kernel(d_ref, rows_ref, dgate_ref, l_ref, t_ref):
    carried = from_blocks(d_ref, t_ref)
    l_ref[:, 0:256] = (carried * rows_ref[1].astype(F32)).astype(BF)
    l_ref[:, 256:512] = (carried * rows_ref[0].astype(F32)).astype(BF)
    l_ref[:, 512:768] = dgate_ref[...]


def gradient_rows(d_blocks, pair, d_gate):
    return pl.pallas_call(
        rows_kernel,
        out_shape=jax.ShapeDtypeStruct((512, 768), BF),
        in_specs=[VM] * 3,
        out_specs=VM,
        scratch_shapes=[pltpu.VMEM((256, 512), F32)],
        compiler_params=grant(5),
        name="gradient_rows",
    )(d_blocks, pair, d_gate)


def piece_kernel(half, d, pos_ref, l_ref, w_ref, *refs):
    out_ref, buf_ref, sems = refs[-3:]
    y, x = pos_ref[1], pos_ref[2]

    if half == 1:

        @pl.when(pos_ref[0] == 0)
        def _():
            out_ref[...] = refs[0][...]

    def copies(e):
        place = turned_place(y, x, *((e, d) if half == 0 else (d, e)))
        start = pl.multiple_of(place * 256 + half * 128, 128)
        for k in range(3):
            yield pltpu.make_async_copy(
                w_ref.at[k, pl.ds(start, 128), :],
                buf_ref.at[pl.ds(e * 128, 128), pl.ds(k * 256, 256)],
                sems.at[e, k],
            )

    @pl.when(pos_ref[0] == 1)
    def _():
        for e in range(4):
            for copy in copies(e):
                copy.start()

        def two(i, carry):
            for e in (2 * i, 2 * i + 1):
                for copy in copies(e):
                    copy.wait()
            part = lax.dot_general(
                l_ref[...],
                buf_ref[pl.ds(pl.multiple_of(i * 256, 256), 256), :],
                (((1,), (1,)), ((), ())),
                preferred_element_type=F32,
            ).astype(BF)
            out_ref[2 * i] = part[:, :128]
            out_ref[2 * i + 1] = part[:, 128:]
            return carry

        lax.fori_loop(0, 2, two, 0)


def input_piece(pos, rows, w, half, d, under=None):
    ins = [pos, rows, w] + ([] if under is None else [under])
    return pl.pallas_call(
        functools.partial(piece_kernel, half, d),
        out_shape=jax.ShapeDtypeStruct((4, 512, 128), BF),
        in_specs=[SM, VM, ANYWHERE] + ([] if under is None else [VM]),
        out_specs=VM,
        scratch_shapes=[pltpu.VMEM((512, 768), BF), pltpu.SemaphoreType.DMA((4, 3))],
        cost_estimate=pl.CostEstimate(
            flops=2 * 512 * 768 * 512, bytes_accessed=2000000, transcendentals=0
        ),
        compiler_params=grant(8),
        name="input_piece",
    )(*ins)


def blank_kernel(*refs):
    pass


def blank(pos, *shapes):
    return pl.pallas_call(
        blank_kernel,
        out_shape=tuple(jax.ShapeDtypeStruct(shape, kind) for shape, kind in shapes),
        in_specs=[SM],
        out_specs=(ANYWHERE,) * len(shapes),
        compiler_params=grant(1),
        name="blank",
    )(pos)


def plane_pairs(axes, by):
    pairs = []
    for g in range(2):
        for y in range(4):
            for x in range(4):
                ty, tx = (y, (x + by) % 4) if axes[g] == "x" else ((y + by) % 4, x)
                pairs.append((g * 16 + y * 4 + x, g * 16 + ty * 4 + tx))
    return pairs


def along(value, axes, by):
    return lax.ppermute(value, HX, plane_pairs(axes, by))


def ring(value, by):
    return lax.ppermute(value, "seq", [(i, (i + by) % 8) for i in range(8)])


def swapped(value):
    return lax.ppermute(value, "grp", [(0, 1), (1, 0)])


def exchanged(value, axis):
    return lax.all_to_all(value, axis, 0, 0, tiled=True)


ORDER = (1, 3, 2)


def gather_product(half, step):
    near = {d: along(half, "xy", d) for d in ORDER}
    stack = jnp.stack([half] + [near[d] for d in (1, 2, 3)])
    mine = {d: along(stack, "yx", d) for d in ORDER}
    total = step((stack, swapped(stack)), ((True, 0), (False, 0)), None, False)
    for d in ORDER:
        mine[d], total = lax.optimization_barrier((mine[d], total))
    other = [swapped(mine[d]) for d in ORDER]
    total = step([mine[d] for d in ORDER], [(True, d) for d in ORDER], total, False)
    return step(other, [(False, d) for d in ORDER], total, True)


def added(first, others):
    total = first.astype(F32)
    for other in others:
        total += other.astype(F32)
    return total.astype(BF)


def scatter_features(a, b):
    ra = [along(a[d], "xx", d) for d in ORDER]
    rb = [along(b[d], "yy", d) for d in ORDER]
    sa, sb = added(a[0], ra), added(b[0], rb)
    ta = [along(sa[d], "yy", d) for d in ORDER]
    tb = [along(sb[d], "xx", d) for d in ORDER]
    return jnp.concatenate([added(sa[0], ta), added(sb[0], tb)], axis=1)


def scatter_input(pos, rows, w):
    pieces = {}
    for d in ORDER + (0,):
        pieces[d] = swapped(input_piece(pos, rows, w, 0, d))
    for d in ORDER + (0,):
        pieces[d] = input_piece(pos, rows, w, 1, d, pieces[d])
    row = added(pieces[0], [along(pieces[d], "xy", d) for d in ORDER])
    return added(row[0], [along(row[d], "yx", d) for d in ORDER])


def body(seq_in, w_proj, w_out, filters):
    g, y, x, z = (lax.axis_index(name) for name in ("grp", "hy", "hx", "seq"))
    teacher = g == 0
    pos = jnp.stack([g, y, x, z]).astype(jnp.int32)
    weights_in, weights_out = w_proj[0], w_out[0]
    length = 4096
    tap_scale = length ** (-0.5)
    tables = dft_constants()
    spec_shape = ((NK, 32, 256), F32)
    row_shape = ((512, 256), BF)

    weights_hbm = pltpu.with_memory_space_constraint(weights_in, pltpu.HBM)
    half = lax.dynamic_slice_in_dim(seq_in, g * 128, 128, 1)

    def project(blocks, marks, before, last):
        return project_part(pos, blocks, marks, weights_hbm, before, last)

    pair, single, carried = gather_product(half, project)

    def teach(operands):
        pair, q, carried = operands
        moved = (ring(pair, 1), ring(pair, -1))
        state = attend(pos, q, [pair], None, [(0, True)], False)
        for step in range(1, 5):
            moved, state = lax.optimization_barrier((moved, state))
            blocks, steps = moved, [(step, True), (step, False)]
            if step < 3:
                moved = (ring(blocks[0], 1), ring(blocks[1], -1))
            elif step == 3:
                moved = (ring(blocks[0], 1),)
            else:
                steps = steps[:1]
            state = attend(pos, q, blocks, state, steps, step == 4)
        return (state[0],) + tuple(blank(pos, row_shape, spec_shape, spec_shape))

    def learn(operands):
        pair, gate, carried = operands
        field = exchanged(carried, "seq")
        spec_h = filter_spectrum(filters, tables, tap_scale)
        conv, spec_u = convolve(field, spec_h, tables, False)
        mixed, conv_rows = gate_rows(exchanged(conv, "seq"), gate)
        return (mixed, conv_rows, spec_u, spec_h)

    mixed, conv_rows, spec_u, spec_h = lax.cond(teacher, teach, learn, (pair, single, carried))
    y_own = scatter_features(*spread_out(pos, mixed, weights_out))
    sent = jnp.where(teacher, y_own[:, 128:], y_own[:, :128])
    kept = jnp.where(teacher, y_own[:, :128], y_own[:, 128:])
    got = swapped(sent)
    low, high = kept.astype(F32), got.astype(F32)
    diff = jnp.where(teacher, high - low, low - high).astype(BF)

    def gated(blocks, marks, before, last):
        extra = (conv_rows, single) if last else None
        return gated_part(pos, blocks, marks, weights_out, before, extra)

    d_conv, d_gate = gather_product(diff, gated)

    def rest(operands):
        return tuple(blank(pos, ((512, 768), BF), ((32, 4096), F32)))

    def learn_back(operands):
        d_conv, d_gate, pair, spec_u, spec_h = operands
        d_field, spec_d = convolve(exchanged(d_conv, "seq"), spec_h, tables, True)
        d_blocks = exchanged(d_field, "seq")
        d_taps = taps_gradient(spec_u, spec_d, tables, tap_scale)
        return (gradient_rows(d_blocks, pair, d_gate), d_taps)

    d_rows, d_taps = lax.cond(
        teacher, rest, learn_back, (d_conv, d_gate, pair, spec_u, spec_h)
    )
    lower = swapped(d_taps[:, :2048].astype(BF)).astype(F32)
    sums = scatter_input(pos, d_rows, weights_in)
    d_input = jnp.concatenate([swapped(sums), sums], axis=1)
    paired = jnp.where(teacher, y_own, d_input)[None]
    grad_filters = jnp.where(teacher, lower, d_taps[:, 2048:])
    return (paired, grad_filters)


def solution(mesh):
    fine = Mesh(mesh.devices.reshape(2, 4, 4, 8), ("grp", "hy", "hx", "seq"))
    return jax.shard_map(
        body,
        mesh=fine,
        in_specs=(
            P("seq", HEAD),
            P("grp", None, None, HEAD),
            P("grp", HEAD, None),
            P(HEAD + ("seq",), None),
        ),
        out_specs=(P("grp", "seq", HEAD), P(HEAD + ("seq",), "grp")),
        check_vma=False,
    )
```

```python
import functools
import math

import jax
import jax.numpy as jnp
import numpy as np
from jax import lax
from jax.experimental import pallas as pl
from jax.experimental.pallas import tpu as pltpu
from jax.sharding import Mesh
from jax.sharding import PartitionSpec as P

F32 = jnp.float32
BF = jnp.bfloat16
HX = ("grp", "hy", "hx")
GZ = ("grp", "seq")
HEAD = ("hy", "hx")
VM = pl.BlockSpec(memory_space=pltpu.VMEM)
SM = pl.BlockSpec(memory_space=pltpu.SMEM)
ANYWHERE = pl.BlockSpec(memory_space=pl.ANY)
IN_HBM = pl.BlockSpec(memory_space=pltpu.HBM)

ROOT_HALF = math.sqrt(0.5)
MIB = 1 << 20


def grant(mib):
    return pltpu.CompilerParams(vmem_limit_bytes=mib * MIB)

KEPT = [(k0, k1) for k0 in (1, 2, 3) for k1 in range(8)]
KEPT += [(0, k1) for k1 in range(5)] + [(4, k1) for k1 in range(4)]
NK = len(KEPT)


def dft_constants():
    m = np.arange(128)
    k = np.array([k0 + 8 * k1 for k0, k1 in KEPT])
    twist = np.exp(-2j * np.pi * np.outer(k, m) / 8192.0)
    weight = np.array([1.0 if kk in (0, 32) else 2.0 for kk in k]) / 8192.0
    back = np.conj(twist) * weight[:, None]
    inner = np.exp(-2j * np.pi * np.outer(m, m) / 128.0)
    c, s = inner.real, inner.imag
    forward = np.block([[c, s], [-s, c]])
    inverse = np.block([[c, -s], [s, c]])

    def split(mat):
        mat = jnp.asarray(mat, F32)
        hi = mat.astype(BF)
        lo = (mat - hi.astype(F32)).astype(BF)
        return jnp.stack([hi, lo])

    tw = np.stack([twist.real, twist.imag, back.real, back.imag]).astype(np.float32)
    return jnp.asarray(tw), split(forward), split(inverse)


def add_(a, b):
    if a is None:
        return b
    return a if b is None else a + b


def sub_(a, b):
    if b is None:
        return a
    return -b if a is None else a - b


def cadd(p, q):
    return (add_(p[0], q[0]), add_(p[1], q[1]))


def csub(p, q):
    return (sub_(p[0], q[0]), sub_(p[1], q[1]))


def scaled(a, by):
    if a is None or by == 0.0:
        return None
    return a if by == 1.0 else (-a if by == -1.0 else a * np.float32(by))


def turned(p, angle):
    eighth = angle / (math.pi / 4)
    near = round(eighth)
    re, im = p
    if abs(eighth - near) < 1e-9:
        near %= 8
        if near == 0:
            return p
        if near == 4:
            return (scaled(re, -1.0), scaled(im, -1.0))
        if near == 2:
            return (scaled(im, -1.0), re)
        if near == 6:
            return (im, scaled(re, -1.0))
        cc = ROOT_HALF if near in (1, 7) else -ROOT_HALF
        ss = ROOT_HALF if near in (1, 3) else -ROOT_HALF
        if re is not None and im is not None:
            if cc * ss > 0:
                return (scaled(re - im, cc), scaled(re + im, cc))
            return (scaled(re + im, cc), scaled(im - re, cc))
        return (sub_(scaled(re, cc), scaled(im, ss)), add_(scaled(re, ss), scaled(im, cc)))
    cc, ss = math.cos(angle), math.sin(angle)
    return (sub_(scaled(re, cc), scaled(im, ss)), add_(scaled(re, ss), scaled(im, cc)))


def dft_small(values, sign):
    count = len(values)
    if count == 1:
        return values
    even = dft_small(values[0::2], sign)
    odd = dft_small(values[1::2], sign)
    half = count // 2
    first, second = [], []
    for i in range(half):
        t = turned(odd[i], sign * 2 * math.pi * i / count)
        first.append(cadd(even[i], t))
        second.append(csub(even[i], t))
    return first + second


def outer_forward(x):
    c = np.float32(ROOT_HALF)
    cols = {k0: [] for k0 in range(5)}
    for b in range(8):
        x0, x1, x2, x3 = x[b], x[8 + b], x[16 + b], x[24 + b]
        e02, e13, d02 = x0 + x2, x1 + x3, x0 - x2
        cd, cs = c * (x1 - x3), c * e13
        part = {
            0: (e02 + e13, None),
            4: (e02 - e13, None),
            2: (d02, x3 - x1),
            1: (x0 + cd, -x2 - cs),
            3: (x0 - cd, x2 - cs),
        }
        for k0 in range(5):
            cols[k0].append(turned(part[k0], -2 * math.pi * b * k0 / 64))
    found = {k0: dft_small(cols[k0], -1) for k0 in range(5)}
    return [found[k0][k1] for k0, k1 in KEPT]


def outer_inverse(z):
    at = {kk: z[i] for i, kk in enumerate(KEPT)}
    zero = (None, None)
    grown = {}
    for k0 in (1, 2, 3):
        spread = dft_small([at[k0, k1] for k1 in range(8)], 1)
        grown[k0] = [turned(spread[b], 2 * math.pi * b * k0 / 64) for b in range(8)]
    real0 = dft_small([at[0, k1] if k1 < 5 else zero for k1 in range(8)], 1)
    spread4 = dft_small([at[4, k1] if k1 < 4 else zero for k1 in range(8)], 1)
    out = [None] * 32
    c = np.float32(ROOT_HALF)
    for b in range(8):
        r4 = turned(spread4[b], 2 * math.pi * b * 4 / 64)[0]
        g1, g2, g3 = grown[1][b], grown[2][b], grown[3][b]
        plus, minus = real0[b][0] + r4, real0[b][0] - r4
        out[b] = plus + g1[0] + g2[0] + g3[0]
        out[16 + b] = plus - g1[1] - g2[0] + g3[1]
        diag, anti = c * (g1[0] - g3[0]), c * (g1[1] + g3[1])
        out[8 + b] = minus + diag - anti - g2[1]
        out[24 + b] = minus - diag - anti + g2[1]
    return out


def store_split(hi_ref, lo_ref, k, rows, re, im):
    rh, ih = re.astype(BF), im.astype(BF)
    hi_ref[k, rows, 0:128] = rh
    hi_ref[k, rows, 128:256] = ih
    lo_ref[k, rows, 0:128] = (re - rh.astype(F32)).astype(BF)
    lo_ref[k, rows, 128:256] = (im - ih.astype(F32)).astype(BF)


def inner_product(hi_ref, lo_ref, mat_ref, out_ref):
    chans = hi_ref.shape[1]
    hi = hi_ref[...].reshape(NK * chans, 256)
    lo = lo_ref[...].reshape(NK * chans, 256)
    out = jnp.dot(hi, mat_ref[0], preferred_element_type=F32)
    out += jnp.dot(hi, mat_ref[1], preferred_element_type=F32)
    out += jnp.dot(lo, mat_ref[0], preferred_element_type=F32)
    out_ref[...] = out.reshape(NK, chans, 256)


def over_rows(chans, step):
    def one(part, carry):
        step(pl.ds(pl.multiple_of(part * 16, 16), 16))
        return carry

    lax.fori_loop(0, chans // 16, one, 0)


def forward_spectrum(read, tw_ref, fwd_ref, hi_ref, lo_ref, out_ref):
    def step(rows):
        outs = outer_forward([read(n, rows) for n in range(32)])
        for k in range(NK):
            re, im = outs[k]
            tr, ti = tw_ref[0, k : k + 1, :], tw_ref[1, k : k + 1, :]
            if im is None:
                store_split(hi_ref, lo_ref, k, rows, re * tr, re * ti)
            else:
                store_split(hi_ref, lo_ref, k, rows, re * tr - im * ti, re * ti + im * tr)

    over_rows(hi_ref.shape[1], step)
    inner_product(hi_ref, lo_ref, fwd_ref, out_ref)


def multiply_spectra(a_ref, b_ref, conj, hi_ref, lo_ref):
    chans = a_ref.shape[1]

    def one(k, carry):
        ar, ai = a_ref[k, :, 0:128], a_ref[k, :, 128:256]
        br, bi = b_ref[k, :, 0:128], b_ref[k, :, 128:256]
        if conj:
            re, im = ar * br + ai * bi, ar * bi - ai * br
        else:
            re, im = ar * br - ai * bi, ar * bi + ai * br
        store_split(hi_ref, lo_ref, k, slice(0, chans), re, im)
        return carry

    lax.fori_loop(0, NK, one, 0)


def inverse_field(hi_ref, lo_ref, inv_ref, tw_ref, mid_ref, write):
    inner_product(hi_ref, lo_ref, inv_ref, mid_ref)

    def step(rows):
        z = []
        for k in range(NK):
            re, im = mid_ref[k, rows, 0:128], mid_ref[k, rows, 128:256]
            tr, ti = tw_ref[2, k : k + 1, :], tw_ref[3, k : k + 1, :]
            z.append((re * tr - im * ti, re * ti + im * tr))
        out = outer_inverse(z)
        for n in range(32):
            write(n, rows, out[n])

    over_rows(hi_ref.shape[1], step)


def spec_scratch(chans):
    return [
        pltpu.VMEM((NK, chans, 256), BF),
        pltpu.VMEM((NK, chans, 256), BF),
        pltpu.VMEM((NK, chans, 256), F32),
    ]


def filter_kernel(scale, f_ref, tw_ref, fwd_ref, out_ref, hi, lo, mid):
    def read(n, rows):
        return f_ref[rows, n * 128 : n * 128 + 128] * np.float32(scale)

    forward_spectrum(read, tw_ref, fwd_ref, hi, lo, out_ref)


def filter_spectrum(filters, tables, scale):
    tw, fwd, _ = tables
    chans = filters.shape[0]
    return pl.pallas_call(
        functools.partial(filter_kernel, scale),
        out_shape=jax.ShapeDtypeStruct((NK, chans, 256), F32),
        in_specs=[VM] * 3,
        out_specs=VM,
        scratch_shapes=spec_scratch(chans),
        compiler_params=grant(10),
        name="filter_spectrum",
    )(filters, tw, fwd)


def conv_kernel(conj, x_ref, h_ref, tw_ref, fwd_ref, inv_ref, out_ref, u_ref, hi, lo, mid):
    def read(n, rows):
        z, i = divmod(n, 4)
        return x_ref[z, i, rows, :].astype(F32)

    def write(n, rows, value):
        z, i = divmod(n, 4)
        out_ref[z, i, rows, :] = value.astype(BF)

    forward_spectrum(read, tw_ref, fwd_ref, hi, lo, u_ref)
    multiply_spectra(h_ref, u_ref, conj, hi, lo)
    inverse_field(hi, lo, inv_ref, tw_ref, mid, write)


def convolve(field, spec_h, tables, conj):
    tw, fwd, inv = tables
    chans = field.shape[2]
    return pl.pallas_call(
        functools.partial(conv_kernel, conj),
        out_shape=(
            jax.ShapeDtypeStruct((8, 4, chans, 128), BF),
            jax.ShapeDtypeStruct((NK, chans, 256), F32),
        ),
        in_specs=[VM] * 5,
        out_specs=(VM, VM),
        scratch_shapes=spec_scratch(chans),
        compiler_params=grant(12),
        name="convolve_back" if conj else "convolve",
    )(field, spec_h, tw, fwd, inv)


def taps_kernel(scale, u_ref, d_ref, tw_ref, inv_ref, out_ref, hi, lo, mid):
    def write(n, rows, value):
        out_ref[rows, n * 128 : n * 128 + 128] = value * np.float32(scale)

    multiply_spectra(u_ref, d_ref, True, hi, lo)
    inverse_field(hi, lo, inv_ref, tw_ref, mid, write)


def taps_gradient(spec_u, spec_d, tables, scale):
    tw, _, inv = tables
    chans = spec_u.shape[1]
    return pl.pallas_call(
        functools.partial(taps_kernel, scale),
        out_shape=jax.ShapeDtypeStruct((chans, 4096), F32),
        in_specs=[VM] * 4,
        out_specs=VM,
        scratch_shapes=spec_scratch(chans),
        compiler_params=grant(10),
        name="taps_gradient",
    )(spec_u, spec_d, tw, inv)


def to_blocks(rows, out_ref):
    for i in range(4):
        part = rows[i * 128 : i * 128 + 128, :].T.astype(BF)
        for z in range(8):
            out_ref[z, i] = part[z * 32 : z * 32 + 32, :]


def from_blocks(in_ref, t_ref):
    for z in range(8):
        for i in range(4):
            t_ref[z * 32 : z * 32 + 32, i * 128 : i * 128 + 128] = in_ref[z, i].astype(F32)
    return t_ref[...].T


def turned_place(y, x, dy, dx):
    return lax.rem(y + dy, 4) * 4 + lax.rem(x + dx, 4)


def feature_start(pos_ref, mine, k1, k2):
    g, y, x = pos_ref[0], pos_ref[1], pos_ref[2]
    owner = g if mine else 1 - g
    along_x = jnp.where(owner == 0, k1, k2)
    along_y = jnp.where(owner == 0, k2, k1)
    place = turned_place(y, x, 4 - along_y, 4 - along_x)
    return pl.multiple_of(place * 256 + owner * 128, 128)


def fetch_parts(pos_ref, blocks, marks, w_ref, transposed, x_ref, buf_ref, sems):
    count = len(marks)
    layers = 1 if transposed else 3
    copies = []
    for k1 in range(4):
        for i, (mine, k2) in enumerate(marks):
            start = feature_start(pos_ref, mine, k1, k2)
            part = pl.ds((k1 * count + i) * 128, 128)
            for k in range(layers):
                if transposed:
                    src, dst = w_ref.at[:, pl.ds(start, 128)], buf_ref.at[:, part]
                else:
                    src, dst = w_ref.at[k, pl.ds(start, 128), :], buf_ref.at[k, part, :]
                copies.append(pltpu.make_async_copy(src, dst, sems.at[k1, i * layers + k]))
                copies[-1].start()
    for k1 in range(4):
        for i in range(count):
            x_ref[:, (k1 * count + i) * 128 : (k1 * count + i + 1) * 128] = blocks[i][k1]
    for copy in copies:
        copy.wait()


def project_kernel(marks, first, last, pos_ref, *refs):
    count = len(marks)
    blocks, refs = refs[:count], refs[count:]
    w_ref, refs = refs[0], refs[1:]
    if not first:
        before, refs = refs[0], refs[1:]
    x_ref, buf_ref, sems = refs[-3:]
    fetch_parts(pos_ref, blocks, marks, w_ref, False, x_ref, buf_ref, sems)
    g = pos_ref[0]
    for k in range(3):
        total = jnp.dot(x_ref[...], buf_ref[k], preferred_element_type=F32)
        if not first:
            total += before[k]
        if not last:
            refs[0][k] = total
            continue
        pair_ref, single_ref = refs[:2]
        low = total.astype(BF)
        if k == 0:

            @pl.when(g == 0)
            def _(low=low):
                single_ref[...] = low

            @pl.when(g == 1)
            def _(low=low):
                pair_ref[0] = low

        elif k == 1:
            pair_ref[g] = low
        else:

            @pl.when(g == 0)
            def _(low=low):
                pair_ref[1] = low

            @pl.when(g == 1)
            def _(low=low):
                single_ref[...] = low

    if last:

        @pl.when(g == 1)
        def _():
            to_blocks(refs[0][0].astype(F32) * refs[0][1].astype(F32), refs[2])


def project_part(pos, blocks, marks, w, before, last):
    total = jax.ShapeDtypeStruct((3, 512, 256), F32)
    if last:
        shapes = (
            jax.ShapeDtypeStruct((2, 512, 256), BF),
            jax.ShapeDtypeStruct((512, 256), BF),
            jax.ShapeDtypeStruct((8, 4, 32, 128), BF),
        )
    else:
        shapes = (total,)
    ins = [pos] + list(blocks) + [w] + ([] if before is None else [before])
    outs = pl.pallas_call(
        functools.partial(project_kernel, marks, before is None, last),
        out_shape=shapes,
        in_specs=[SM] + [VM] * len(blocks) + [IN_HBM] + [VM] * (before is not None),
        out_specs=(VM,) * len(shapes),
        scratch_shapes=[
            pltpu.VMEM((512, 512 * len(marks)), BF),
            pltpu.VMEM((3, 512 * len(marks), 256), BF),
            pltpu.SemaphoreType.DMA((4, 3 * len(marks))),
        ],
        cost_estimate=pl.CostEstimate(
            flops=2 * 512 * 512 * 768 * len(marks), bytes_accessed=3000000, transcendentals=0
        ),
        compiler_params=grant(24),
        name="project_part",
    )(*ins)
    return outs if last else outs[0]


def gated_kernel(marks, first, last, pos_ref, *refs):
    @pl.when(pos_ref[0] == 1)
    def _():
        rest = refs
        blocks, rest = rest[: len(marks)], rest[len(marks) :]
        w_ref, rest = rest[0], rest[1:]
        if not first:
            before, rest = rest[0], rest[1:]
        x_ref, buf_ref, sems = rest[-3:]
        fetch_parts(pos_ref, blocks, marks, w_ref, True, x_ref, buf_ref, sems)
        total = lax.dot_general(
            x_ref[...], buf_ref[...], (((1,), (1,)), ((), ())), preferred_element_type=F32
        )
        if not first:
            total += before[...]
        if not last:
            rest[0][...] = total
        else:
            conv_ref, gate_ref, dconv_ref, dgate_ref = rest[:4]
            grad = total.astype(BF).astype(F32)
            dgate_ref[...] = (conv_ref[...].astype(F32) * grad).astype(BF)
            to_blocks(gate_ref[...].astype(F32) * grad, dconv_ref)


def gated_part(pos, blocks, marks, w, before, rows):
    last = rows is not None
    if last:
        shapes = (
            jax.ShapeDtypeStruct((8, 4, 32, 128), BF),
            jax.ShapeDtypeStruct((512, 256), BF),
        )
    else:
        shapes = (jax.ShapeDtypeStruct((512, 256), F32),)
    ins = [pos] + list(blocks) + [w] + ([] if before is None else [before])
    ins += list(rows) if last else []
    outs = pl.pallas_call(
        functools.partial(gated_kernel, marks, before is None, last),
        out_shape=shapes,
        in_specs=[SM]
        + [VM] * len(blocks)
        + [ANYWHERE]
        + [VM] * (len(ins) - len(blocks) - 2),
        out_specs=(VM,) * len(shapes),
        scratch_shapes=[
            pltpu.VMEM((512, 512 * len(marks)), BF),
            pltpu.VMEM((256, 512 * len(marks)), BF),
            pltpu.SemaphoreType.DMA((4, len(marks))),
        ],
        cost_estimate=pl.CostEstimate(
            flops=2 * 512 * 512 * 256 * len(marks), bytes_accessed=2000000, transcendentals=0
        ),
        compiler_params=grant(12),
        name="gated_part",
    )(*ins)
    return outs if last else outs[0]


SCORE = 128 ** (-0.5) * math.log2(math.e)


def attend_kernel(first, last, steps, pos_ref, q_ref, *refs):
    kv = refs[: len(steps)]
    refs = refs[len(steps) :]
    if not first:
        m_in, l_in, a_in = refs[:3]
        refs = refs[3:]
    if last:
        out_ref, m_ref, l_ref, a_ref = refs
    else:
        m_ref, l_ref, a_ref = refs
    z = pos_ref[3]
    if not first:
        m_ref[...] = m_in[...]
        l_ref[...] = l_in[...]
        a_ref[...] = a_in[...]

    def block(kv_ref):
        def one(i, carry):
            h, part = i // 2, i % 2
            cols = pl.ds(pl.multiple_of(h * 128, 128), 128)
            rows = pl.ds(pl.multiple_of(part * 256, 256), 256)
            s = lax.dot_general(
                kv_ref[0, :, cols],
                q_ref[rows, cols],
                (((1,), (1,)), ((), ())),
                preferred_element_type=F32,
            ) * np.float32(SCORE)
            if first:
                key = lax.broadcasted_iota(jnp.int32, s.shape, 0)
                qry = lax.broadcasted_iota(jnp.int32, s.shape, 1) + part * 256
                s = jnp.where(key <= qry, s, np.float32(-1e30))
                top = jnp.max(s, axis=0, keepdims=True)
            else:
                old = m_ref[h, 0:1, rows]
                top = jnp.maximum(old, jnp.max(s, axis=0, keepdims=True))
            p = jnp.exp2(s - top)
            total = jnp.sum(p, axis=0, keepdims=True)
            prod = lax.dot_general(
                kv_ref[1, :, cols],
                p.astype(BF),
                (((0,), (0,)), ((), ())),
                preferred_element_type=F32,
            )
            if not first:
                fade = jnp.exp2(old - top)
                total += l_ref[h, 0:1, rows] * fade
                prod += a_ref[h, :, rows] * fade
            m_ref[h, 0:1, rows] = top
            l_ref[h, 0:1, rows] = total
            a_ref[h, :, rows] = prod
            return carry

        lax.fori_loop(0, 4, one, 0)

    for i, (step, forward) in enumerate(steps):
        if first:
            block(kv[i])
        else:
            pl.when(z >= step if forward else z + step >= 8)(functools.partial(block, kv[i]))

    if last:
        for h in range(2):
            done = a_ref[h] / l_ref[h, 0:1, :]
            out_ref[:, h * 128 : h * 128 + 128] = done.T.astype(BF)


def attend(pos, q, blocks, state, steps, last):
    first = state is None
    shapes = [
        jax.ShapeDtypeStruct((2, 8, 512), F32),
        jax.ShapeDtypeStruct((2, 8, 512), F32),
        jax.ShapeDtypeStruct((2, 128, 512), F32),
    ]
    scratch = []
    if last:
        scratch = [pltpu.VMEM(s.shape, s.dtype) for s in shapes]
        shapes = [jax.ShapeDtypeStruct((512, 256), BF)]
    ins = [pos, q] + list(blocks) + ([] if first else list(state))
    return pl.pallas_call(
        functools.partial(attend_kernel, first, last, steps),
        out_shape=tuple(shapes),
        in_specs=[SM] + [VM] * (len(ins) - 1),
        out_specs=tuple([VM] * len(shapes)),
        scratch_shapes=scratch,
        cost_estimate=pl.CostEstimate(
            flops=1000000000 * len(steps), bytes_accessed=1000000, transcendentals=500000
        ),
        compiler_params=grant(14),
        name="attend",
    )(*ins)


def gate_kernel(in_ref, gate_ref, mixed_ref, conv_ref, t_ref):
    conv = from_blocks(in_ref, t_ref)
    conv_ref[...] = conv.astype(BF)
    mixed_ref[...] = (gate_ref[...].astype(F32) * conv).astype(BF)


def gate_rows(blocks, gate):
    shape = jax.ShapeDtypeStruct((512, 256), BF)
    return pl.pallas_call(
        gate_kernel,
        out_shape=(shape, shape),
        in_specs=[VM, VM],
        out_specs=(VM, VM),
        scratch_shapes=[pltpu.VMEM((256, 512), F32)],
        compiler_params=grant(4),
        name="gate_rows",
    )(blocks, gate)


def spread_kernel(pos_ref, x_ref, w_ref, *outs):
    y, x = pos_ref[1], pos_ref[2]
    a_refs, b_refs = outs[:4], outs[4:]
    for dx in range(4):
        for dy in range(4):
            cols = pl.ds(pl.multiple_of(turned_place(y, x, dy, dx) * 256, 256), 256)
            part = jnp.dot(x_ref[...], w_ref[:, cols], preferred_element_type=F32).astype(BF)
            a_refs[dx][dy] = part[:, :128]
            b_refs[dy][dx] = part[:, 128:]


def spread_out(pos, mixed, w):
    shape = jax.ShapeDtypeStruct((4, 512, 128), BF)
    outs = pl.pallas_call(
        spread_kernel,
        out_shape=(shape,) * 8,
        in_specs=[SM, VM, VM],
        out_specs=(VM,) * 8,
        compiler_params=grant(10),
        name="spread_out",
    )(pos, mixed, w)
    return outs[:4], outs[4:]


def rows_kernel(d_ref, rows_ref, dgate_ref, l_ref, t_ref):
    carried = from_blocks(d_ref, t_ref)
    l_ref[:, 0:256] = (carried * rows_ref[1].astype(F32)).astype(BF)
    l_ref[:, 256:512] = (carried * rows_ref[0].astype(F32)).astype(BF)
    l_ref[:, 512:768] = dgate_ref[...]


def gradient_rows(d_blocks, pair, d_gate):
    return pl.pallas_call(
        rows_kernel,
        out_shape=jax.ShapeDtypeStruct((512, 768), BF),
        in_specs=[VM] * 3,
        out_specs=VM,
        scratch_shapes=[pltpu.VMEM((256, 512), F32)],
        compiler_params=grant(5),
        name="gradient_rows",
    )(d_blocks, pair, d_gate)


def piece_kernel(half, d, pos_ref, l_ref, w_ref, *refs):
    out_ref, buf_ref, sems = refs[-3:]
    y, x = pos_ref[1], pos_ref[2]

    if half == 1:

        @pl.when(pos_ref[0] == 0)
        def _():
            out_ref[...] = refs[0][...]

    def copies(e):
        place = turned_place(y, x, *((e, d) if half == 0 else (d, e)))
        start = pl.multiple_of(place * 256 + half * 128, 128)
        for k in range(3):
            yield pltpu.make_async_copy(
                w_ref.at[k, pl.ds(start, 128), :],
                buf_ref.at[pl.ds(e * 128, 128), pl.ds(k * 256, 256)],
                sems.at[e, k],
            )

    @pl.when(pos_ref[0] == 1)
    def _():
        for e in range(4):
            for copy in copies(e):
                copy.start()

        def two(i, carry):
            for e in (2 * i, 2 * i + 1):
                for copy in copies(e):
                    copy.wait()
            part = lax.dot_general(
                l_ref[...],
                buf_ref[pl.ds(pl.multiple_of(i * 256, 256), 256), :],
                (((1,), (1,)), ((), ())),
                preferred_element_type=F32,
            ).astype(BF)
            out_ref[2 * i] = part[:, :128]
            out_ref[2 * i + 1] = part[:, 128:]
            return carry

        lax.fori_loop(0, 2, two, 0)


def input_piece(pos, rows, w, half, d, under=None):
    ins = [pos, rows, w] + ([] if under is None else [under])
    return pl.pallas_call(
        functools.partial(piece_kernel, half, d),
        out_shape=jax.ShapeDtypeStruct((4, 512, 128), BF),
        in_specs=[SM, VM, ANYWHERE] + ([] if under is None else [VM]),
        out_specs=VM,
        scratch_shapes=[pltpu.VMEM((512, 768), BF), pltpu.SemaphoreType.DMA((4, 3))],
        cost_estimate=pl.CostEstimate(
            flops=2 * 512 * 768 * 512, bytes_accessed=2000000, transcendentals=0
        ),
        compiler_params=grant(8),
        name="input_piece",
    )(*ins)


def blank_kernel(*refs):
    pass


def blank(pos, *shapes):
    return pl.pallas_call(
        blank_kernel,
        out_shape=tuple(jax.ShapeDtypeStruct(shape, kind) for shape, kind in shapes),
        in_specs=[SM],
        out_specs=(ANYWHERE,) * len(shapes),
        compiler_params=grant(1),
        name="blank",
    )(pos)


def plane_pairs(axes, by):
    pairs = []
    for g in range(2):
        for y in range(4):
            for x in range(4):
                ty, tx = (y, (x + by) % 4) if axes[g] == "x" else ((y + by) % 4, x)
                pairs.append((g * 16 + y * 4 + x, g * 16 + ty * 4 + tx))
    return pairs


def along(value, axes, by):
    return lax.ppermute(value, HX, plane_pairs(axes, by))


def ring(value, by):
    return lax.ppermute(value, "seq", [(i, (i + by) % 8) for i in range(8)])


def swapped(value):
    return lax.ppermute(value, "grp", [(0, 1), (1, 0)])


def exchanged(value, axis):
    return lax.all_to_all(value, axis, 0, 0, tiled=True)


ORDER = (1, 3, 2)


def gather_product(half, step):
    near = {d: along(half, "xy", d) for d in ORDER}
    stack = jnp.stack([half] + [near[d] for d in (1, 2, 3)])
    mine = {d: along(stack, "yx", d) for d in ORDER}
    total = step((stack, swapped(stack)), ((True, 0), (False, 0)), None, False)
    for d in ORDER:
        mine[d], total = lax.optimization_barrier((mine[d], total))
    other = [swapped(mine[d]) for d in ORDER]
    total = step([mine[d] for d in ORDER], [(True, d) for d in ORDER], total, False)
    return step(other, [(False, d) for d in ORDER], total, True)


def added(first, others):
    total = first.astype(F32)
    for other in others:
        total += other.astype(F32)
    return total.astype(BF)


def scatter_features(a, b):
    ra = [along(a[d], "xx", d) for d in ORDER]
    rb = [along(b[d], "yy", d) for d in ORDER]
    sa, sb = added(a[0], ra), added(b[0], rb)
    ta = [along(sa[d], "yy", d) for d in ORDER]
    tb = [along(sb[d], "xx", d) for d in ORDER]
    return jnp.concatenate([added(sa[0], ta), added(sb[0], tb)], axis=1)


def scatter_input(pos, rows, w):
    pieces = {}
    for d in ORDER + (0,):
        pieces[d] = swapped(input_piece(pos, rows, w, 0, d))
    for d in ORDER + (0,):
        pieces[d] = input_piece(pos, rows, w, 1, d, pieces[d])
    row = added(pieces[0], [along(pieces[d], "xy", d) for d in ORDER])
    return added(row[0], [along(row[d], "yx", d) for d in ORDER])


def body(seq_in, w_proj, w_out, filters):
    g, y, x, z = (lax.axis_index(name) for name in ("grp", "hy", "hx", "seq"))
    teacher = g == 0
    pos = jnp.stack([g, y, x, z]).astype(jnp.int32)
    weights_in, weights_out = w_proj[0], w_out[0]
    length = 4096
    tap_scale = length ** (-0.5)
    tables = dft_constants()
    spec_shape = ((NK, 32, 256), F32)
    row_shape = ((512, 256), BF)

    weights_hbm = pltpu.with_memory_space_constraint(weights_in, pltpu.HBM)
    half = lax.dynamic_slice_in_dim(seq_in, g * 128, 128, 1)

    def project(blocks, marks, before, last):
        return project_part(pos, blocks, marks, weights_hbm, before, last)

    pair, single, carried = gather_product(half, project)

    def teach(operands):
        pair, q, carried = operands
        moved = (ring(pair, 1), ring(pair, -1))
        state = attend(pos, q, [pair], None, [(0, True)], False)
        for step in range(1, 5):
            moved, state = lax.optimization_barrier((moved, state))
            blocks, steps = moved, [(step, True), (step, False)]
            if step < 3:
                moved = (ring(blocks[0], 1), ring(blocks[1], -1))
            elif step == 3:
                moved = (ring(blocks[0], 1),)
            else:
                steps = steps[:1]
            state = attend(pos, q, blocks, state, steps, step == 4)
        return (state[0],) + tuple(blank(pos, row_shape, spec_shape, spec_shape))

    def learn(operands):
        pair, gate, carried = operands
        field = exchanged(carried, "seq")
        spec_h = filter_spectrum(filters, tables, tap_scale)
        conv, spec_u = convolve(field, spec_h, tables, False)
        mixed, conv_rows = gate_rows(exchanged(conv, "seq"), gate)
        return (mixed, conv_rows, spec_u, spec_h)

    mixed, conv_rows, spec_u, spec_h = lax.cond(g == 1, learn, teach, (pair, single, carried))
    y_own = scatter_features(*spread_out(pos, mixed, weights_out))
    sent = jnp.where(teacher, y_own[:, 128:], y_own[:, :128])
    kept = jnp.where(teacher, y_own[:, :128], y_own[:, 128:])
    got = swapped(sent)
    low, high = kept.astype(F32), got.astype(F32)
    diff = jnp.where(teacher, high - low, low - high).astype(BF)

    def gated(blocks, marks, before, last):
        extra = (conv_rows, single) if last else None
        return gated_part(pos, blocks, marks, weights_out, before, extra)

    d_conv, d_gate = gather_product(diff, gated)

    def rest(operands):
        return tuple(blank(pos, ((512, 768), BF), ((32, 4096), F32)))

    def learn_back(operands):
        d_conv, d_gate, pair, spec_u, spec_h = operands
        d_field, spec_d = convolve(exchanged(d_conv, "seq"), spec_h, tables, True)
        d_blocks = exchanged(d_field, "seq")
        d_taps = taps_gradient(spec_u, spec_d, tables, tap_scale)
        return (gradient_rows(d_blocks, pair, d_gate), d_taps)

    d_rows, d_taps = lax.cond(
        teacher, rest, learn_back, (d_conv, d_gate, pair, spec_u, spec_h)
    )
    lower = swapped(d_taps[:, :2048].astype(BF)).astype(F32)
    sums = scatter_input(pos, d_rows, weights_in)
    d_input = jnp.concatenate([swapped(sums), sums], axis=1)
    paired = jnp.where(teacher, y_own, d_input)[None]
    grad_filters = jnp.where(teacher, lower, d_taps[:, 2048:])
    return (paired, grad_filters)


def solution(mesh):
    fine = Mesh(mesh.devices.reshape(2, 4, 4, 8), ("grp", "hy", "hx", "seq"))
    return jax.shard_map(
        body,
        mesh=fine,
        in_specs=(
            P("seq", HEAD),
            P("grp", None, None, HEAD),
            P("grp", HEAD, None),
            P(HEAD + ("seq",), None),
        ),
        out_specs=(P("grp", "seq", HEAD), P(HEAD + ("seq",), "grp")),
        check_vma=False,
    )
```

```python
import functools
import math

import jax
import jax.numpy as jnp
import numpy as np
from jax import lax
from jax.experimental import pallas as pl
from jax.experimental.pallas import tpu as pltpu
from jax.sharding import Mesh
from jax.sharding import PartitionSpec as P

F32 = jnp.float32
BF = jnp.bfloat16
HX = ("grp", "hy", "hx")
GZ = ("grp", "seq")
HEAD = ("hy", "hx")
VM = pl.BlockSpec(memory_space=pltpu.VMEM)
SM = pl.BlockSpec(memory_space=pltpu.SMEM)
ANYWHERE = pl.BlockSpec(memory_space=pl.ANY)
IN_HBM = pl.BlockSpec(memory_space=pltpu.HBM)

ROOT_HALF = math.sqrt(0.5)
MIB = 1 << 20


def grant(mib):
    return pltpu.CompilerParams(vmem_limit_bytes=mib * MIB)

KEPT = [(k0, k1) for k0 in (1, 2, 3) for k1 in range(8)]
KEPT += [(0, k1) for k1 in range(5)] + [(4, k1) for k1 in range(4)]
NK = len(KEPT)


def dft_constants():
    m = np.arange(128)
    k = np.array([k0 + 8 * k1 for k0, k1 in KEPT])
    twist = np.exp(-2j * np.pi * np.outer(k, m) / 8192.0)
    weight = np.array([1.0 if kk in (0, 32) else 2.0 for kk in k]) / 8192.0
    back = np.conj(twist) * weight[:, None]
    inner = np.exp(-2j * np.pi * np.outer(m, m) / 128.0)
    c, s = inner.real, inner.imag
    forward = np.block([[c, s], [-s, c]])
    inverse = np.block([[c, -s], [s, c]])

    def split(mat):
        mat = jnp.asarray(mat, F32)
        hi = mat.astype(BF)
        lo = (mat - hi.astype(F32)).astype(BF)
        return jnp.stack([hi, lo])

    tw = np.stack([twist.real, twist.imag, back.real, back.imag]).astype(np.float32)
    return jnp.asarray(tw), split(forward), split(inverse)


def add_(a, b):
    if a is None:
        return b
    return a if b is None else a + b


def sub_(a, b):
    if b is None:
        return a
    return -b if a is None else a - b


def cadd(p, q):
    return (add_(p[0], q[0]), add_(p[1], q[1]))


def csub(p, q):
    return (sub_(p[0], q[0]), sub_(p[1], q[1]))


def scaled(a, by):
    if a is None or by == 0.0:
        return None
    return a if by == 1.0 else (-a if by == -1.0 else a * np.float32(by))


def turned(p, angle):
    eighth = angle / (math.pi / 4)
    near = round(eighth)
    re, im = p
    if abs(eighth - near) < 1e-9:
        near %= 8
        if near == 0:
            return p
        if near == 4:
            return (scaled(re, -1.0), scaled(im, -1.0))
        if near == 2:
            return (scaled(im, -1.0), re)
        if near == 6:
            return (im, scaled(re, -1.0))
        cc = ROOT_HALF if near in (1, 7) else -ROOT_HALF
        ss = ROOT_HALF if near in (1, 3) else -ROOT_HALF
        if re is not None and im is not None:
            if cc * ss > 0:
                return (scaled(re - im, cc), scaled(re + im, cc))
            return (scaled(re + im, cc), scaled(im - re, cc))
        return (sub_(scaled(re, cc), scaled(im, ss)), add_(scaled(re, ss), scaled(im, cc)))
    cc, ss = math.cos(angle), math.sin(angle)
    return (sub_(scaled(re, cc), scaled(im, ss)), add_(scaled(re, ss), scaled(im, cc)))


def dft_small(values, sign):
    count = len(values)
    if count == 1:
        return values
    even = dft_small(values[0::2], sign)
    odd = dft_small(values[1::2], sign)
    half = count // 2
    first, second = [], []
    for i in range(half):
        t = turned(odd[i], sign * 2 * math.pi * i / count)
        first.append(cadd(even[i], t))
        second.append(csub(even[i], t))
    return first + second


def outer_forward(x):
    c = np.float32(ROOT_HALF)
    cols = {k0: [] for k0 in range(5)}
    for b in range(8):
        x0, x1, x2, x3 = x[b], x[8 + b], x[16 + b], x[24 + b]
        e02, e13, d02 = x0 + x2, x1 + x3, x0 - x2
        cd, cs = c * (x1 - x3), c * e13
        part = {
            0: (e02 + e13, None),
            4: (e02 - e13, None),
            2: (d02, x3 - x1),
            1: (x0 + cd, -x2 - cs),
            3: (x0 - cd, x2 - cs),
        }
        for k0 in range(5):
            cols[k0].append(turned(part[k0], -2 * math.pi * b * k0 / 64))
    found = {k0: dft_small(cols[k0], -1) for k0 in range(5)}
    return [found[k0][k1] for k0, k1 in KEPT]


def outer_inverse(z):
    at = {kk: z[i] for i, kk in enumerate(KEPT)}
    zero = (None, None)
    grown = {}
    for k0 in (1, 2, 3):
        spread = dft_small([at[k0, k1] for k1 in range(8)], 1)
        grown[k0] = [turned(spread[b], 2 * math.pi * b * k0 / 64) for b in range(8)]
    real0 = dft_small([at[0, k1] if k1 < 5 else zero for k1 in range(8)], 1)
    spread4 = dft_small([at[4, k1] if k1 < 4 else zero for k1 in range(8)], 1)
    out = [None] * 32
    c = np.float32(ROOT_HALF)
    for b in range(8):
        r4 = turned(spread4[b], 2 * math.pi * b * 4 / 64)[0]
        g1, g2, g3 = grown[1][b], grown[2][b], grown[3][b]
        plus, minus = real0[b][0] + r4, real0[b][0] - r4
        out[b] = plus + g1[0] + g2[0] + g3[0]
        out[16 + b] = plus - g1[1] - g2[0] + g3[1]
        diag, anti = c * (g1[0] - g3[0]), c * (g1[1] + g3[1])
        out[8 + b] = minus + diag - anti - g2[1]
        out[24 + b] = minus - diag - anti + g2[1]
    return out


def store_split(hi_ref, lo_ref, k, rows, re, im):
    rh, ih = re.astype(BF), im.astype(BF)
    hi_ref[k, rows, 0:128] = rh
    hi_ref[k, rows, 128:256] = ih
    lo_ref[k, rows, 0:128] = (re - rh.astype(F32)).astype(BF)
    lo_ref[k, rows, 128:256] = (im - ih.astype(F32)).astype(BF)


def inner_product(hi_ref, lo_ref, mat_ref, out_ref):
    chans = hi_ref.shape[1]
    hi = hi_ref[...].reshape(NK * chans, 256)
    lo = lo_ref[...].reshape(NK * chans, 256)
    out = jnp.dot(hi, mat_ref[0], preferred_element_type=F32)
    out += jnp.dot(hi, mat_ref[1], preferred_element_type=F32)
    out += jnp.dot(lo, mat_ref[0], preferred_element_type=F32)
    out_ref[...] = out.reshape(NK, chans, 256)


def over_rows(chans, step):
    def one(part, carry):
        step(pl.ds(pl.multiple_of(part * 16, 16), 16))
        return carry

    lax.fori_loop(0, chans // 16, one, 0)


def forward_spectrum(read, tw_ref, fwd_ref, hi_ref, lo_ref, out_ref):
    def step(rows):
        outs = outer_forward([read(n, rows) for n in range(32)])
        for k in range(NK):
            re, im = outs[k]
            tr, ti = tw_ref[0, k : k + 1, :], tw_ref[1, k : k + 1, :]
            if im is None:
                store_split(hi_ref, lo_ref, k, rows, re * tr, re * ti)
            else:
                store_split(hi_ref, lo_ref, k, rows, re * tr - im * ti, re * ti + im * tr)

    over_rows(hi_ref.shape[1], step)
    inner_product(hi_ref, lo_ref, fwd_ref, out_ref)


def multiply_spectra(a_ref, b_ref, conj, hi_ref, lo_ref):
    chans = a_ref.shape[1]

    def one(k, carry):
        ar, ai = a_ref[k, :, 0:128], a_ref[k, :, 128:256]
        br, bi = b_ref[k, :, 0:128], b_ref[k, :, 128:256]
        if conj:
            re, im = ar * br + ai * bi, ar * bi - ai * br
        else:
            re, im = ar * br - ai * bi, ar * bi + ai * br
        store_split(hi_ref, lo_ref, k, slice(0, chans), re, im)
        return carry

    lax.fori_loop(0, NK, one, 0)


def inverse_field(hi_ref, lo_ref, inv_ref, tw_ref, mid_ref, write):
    inner_product(hi_ref, lo_ref, inv_ref, mid_ref)

    def step(rows):
        z = []
        for k in range(NK):
            re, im = mid_ref[k, rows, 0:128], mid_ref[k, rows, 128:256]
            tr, ti = tw_ref[2, k : k + 1, :], tw_ref[3, k : k + 1, :]
            z.append((re * tr - im * ti, re * ti + im * tr))
        out = outer_inverse(z)
        for n in range(32):
            write(n, rows, out[n])

    over_rows(hi_ref.shape[1], step)


def spec_scratch(chans):
    return [
        pltpu.VMEM((NK, chans, 256), BF),
        pltpu.VMEM((NK, chans, 256), BF),
        pltpu.VMEM((NK, chans, 256), F32),
    ]


def filter_kernel(scale, f_ref, tw_ref, fwd_ref, out_ref, hi, lo, mid):
    def read(n, rows):
        return f_ref[rows, n * 128 : n * 128 + 128] * np.float32(scale)

    forward_spectrum(read, tw_ref, fwd_ref, hi, lo, out_ref)


def filter_spectrum(filters, tables, scale):
    tw, fwd, _ = tables
    chans = filters.shape[0]
    return pl.pallas_call(
        functools.partial(filter_kernel, scale),
        out_shape=jax.ShapeDtypeStruct((NK, chans, 256), F32),
        in_specs=[VM] * 3,
        out_specs=VM,
        scratch_shapes=spec_scratch(chans),
        compiler_params=grant(10),
        name="filter_spectrum",
    )(filters, tw, fwd)


def conv_kernel(conj, x_ref, h_ref, tw_ref, fwd_ref, inv_ref, out_ref, u_ref, hi, lo, mid):
    def read(n, rows):
        z, i = divmod(n, 4)
        return x_ref[z, i, rows, :].astype(F32)

    def write(n, rows, value):
        z, i = divmod(n, 4)
        out_ref[z, i, rows, :] = value.astype(BF)

    forward_spectrum(read, tw_ref, fwd_ref, hi, lo, u_ref)
    multiply_spectra(h_ref, u_ref, conj, hi, lo)
    inverse_field(hi, lo, inv_ref, tw_ref, mid, write)


def convolve(field, spec_h, tables, conj):
    tw, fwd, inv = tables
    chans = field.shape[2]
    return pl.pallas_call(
        functools.partial(conv_kernel, conj),
        out_shape=(
            jax.ShapeDtypeStruct((8, 4, chans, 128), BF),
            jax.ShapeDtypeStruct((NK, chans, 256), F32),
        ),
        in_specs=[VM] * 5,
        out_specs=(VM, VM),
        scratch_shapes=spec_scratch(chans),
        compiler_params=grant(12),
        name="convolve_back" if conj else "convolve",
    )(field, spec_h, tw, fwd, inv)


def taps_kernel(scale, u_ref, d_ref, tw_ref, inv_ref, out_ref, hi, lo, mid):
    def write(n, rows, value):
        out_ref[rows, n * 128 : n * 128 + 128] = value * np.float32(scale)

    multiply_spectra(u_ref, d_ref, True, hi, lo)
    inverse_field(hi, lo, inv_ref, tw_ref, mid, write)


def taps_gradient(spec_u, spec_d, tables, scale):
    tw, _, inv = tables
    chans = spec_u.shape[1]
    return pl.pallas_call(
        functools.partial(taps_kernel, scale),
        out_shape=jax.ShapeDtypeStruct((chans, 4096), F32),
        in_specs=[VM] * 4,
        out_specs=VM,
        scratch_shapes=spec_scratch(chans),
        compiler_params=grant(10),
        name="taps_gradient",
    )(spec_u, spec_d, tw, inv)


def to_blocks(rows, out_ref):
    for i in range(4):
        part = rows[i * 128 : i * 128 + 128, :].T.astype(BF)
        for z in range(8):
            out_ref[z, i] = part[z * 32 : z * 32 + 32, :]


def from_blocks(in_ref, t_ref):
    for z in range(8):
        for i in range(4):
            t_ref[z * 32 : z * 32 + 32, i * 128 : i * 128 + 128] = in_ref[z, i].astype(F32)
    return t_ref[...].T


def turned_place(y, x, dy, dx):
    return lax.rem(y + dy, 4) * 4 + lax.rem(x + dx, 4)


def feature_start(pos_ref, mine, k1, k2):
    g, y, x = pos_ref[0], pos_ref[1], pos_ref[2]
    owner = g if mine else 1 - g
    along_x = jnp.where(owner == 0, k1, k2)
    along_y = jnp.where(owner == 0, k2, k1)
    place = turned_place(y, x, 4 - along_y, 4 - along_x)
    return pl.multiple_of(place * 256 + owner * 128, 128)


def fetch_parts(pos_ref, blocks, marks, w_ref, transposed, x_ref, buf_ref, sems):
    count = len(marks)
    layers = 1 if transposed else 3
    copies = []
    for k1 in range(4):
        for i, (mine, k2) in enumerate(marks):
            start = feature_start(pos_ref, mine, k1, k2)
            part = pl.ds((k1 * count + i) * 128, 128)
            for k in range(layers):
                if transposed:
                    src, dst = w_ref.at[:, pl.ds(start, 128)], buf_ref.at[:, part]
                else:
                    src, dst = w_ref.at[k, pl.ds(start, 128), :], buf_ref.at[k, part, :]
                copies.append(pltpu.make_async_copy(src, dst, sems.at[k1, i * layers + k]))
                copies[-1].start()
    for k1 in range(4):
        for i in range(count):
            x_ref[:, (k1 * count + i) * 128 : (k1 * count + i + 1) * 128] = blocks[i][k1]
    for copy in copies:
        copy.wait()


def project_kernel(marks, first, last, pos_ref, *refs):
    count = len(marks)
    blocks, refs = refs[:count], refs[count:]
    w_ref, refs = refs[0], refs[1:]
    if not first:
        before, refs = refs[0], refs[1:]
    x_ref, buf_ref, sems = refs[-3:]
    fetch_parts(pos_ref, blocks, marks, w_ref, False, x_ref, buf_ref, sems)
    g = pos_ref[0]
    for k in range(3):
        total = jnp.dot(x_ref[...], buf_ref[k], preferred_element_type=F32)
        if not first:
            total += before[k]
        if not last:
            refs[0][k] = total
            continue
        pair_ref, single_ref = refs[:2]
        low = total.astype(BF)
        if k == 0:

            @pl.when(g == 0)
            def _(low=low):
                single_ref[...] = low

            @pl.when(g == 1)
            def _(low=low):
                pair_ref[0] = low

        elif k == 1:
            pair_ref[g] = low
        else:

            @pl.when(g == 0)
            def _(low=low):
                pair_ref[1] = low

            @pl.when(g == 1)
            def _(low=low):
                single_ref[...] = low

    if last:

        @pl.when(g == 1)
        def _():
            to_blocks(refs[0][0].astype(F32) * refs[0][1].astype(F32), refs[2])


def project_part(pos, blocks, marks, w, before, last):
    total = jax.ShapeDtypeStruct((3, 512, 256), F32)
    if last:
        shapes = (
            jax.ShapeDtypeStruct((2, 512, 256), BF),
            jax.ShapeDtypeStruct((512, 256), BF),
            jax.ShapeDtypeStruct((8, 4, 32, 128), BF),
        )
    else:
        shapes = (total,)
    ins = [pos] + list(blocks) + [w] + ([] if before is None else [before])
    outs = pl.pallas_call(
        functools.partial(project_kernel, marks, before is None, last),
        out_shape=shapes,
        in_specs=[SM] + [VM] * len(blocks) + [IN_HBM] + [VM] * (before is not None),
        out_specs=(VM,) * len(shapes),
        scratch_shapes=[
            pltpu.VMEM((512, 512 * len(marks)), BF),
            pltpu.VMEM((3, 512 * len(marks), 256), BF),
            pltpu.SemaphoreType.DMA((4, 3 * len(marks))),
        ],
        cost_estimate=pl.CostEstimate(
            flops=2 * 512 * 512 * 768 * len(marks), bytes_accessed=3000000, transcendentals=0
        ),
        compiler_params=grant(24),
        name="project_part",
    )(*ins)
    return outs if last else outs[0]


def gated_kernel(marks, first, last, pos_ref, *refs):
    @pl.when(pos_ref[0] == 1)
    def _():
        rest = refs
        blocks, rest = rest[: len(marks)], rest[len(marks) :]
        w_ref, rest = rest[0], rest[1:]
        if not first:
            before, rest = rest[0], rest[1:]
        x_ref, buf_ref, sems = rest[-3:]
        fetch_parts(pos_ref, blocks, marks, w_ref, True, x_ref, buf_ref, sems)
        total = lax.dot_general(
            x_ref[...], buf_ref[...], (((1,), (1,)), ((), ())), preferred_element_type=F32
        )
        if not first:
            total += before[...]
        if not last:
            rest[0][...] = total
        else:
            conv_ref, gate_ref, dconv_ref, dgate_ref = rest[:4]
            grad = total.astype(BF).astype(F32)
            dgate_ref[...] = (conv_ref[...].astype(F32) * grad).astype(BF)
            to_blocks(gate_ref[...].astype(F32) * grad, dconv_ref)


def gated_part(pos, blocks, marks, w, before, rows):
    last = rows is not None
    if last:
        shapes = (
            jax.ShapeDtypeStruct((8, 4, 32, 128), BF),
            jax.ShapeDtypeStruct((512, 256), BF),
        )
    else:
        shapes = (jax.ShapeDtypeStruct((512, 256), F32),)
    ins = [pos] + list(blocks) + [w] + ([] if before is None else [before])
    ins += list(rows) if last else []
    outs = pl.pallas_call(
        functools.partial(gated_kernel, marks, before is None, last),
        out_shape=shapes,
        in_specs=[SM]
        + [VM] * len(blocks)
        + [ANYWHERE]
        + [VM] * (len(ins) - len(blocks) - 2),
        out_specs=(VM,) * len(shapes),
        scratch_shapes=[
            pltpu.VMEM((512, 512 * len(marks)), BF),
            pltpu.VMEM((256, 512 * len(marks)), BF),
            pltpu.SemaphoreType.DMA((4, len(marks))),
        ],
        cost_estimate=pl.CostEstimate(
            flops=2 * 512 * 512 * 256 * len(marks), bytes_accessed=2000000, transcendentals=0
        ),
        compiler_params=grant(12),
        name="gated_part",
    )(*ins)
    return outs if last else outs[0]


SCORE = 128 ** (-0.5) * math.log2(math.e)


def attend_kernel(first, last, steps, pos_ref, q_ref, *refs):
    kv = refs[: len(steps)]
    refs = refs[len(steps) :]
    if not first:
        m_in, l_in, a_in = refs[:3]
        refs = refs[3:]
    if last:
        out_ref, m_ref, l_ref, a_ref = refs
    else:
        m_ref, l_ref, a_ref = refs
    z = pos_ref[3]
    if not first:
        m_ref[...] = m_in[...]
        l_ref[...] = l_in[...]
        a_ref[...] = a_in[...]

    def block(kv_ref):
        def one(i, carry):
            h, part = i // 2, i % 2
            cols = pl.ds(pl.multiple_of(h * 128, 128), 128)
            rows = pl.ds(pl.multiple_of(part * 256, 256), 256)
            s = lax.dot_general(
                kv_ref[0, :, cols],
                q_ref[rows, cols],
                (((1,), (1,)), ((), ())),
                preferred_element_type=F32,
            ) * np.float32(SCORE)
            if first:
                key = lax.broadcasted_iota(jnp.int32, s.shape, 0)
                qry = lax.broadcasted_iota(jnp.int32, s.shape, 1) + part * 256
                s = jnp.where(key <= qry, s, np.float32(-1e30))
                top = jnp.max(s, axis=0, keepdims=True)
            else:
                old = m_ref[h, 0:1, rows]
                top = jnp.maximum(old, jnp.max(s, axis=0, keepdims=True))
            p = jnp.exp2(s - top)
            total = jnp.sum(p, axis=0, keepdims=True)
            prod = lax.dot_general(
                kv_ref[1, :, cols],
                p.astype(BF),
                (((0,), (0,)), ((), ())),
                preferred_element_type=F32,
            )
            if not first:
                fade = jnp.exp2(old - top)
                total += l_ref[h, 0:1, rows] * fade
                prod += a_ref[h, :, rows] * fade
            m_ref[h, 0:1, rows] = top
            l_ref[h, 0:1, rows] = total
            a_ref[h, :, rows] = prod
            return carry

        lax.fori_loop(0, 4, one, 0)

    for i, (step, forward) in enumerate(steps):
        if first:
            block(kv[i])
        else:
            pl.when(z >= step if forward else z + step >= 8)(functools.partial(block, kv[i]))

    if last:
        for h in range(2):
            done = a_ref[h] / l_ref[h, 0:1, :]
            out_ref[:, h * 128 : h * 128 + 128] = done.T.astype(BF)


def attend(pos, q, blocks, state, steps, last):
    first = state is None
    shapes = [
        jax.ShapeDtypeStruct((2, 8, 512), F32),
        jax.ShapeDtypeStruct((2, 8, 512), F32),
        jax.ShapeDtypeStruct((2, 128, 512), F32),
    ]
    scratch = []
    if last:
        scratch = [pltpu.VMEM(s.shape, s.dtype) for s in shapes]
        shapes = [jax.ShapeDtypeStruct((512, 256), BF)]
    ins = [pos, q] + list(blocks) + ([] if first else list(state))
    return pl.pallas_call(
        functools.partial(attend_kernel, first, last, steps),
        out_shape=tuple(shapes),
        in_specs=[SM] + [VM] * (len(ins) - 1),
        out_specs=tuple([VM] * len(shapes)),
        scratch_shapes=scratch,
        cost_estimate=pl.CostEstimate(
            flops=1000000000 * len(steps), bytes_accessed=1000000, transcendentals=500000
        ),
        compiler_params=grant(14),
        name="attend",
    )(*ins)


def gate_kernel(in_ref, gate_ref, mixed_ref, conv_ref, t_ref):
    conv = from_blocks(in_ref, t_ref)
    conv_ref[...] = conv.astype(BF)
    mixed_ref[...] = (gate_ref[...].astype(F32) * conv).astype(BF)


def gate_rows(blocks, gate):
    shape = jax.ShapeDtypeStruct((512, 256), BF)
    return pl.pallas_call(
        gate_kernel,
        out_shape=(shape, shape),
        in_specs=[VM, VM],
        out_specs=(VM, VM),
        scratch_shapes=[pltpu.VMEM((256, 512), F32)],
        compiler_params=grant(4),
        name="gate_rows",
    )(blocks, gate)


def spread_kernel(kept, pos_ref, x_ref, w_ref, *refs):
    g, y, x = pos_ref[0], pos_ref[1], pos_ref[2]
    half = g if kept else 1 - g
    other = refs[0] if kept else None
    all_ref = refs[-1]
    for d in range(4):
        for pair in range(2):
            right, places = [], []
            for e in (2 * pair, 2 * pair + 1):
                dy, dx = jnp.where(half == 0, e, d), jnp.where(half == 0, d, e)
                places.append(turned_place(y, x, dy, dx))
                start = pl.multiple_of(places[-1] * 256 + half * 128, 128)
                right.append(w_ref[:, pl.ds(start, 128)])
            part = jnp.dot(
                x_ref[...], jnp.concatenate(right, axis=1), preferred_element_type=F32
            )
            for i, e in enumerate((2 * pair, 2 * pair + 1)):
                own = part[:, i * 128 : i * 128 + 128]
                all_ref[places[i]] = own.astype(BF)
                if kept:
                    theirs = other[d, e].astype(F32)
                    refs[1 + d][e] = jnp.where(g == 0, theirs - own, own - theirs).astype(BF)
                else:
                    refs[0][d, e] = own.astype(BF)


def spread_out(pos, mixed, w, other=None):
    kept = other is not None
    every = jax.ShapeDtypeStruct((16, 512, 128), BF)
    if kept:
        shapes = (jax.ShapeDtypeStruct((4, 512, 128), BF),) * 4 + (every,)
    else:
        shapes = (jax.ShapeDtypeStruct((4, 4, 512, 128), BF), every)
    ins = [pos, mixed, w] + ([other] if kept else [])
    return pl.pallas_call(
        functools.partial(spread_kernel, kept),
        out_shape=shapes,
        in_specs=[SM] + [VM] * (len(ins) - 1),
        out_specs=(VM,) * len(shapes),
        compiler_params=grant(12),
        cost_estimate=pl.CostEstimate(
            flops=2 * 512 * 256 * 2048, bytes_accessed=6000000, transcendentals=0
        ),
        name="spread_out",
    )(*ins)


def sum_kernel(x_ref, out_ref):
    acc = x_ref[0].astype(F32)
    for i in range(1, 16):
        acc += x_ref[i].astype(F32)
    out_ref[...] = acc.astype(BF)


def sum_blocks(blocks):
    return pl.pallas_call(
        sum_kernel,
        out_shape=jax.ShapeDtypeStruct((512, 256), BF),
        in_specs=[VM],
        out_specs=VM,
        compiler_params=grant(8),
        name="sum_blocks",
    )(blocks)


def rows_kernel(d_ref, rows_ref, dgate_ref, l_ref, t_ref):
    carried = from_blocks(d_ref, t_ref)
    l_ref[:, 0:256] = (carried * rows_ref[1].astype(F32)).astype(BF)
    l_ref[:, 256:512] = (carried * rows_ref[0].astype(F32)).astype(BF)
    l_ref[:, 512:768] = dgate_ref[...]


def gradient_rows(d_blocks, pair, d_gate):
    return pl.pallas_call(
        rows_kernel,
        out_shape=jax.ShapeDtypeStruct((512, 768), BF),
        in_specs=[VM] * 3,
        out_specs=VM,
        scratch_shapes=[pltpu.VMEM((256, 512), F32)],
        compiler_params=grant(5),
        name="gradient_rows",
    )(d_blocks, pair, d_gate)


def piece_kernel(half, d, pos_ref, l_ref, w_ref, *refs):
    out_ref, buf_ref, sems = refs[-3:]
    y, x = pos_ref[1], pos_ref[2]

    if half == 1:

        @pl.when(pos_ref[0] == 0)
        def _():
            out_ref[...] = refs[0][...]

    def copies(e):
        place = turned_place(y, x, *((e, d) if half == 0 else (d, e)))
        start = pl.multiple_of(place * 256 + half * 128, 128)
        for k in range(3):
            yield pltpu.make_async_copy(
                w_ref.at[k, pl.ds(start, 128), :],
                buf_ref.at[pl.ds(e * 128, 128), pl.ds(k * 256, 256)],
                sems.at[e, k],
            )

    @pl.when(pos_ref[0] == 1)
    def _():
        for e in range(4):
            for copy in copies(e):
                copy.start()

        def two(i, carry):
            for e in (2 * i, 2 * i + 1):
                for copy in copies(e):
                    copy.wait()
            part = lax.dot_general(
                l_ref[...],
                buf_ref[pl.ds(pl.multiple_of(i * 256, 256), 256), :],
                (((1,), (1,)), ((), ())),
                preferred_element_type=F32,
            ).astype(BF)
            out_ref[2 * i] = part[:, :128]
            out_ref[2 * i + 1] = part[:, 128:]
            return carry

        lax.fori_loop(0, 2, two, 0)


def input_piece(pos, rows, w, half, d, under=None):
    ins = [pos, rows, w] + ([] if under is None else [under])
    return pl.pallas_call(
        functools.partial(piece_kernel, half, d),
        out_shape=jax.ShapeDtypeStruct((4, 512, 128), BF),
        in_specs=[SM, VM, ANYWHERE] + ([] if under is None else [VM]),
        out_specs=VM,
        scratch_shapes=[pltpu.VMEM((512, 768), BF), pltpu.SemaphoreType.DMA((4, 3))],
        cost_estimate=pl.CostEstimate(
            flops=2 * 512 * 768 * 512, bytes_accessed=2000000, transcendentals=0
        ),
        compiler_params=grant(8),
        name="input_piece",
    )(*ins)


def blank_kernel(*refs):
    pass


def blank(pos, *shapes):
    return pl.pallas_call(
        blank_kernel,
        out_shape=tuple(jax.ShapeDtypeStruct(shape, kind) for shape, kind in shapes),
        in_specs=[SM],
        out_specs=(ANYWHERE,) * len(shapes),
        compiler_params=grant(1),
        name="blank",
    )(pos)


def plane_pairs(axes, by):
    pairs = []
    for g in range(2):
        for y in range(4):
            for x in range(4):
                ty, tx = (y, (x + by) % 4) if axes[g] == "x" else ((y + by) % 4, x)
                pairs.append((g * 16 + y * 4 + x, g * 16 + ty * 4 + tx))
    return pairs


def along(value, axes, by):
    return lax.ppermute(value, HX, plane_pairs(axes, by))


def ring(value, by):
    return lax.ppermute(value, "seq", [(i, (i + by) % 8) for i in range(8)])


def swapped(value):
    return lax.ppermute(value, "grp", [(0, 1), (1, 0)])


def exchanged(value, axis):
    return lax.all_to_all(value, axis, 0, 0, tiled=True)


ORDER = (1, 3, 2)


def gather_product(half, step):
    near = {d: along(half, "xy", d) for d in ORDER}
    stack = jnp.stack([half] + [near[d] for d in (1, 2, 3)])
    mine = {d: along(stack, "yx", d) for d in ORDER}
    total = step((stack, swapped(stack)), ((True, 0), (False, 0)), None, False)
    for d in ORDER:
        mine[d], total = lax.optimization_barrier((mine[d], total))
    other = [swapped(mine[d]) for d in ORDER]
    total = step([mine[d] for d in ORDER], [(True, d) for d in ORDER], total, False)
    return step(other, [(False, d) for d in ORDER], total, True)


def added(first, others):
    total = first.astype(F32)
    for other in others:
        total += other.astype(F32)
    return total.astype(BF)


def scatter_half(pieces):
    row = added(pieces[0], [along(pieces[d], "xy", d) for d in ORDER])
    return added(row[0], [along(row[d], "yx", d) for d in ORDER])


def scatter_input(pos, rows, w):
    pieces = {}
    for d in ORDER + (0,):
        pieces[d] = swapped(input_piece(pos, rows, w, 0, d))
    for d in ORDER + (0,):
        pieces[d] = input_piece(pos, rows, w, 1, d, pieces[d])
    return scatter_half(pieces)


def body(seq_in, w_proj, w_out, filters):
    g, y, x, z = (lax.axis_index(name) for name in ("grp", "hy", "hx", "seq"))
    teacher = g == 0
    pos = jnp.stack([g, y, x, z]).astype(jnp.int32)
    weights_in, weights_out = w_proj[0], w_out[0]
    length = 4096
    tap_scale = length ** (-0.5)
    tables = dft_constants()
    spec_shape = ((NK, 32, 256), F32)
    row_shape = ((512, 256), BF)

    weights_hbm = pltpu.with_memory_space_constraint(weights_in, pltpu.HBM)
    half = lax.dynamic_slice_in_dim(seq_in, g * 128, 128, 1)

    def project(blocks, marks, before, last):
        return project_part(pos, blocks, marks, weights_hbm, before, last)

    pair, single, carried = gather_product(half, project)

    def teach(operands):
        pair, q, carried = operands
        moved = (ring(pair, 1), ring(pair, -1))
        state = attend(pos, q, [pair], None, [(0, True)], False)
        for step in range(1, 5):
            moved, state = lax.optimization_barrier((moved, state))
            blocks, steps = moved, [(step, True), (step, False)]
            if step < 3:
                moved = (ring(blocks[0], 1), ring(blocks[1], -1))
            elif step == 3:
                moved = (ring(blocks[0], 1),)
            else:
                steps = steps[:1]
            state = attend(pos, q, blocks, state, steps, step == 4)
        return (state[0],) + tuple(blank(pos, row_shape, spec_shape, spec_shape))

    def learn(operands):
        pair, gate, carried = operands
        field = exchanged(carried, "seq")
        spec_h = filter_spectrum(filters, tables, tap_scale)
        conv, spec_u = convolve(field, spec_h, tables, False)
        mixed, conv_rows = gate_rows(exchanged(conv, "seq"), gate)
        return (mixed, conv_rows, spec_u, spec_h)

    mixed, conv_rows, spec_u, spec_h = lax.cond(g == 1, learn, teach, (pair, single, carried))
    sent, sent_all = spread_out(pos, mixed, weights_out)
    *pieces, kept_all = spread_out(pos, mixed, weights_out, swapped(sent))
    diff = scatter_half(pieces)

    def gated(blocks, marks, before, last):
        extra = (conv_rows, single) if last else None
        return gated_part(pos, blocks, marks, weights_out, before, extra)

    d_conv, d_gate = gather_product(diff, gated)

    def teach_target(operands):
        sums = jnp.concatenate([kept_all, sent_all], axis=2)
        target = sum_blocks(lax.all_to_all(sums, HEAD, 0, 0, tiled=True))
        return tuple(blank(pos, ((512, 768), BF), ((32, 4096), F32))) + (target,)

    def learn_back(operands):
        d_conv, d_gate, pair, spec_u, spec_h = operands
        d_field, spec_d = convolve(exchanged(d_conv, "seq"), spec_h, tables, True)
        d_blocks = exchanged(d_field, "seq")
        d_taps = taps_gradient(spec_u, spec_d, tables, tap_scale)
        return (gradient_rows(d_blocks, pair, d_gate), d_taps) + tuple(blank(pos, row_shape))

    d_rows, d_taps, target = lax.cond(
        teacher, teach_target, learn_back, (d_conv, d_gate, pair, spec_u, spec_h)
    )
    lower = swapped(d_taps[:, :2048].astype(BF)).astype(F32)
    sums = scatter_input(pos, d_rows, weights_in)
    d_input = jnp.concatenate([swapped(sums), sums], axis=1)
    paired = jnp.where(teacher, target, d_input)[None]
    grad_filters = jnp.where(teacher, lower, d_taps[:, 2048:])
    return (paired, grad_filters)


def solution(mesh):
    fine = Mesh(mesh.devices.reshape(2, 4, 4, 8), ("grp", "hy", "hx", "seq"))
    return jax.shard_map(
        body,
        mesh=fine,
        in_specs=(
            P("seq", HEAD),
            P("grp", None, None, HEAD),
            P("grp", HEAD, None),
            P(HEAD + ("seq",), None),
        ),
        out_specs=(P("grp", "seq", HEAD), P(HEAD + ("seq",), "grp")),
        check_vma=False,
    )
```

```python
import functools
import math

import jax
import jax.numpy as jnp
import numpy as np
from jax import lax
from jax.experimental import pallas as pl
from jax.experimental.pallas import tpu as pltpu
from jax.sharding import Mesh
from jax.sharding import PartitionSpec as P

F32 = jnp.float32
BF = jnp.bfloat16
HX = ("grp", "hy", "hx")
GZ = ("grp", "seq")
HEAD = ("hy", "hx")
VM = pl.BlockSpec(memory_space=pltpu.VMEM)
SM = pl.BlockSpec(memory_space=pltpu.SMEM)
ANYWHERE = pl.BlockSpec(memory_space=pl.ANY)
IN_HBM = pl.BlockSpec(memory_space=pltpu.HBM)

ROOT_HALF = math.sqrt(0.5)
MIB = 1 << 20


def grant(mib):
    return pltpu.CompilerParams(vmem_limit_bytes=mib * MIB)

KEPT = [(k0, k1) for k0 in (1, 2, 3) for k1 in range(8)]
KEPT += [(0, k1) for k1 in range(5)] + [(4, k1) for k1 in range(4)]
NK = len(KEPT)


def dft_constants():
    m = np.arange(128)
    k = np.array([k0 + 8 * k1 for k0, k1 in KEPT])
    twist = np.exp(-2j * np.pi * np.outer(k, m) / 8192.0)
    weight = np.array([1.0 if kk in (0, 32) else 2.0 for kk in k]) / 8192.0
    back = np.conj(twist) * weight[:, None]
    inner = np.exp(-2j * np.pi * np.outer(m, m) / 128.0)
    c, s = inner.real, inner.imag
    forward = np.block([[c, s], [-s, c]])
    inverse = np.block([[c, -s], [s, c]])

    def split(mat):
        mat = jnp.asarray(mat, F32)
        hi = mat.astype(BF)
        lo = (mat - hi.astype(F32)).astype(BF)
        return jnp.stack([hi, lo])

    tw = np.stack([twist.real, twist.imag, back.real, back.imag]).astype(np.float32)
    return jnp.asarray(tw), split(forward), split(inverse)


def add_(a, b):
    if a is None:
        return b
    return a if b is None else a + b


def sub_(a, b):
    if b is None:
        return a
    return -b if a is None else a - b


def cadd(p, q):
    return (add_(p[0], q[0]), add_(p[1], q[1]))


def csub(p, q):
    return (sub_(p[0], q[0]), sub_(p[1], q[1]))


def scaled(a, by):
    if a is None or by == 0.0:
        return None
    return a if by == 1.0 else (-a if by == -1.0 else a * np.float32(by))


def turned(p, angle):
    eighth = angle / (math.pi / 4)
    near = round(eighth)
    re, im = p
    if abs(eighth - near) < 1e-9:
        near %= 8
        if near == 0:
            return p
        if near == 4:
            return (scaled(re, -1.0), scaled(im, -1.0))
        if near == 2:
            return (scaled(im, -1.0), re)
        if near == 6:
            return (im, scaled(re, -1.0))
        cc = ROOT_HALF if near in (1, 7) else -ROOT_HALF
        ss = ROOT_HALF if near in (1, 3) else -ROOT_HALF
        if re is not None and im is not None:
            if cc * ss > 0:
                return (scaled(re - im, cc), scaled(re + im, cc))
            return (scaled(re + im, cc), scaled(im - re, cc))
        return (sub_(scaled(re, cc), scaled(im, ss)), add_(scaled(re, ss), scaled(im, cc)))
    cc, ss = math.cos(angle), math.sin(angle)
    return (sub_(scaled(re, cc), scaled(im, ss)), add_(scaled(re, ss), scaled(im, cc)))


def dft_small(values, sign):
    count = len(values)
    if count == 1:
        return values
    even = dft_small(values[0::2], sign)
    odd = dft_small(values[1::2], sign)
    half = count // 2
    first, second = [], []
    for i in range(half):
        t = turned(odd[i], sign * 2 * math.pi * i / count)
        first.append(cadd(even[i], t))
        second.append(csub(even[i], t))
    return first + second


def outer_forward(x):
    c = np.float32(ROOT_HALF)
    cols = {k0: [] for k0 in range(5)}
    for b in range(8):
        x0, x1, x2, x3 = x[b], x[8 + b], x[16 + b], x[24 + b]
        e02, e13, d02 = x0 + x2, x1 + x3, x0 - x2
        cd, cs = c * (x1 - x3), c * e13
        part = {
            0: (e02 + e13, None),
            4: (e02 - e13, None),
            2: (d02, x3 - x1),
            1: (x0 + cd, -x2 - cs),
            3: (x0 - cd, x2 - cs),
        }
        for k0 in range(5):
            cols[k0].append(turned(part[k0], -2 * math.pi * b * k0 / 64))
    found = {k0: dft_small(cols[k0], -1) for k0 in range(5)}
    return [found[k0][k1] for k0, k1 in KEPT]


def outer_inverse(z):
    at = {kk: z[i] for i, kk in enumerate(KEPT)}
    zero = (None, None)
    grown = {}
    for k0 in (1, 2, 3):
        spread = dft_small([at[k0, k1] for k1 in range(8)], 1)
        grown[k0] = [turned(spread[b], 2 * math.pi * b * k0 / 64) for b in range(8)]
    real0 = dft_small([at[0, k1] if k1 < 5 else zero for k1 in range(8)], 1)
    spread4 = dft_small([at[4, k1] if k1 < 4 else zero for k1 in range(8)], 1)
    out = [None] * 32
    c = np.float32(ROOT_HALF)
    for b in range(8):
        r4 = turned(spread4[b], 2 * math.pi * b * 4 / 64)[0]
        g1, g2, g3 = grown[1][b], grown[2][b], grown[3][b]
        plus, minus = real0[b][0] + r4, real0[b][0] - r4
        out[b] = plus + g1[0] + g2[0] + g3[0]
        out[16 + b] = plus - g1[1] - g2[0] + g3[1]
        diag, anti = c * (g1[0] - g3[0]), c * (g1[1] + g3[1])
        out[8 + b] = minus + diag - anti - g2[1]
        out[24 + b] = minus - diag - anti + g2[1]
    return out


def store_split(hi_ref, lo_ref, k, rows, re, im):
    rh, ih = re.astype(BF), im.astype(BF)
    hi_ref[k, rows, 0:128] = rh
    hi_ref[k, rows, 128:256] = ih
    lo_ref[k, rows, 0:128] = (re - rh.astype(F32)).astype(BF)
    lo_ref[k, rows, 128:256] = (im - ih.astype(F32)).astype(BF)


def inner_product(hi_ref, lo_ref, mat_ref, out_ref):
    chans = hi_ref.shape[1]
    hi = hi_ref[...].reshape(NK * chans, 256)
    lo = lo_ref[...].reshape(NK * chans, 256)
    out = jnp.dot(hi, mat_ref[0], preferred_element_type=F32)
    out += jnp.dot(hi, mat_ref[1], preferred_element_type=F32)
    out += jnp.dot(lo, mat_ref[0], preferred_element_type=F32)
    out_ref[...] = out.reshape(NK, chans, 256)


def over_rows(chans, step):
    def one(part, carry):
        step(pl.ds(pl.multiple_of(part * 16, 16), 16))
        return carry

    lax.fori_loop(0, chans // 16, one, 0)


def forward_spectrum(read, tw_ref, fwd_ref, hi_ref, lo_ref, out_ref):
    def step(rows):
        outs = outer_forward([read(n, rows) for n in range(32)])
        for k in range(NK):
            re, im = outs[k]
            tr, ti = tw_ref[0, k : k + 1, :], tw_ref[1, k : k + 1, :]
            if im is None:
                store_split(hi_ref, lo_ref, k, rows, re * tr, re * ti)
            else:
                store_split(hi_ref, lo_ref, k, rows, re * tr - im * ti, re * ti + im * tr)

    over_rows(hi_ref.shape[1], step)
    inner_product(hi_ref, lo_ref, fwd_ref, out_ref)


def multiply_spectra(a_ref, b_ref, conj, hi_ref, lo_ref):
    chans = a_ref.shape[1]

    def one(k, carry):
        ar, ai = a_ref[k, :, 0:128], a_ref[k, :, 128:256]
        br, bi = b_ref[k, :, 0:128], b_ref[k, :, 128:256]
        if conj:
            re, im = ar * br + ai * bi, ar * bi - ai * br
        else:
            re, im = ar * br - ai * bi, ar * bi + ai * br
        store_split(hi_ref, lo_ref, k, slice(0, chans), re, im)
        return carry

    lax.fori_loop(0, NK, one, 0)


def inverse_field(hi_ref, lo_ref, inv_ref, tw_ref, mid_ref, write):
    inner_product(hi_ref, lo_ref, inv_ref, mid_ref)

    def step(rows):
        z = []
        for k in range(NK):
            re, im = mid_ref[k, rows, 0:128], mid_ref[k, rows, 128:256]
            tr, ti = tw_ref[2, k : k + 1, :], tw_ref[3, k : k + 1, :]
            z.append((re * tr - im * ti, re * ti + im * tr))
        out = outer_inverse(z)
        for n in range(32):
            write(n, rows, out[n])

    over_rows(hi_ref.shape[1], step)


def spec_scratch(chans):
    return [
        pltpu.VMEM((NK, chans, 256), BF),
        pltpu.VMEM((NK, chans, 256), BF),
        pltpu.VMEM((NK, chans, 256), F32),
    ]


def filter_kernel(scale, f_ref, tw_ref, fwd_ref, out_ref, hi, lo, mid):
    def read(n, rows):
        return f_ref[rows, n * 128 : n * 128 + 128] * np.float32(scale)

    forward_spectrum(read, tw_ref, fwd_ref, hi, lo, out_ref)


def filter_spectrum(filters, tables, scale):
    tw, fwd, _ = tables
    chans = filters.shape[0]
    return pl.pallas_call(
        functools.partial(filter_kernel, scale),
        out_shape=jax.ShapeDtypeStruct((NK, chans, 256), F32),
        in_specs=[VM] * 3,
        out_specs=VM,
        scratch_shapes=spec_scratch(chans),
        compiler_params=grant(10),
        name="filter_spectrum",
    )(filters, tw, fwd)


def conv_kernel(conj, x_ref, h_ref, tw_ref, fwd_ref, inv_ref, out_ref, u_ref, hi, lo, mid):
    def read(n, rows):
        z, i = divmod(n, 4)
        return x_ref[z, i, rows, :].astype(F32)

    def write(n, rows, value):
        z, i = divmod(n, 4)
        out_ref[z, i, rows, :] = value.astype(BF)

    forward_spectrum(read, tw_ref, fwd_ref, hi, lo, u_ref)
    multiply_spectra(h_ref, u_ref, conj, hi, lo)
    inverse_field(hi, lo, inv_ref, tw_ref, mid, write)


def convolve(field, spec_h, tables, conj):
    tw, fwd, inv = tables
    chans = field.shape[2]
    return pl.pallas_call(
        functools.partial(conv_kernel, conj),
        out_shape=(
            jax.ShapeDtypeStruct((8, 4, chans, 128), BF),
            jax.ShapeDtypeStruct((NK, chans, 256), F32),
        ),
        in_specs=[VM] * 5,
        out_specs=(VM, VM),
        scratch_shapes=spec_scratch(chans),
        compiler_params=grant(12),
        name="convolve_back" if conj else "convolve",
    )(field, spec_h, tw, fwd, inv)


def taps_kernel(scale, u_ref, d_ref, tw_ref, inv_ref, out_ref, hi, lo, mid):
    def write(n, rows, value):
        out_ref[rows, n * 128 : n * 128 + 128] = value * np.float32(scale)

    multiply_spectra(u_ref, d_ref, True, hi, lo)
    inverse_field(hi, lo, inv_ref, tw_ref, mid, write)


def taps_gradient(spec_u, spec_d, tables, scale):
    tw, _, inv = tables
    chans = spec_u.shape[1]
    return pl.pallas_call(
        functools.partial(taps_kernel, scale),
        out_shape=jax.ShapeDtypeStruct((chans, 4096), F32),
        in_specs=[VM] * 4,
        out_specs=VM,
        scratch_shapes=spec_scratch(chans),
        compiler_params=grant(10),
        name="taps_gradient",
    )(spec_u, spec_d, tw, inv)


def to_blocks(rows, out_ref):
    for i in range(4):
        part = rows[i * 128 : i * 128 + 128, :].T.astype(BF)
        for z in range(8):
            out_ref[z, i] = part[z * 32 : z * 32 + 32, :]


def from_blocks(in_ref, t_ref):
    for z in range(8):
        for i in range(4):
            t_ref[z * 32 : z * 32 + 32, i * 128 : i * 128 + 128] = in_ref[z, i].astype(F32)
    return t_ref[...].T


def turned_place(y, x, dy, dx):
    return lax.rem(y + dy, 4) * 4 + lax.rem(x + dx, 4)


def feature_start(pos_ref, mine, k1, k2):
    g, y, x = pos_ref[0], pos_ref[1], pos_ref[2]
    owner = g if mine else 1 - g
    along_x = jnp.where(owner == 0, k1, k2)
    along_y = jnp.where(owner == 0, k2, k1)
    place = turned_place(y, x, 4 - along_y, 4 - along_x)
    return pl.multiple_of(place * 256 + owner * 128, 128)


def fetch_parts(pos_ref, blocks, marks, w_ref, transposed, x_ref, buf_ref, sems):
    count = len(marks)
    layers = 1 if transposed else 3
    copies = []
    for k1 in range(4):
        for i, (mine, k2) in enumerate(marks):
            start = feature_start(pos_ref, mine, k1, k2)
            part = pl.ds((k1 * count + i) * 128, 128)
            for k in range(layers):
                if transposed:
                    src, dst = w_ref.at[:, pl.ds(start, 128)], buf_ref.at[:, part]
                else:
                    src, dst = w_ref.at[k, pl.ds(start, 128), :], buf_ref.at[k, part, :]
                copies.append(pltpu.make_async_copy(src, dst, sems.at[k1, i * layers + k]))
                copies[-1].start()
    for k1 in range(4):
        for i in range(count):
            x_ref[:, (k1 * count + i) * 128 : (k1 * count + i + 1) * 128] = blocks[i][k1]
    for copy in copies:
        copy.wait()


def project_kernel(marks, first, last, pos_ref, *refs):
    count = len(marks)
    blocks, refs = refs[:count], refs[count:]
    w_ref, refs = refs[0], refs[1:]
    if not first:
        before, refs = refs[0], refs[1:]
    x_ref, buf_ref, sems = refs[-3:]
    fetch_parts(pos_ref, blocks, marks, w_ref, False, x_ref, buf_ref, sems)
    g = pos_ref[0]
    for k in range(3):
        total = jnp.dot(x_ref[...], buf_ref[k], preferred_element_type=F32)
        if not first:
            total += before[k]
        if not last:
            refs[0][k] = total
            continue
        pair_ref, single_ref = refs[:2]
        low = total.astype(BF)
        if k == 0:

            @pl.when(g == 0)
            def _(low=low):
                single_ref[...] = low

            @pl.when(g == 1)
            def _(low=low):
                pair_ref[0] = low

        elif k == 1:
            pair_ref[g] = low
        else:

            @pl.when(g == 0)
            def _(low=low):
                pair_ref[1] = low

            @pl.when(g == 1)
            def _(low=low):
                single_ref[...] = low

    if last:

        @pl.when(g == 1)
        def _():
            to_blocks(refs[0][0].astype(F32) * refs[0][1].astype(F32), refs[2])


def project_part(pos, blocks, marks, w, before, last):
    total = jax.ShapeDtypeStruct((3, 512, 256), F32)
    if last:
        shapes = (
            jax.ShapeDtypeStruct((2, 512, 256), BF),
            jax.ShapeDtypeStruct((512, 256), BF),
            jax.ShapeDtypeStruct((8, 4, 32, 128), BF),
        )
    else:
        shapes = (total,)
    ins = [pos] + list(blocks) + [w] + ([] if before is None else [before])
    outs = pl.pallas_call(
        functools.partial(project_kernel, marks, before is None, last),
        out_shape=shapes,
        in_specs=[SM] + [VM] * len(blocks) + [IN_HBM] + [VM] * (before is not None),
        out_specs=(VM,) * len(shapes),
        scratch_shapes=[
            pltpu.VMEM((512, 512 * len(marks)), BF),
            pltpu.VMEM((3, 512 * len(marks), 256), BF),
            pltpu.SemaphoreType.DMA((4, 3 * len(marks))),
        ],
        cost_estimate=pl.CostEstimate(
            flops=2 * 512 * 512 * 768 * len(marks), bytes_accessed=3000000, transcendentals=0
        ),
        compiler_params=grant(24),
        name="project_part",
    )(*ins)
    return outs if last else outs[0]


def gated_kernel(marks, first, last, pos_ref, *refs):
    @pl.when(pos_ref[0] == 1)
    def _():
        rest = refs
        blocks, rest = rest[: len(marks)], rest[len(marks) :]
        w_ref, rest = rest[0], rest[1:]
        if not first:
            before, rest = rest[0], rest[1:]
        x_ref, buf_ref, sems = rest[-3:]
        fetch_parts(pos_ref, blocks, marks, w_ref, True, x_ref, buf_ref, sems)
        total = lax.dot_general(
            x_ref[...], buf_ref[...], (((1,), (1,)), ((), ())), preferred_element_type=F32
        )
        if not first:
            total += before[...]
        if not last:
            rest[0][...] = total
        else:
            conv_ref, gate_ref, dconv_ref, dgate_ref = rest[:4]
            grad = total.astype(BF).astype(F32)
            dgate_ref[...] = (conv_ref[...].astype(F32) * grad).astype(BF)
            to_blocks(gate_ref[...].astype(F32) * grad, dconv_ref)


def gated_part(pos, blocks, marks, w, before, rows):
    last = rows is not None
    if last:
        shapes = (
            jax.ShapeDtypeStruct((8, 4, 32, 128), BF),
            jax.ShapeDtypeStruct((512, 256), BF),
        )
    else:
        shapes = (jax.ShapeDtypeStruct((512, 256), F32),)
    ins = [pos] + list(blocks) + [w] + ([] if before is None else [before])
    ins += list(rows) if last else []
    outs = pl.pallas_call(
        functools.partial(gated_kernel, marks, before is None, last),
        out_shape=shapes,
        in_specs=[SM]
        + [VM] * len(blocks)
        + [ANYWHERE]
        + [VM] * (len(ins) - len(blocks) - 2),
        out_specs=(VM,) * len(shapes),
        scratch_shapes=[
            pltpu.VMEM((512, 512 * len(marks)), BF),
            pltpu.VMEM((256, 512 * len(marks)), BF),
            pltpu.SemaphoreType.DMA((4, len(marks))),
        ],
        cost_estimate=pl.CostEstimate(
            flops=2 * 512 * 512 * 256 * len(marks), bytes_accessed=2000000, transcendentals=0
        ),
        compiler_params=grant(12),
        name="gated_part",
    )(*ins)
    return outs if last else outs[0]


SCORE = 128 ** (-0.5) * math.log2(math.e)


def attend_kernel(first, last, steps, pos_ref, q_ref, *refs):
    kv = refs[: len(steps)]
    refs = refs[len(steps) :]
    if not first:
        m_in, l_in, a_in = refs[:3]
        refs = refs[3:]
    if last:
        out_ref, m_ref, l_ref, a_ref = refs
    else:
        m_ref, l_ref, a_ref = refs
    z = pos_ref[3]
    if not first:
        m_ref[...] = m_in[...]
        l_ref[...] = l_in[...]
        a_ref[...] = a_in[...]

    def block(kv_ref):
        def one(i, carry):
            h, part = i // 2, i % 2
            cols = pl.ds(pl.multiple_of(h * 128, 128), 128)
            rows = pl.ds(pl.multiple_of(part * 256, 256), 256)
            s = lax.dot_general(
                kv_ref[0, :, cols],
                q_ref[rows, cols],
                (((1,), (1,)), ((), ())),
                preferred_element_type=F32,
            ) * np.float32(SCORE)
            if first:
                key = lax.broadcasted_iota(jnp.int32, s.shape, 0)
                qry = lax.broadcasted_iota(jnp.int32, s.shape, 1) + part * 256
                s = jnp.where(key <= qry, s, np.float32(-1e30))
                top = jnp.max(s, axis=0, keepdims=True)
            else:
                old = m_ref[h, 0:1, rows]
                top = jnp.maximum(old, jnp.max(s, axis=0, keepdims=True))
            p = jnp.exp2(s - top)
            total = jnp.sum(p, axis=0, keepdims=True)
            prod = lax.dot_general(
                kv_ref[1, :, cols],
                p.astype(BF),
                (((0,), (0,)), ((), ())),
                preferred_element_type=F32,
            )
            if not first:
                fade = jnp.exp2(old - top)
                total += l_ref[h, 0:1, rows] * fade
                prod += a_ref[h, :, rows] * fade
            m_ref[h, 0:1, rows] = top
            l_ref[h, 0:1, rows] = total
            a_ref[h, :, rows] = prod
            return carry

        lax.fori_loop(0, 4, one, 0)

    for i, (step, forward) in enumerate(steps):
        if first:
            block(kv[i])
        else:
            pl.when(z >= step if forward else z + step >= 8)(functools.partial(block, kv[i]))

    if last:
        for h in range(2):
            done = a_ref[h] / l_ref[h, 0:1, :]
            out_ref[:, h * 128 : h * 128 + 128] = done.T.astype(BF)


def attend(pos, q, blocks, state, steps, last):
    first = state is None
    shapes = [
        jax.ShapeDtypeStruct((2, 8, 512), F32),
        jax.ShapeDtypeStruct((2, 8, 512), F32),
        jax.ShapeDtypeStruct((2, 128, 512), F32),
    ]
    scratch = []
    if last:
        scratch = [pltpu.VMEM(s.shape, s.dtype) for s in shapes]
        shapes = [jax.ShapeDtypeStruct((512, 256), BF)]
    ins = [pos, q] + list(blocks) + ([] if first else list(state))
    return pl.pallas_call(
        functools.partial(attend_kernel, first, last, steps),
        out_shape=tuple(shapes),
        in_specs=[SM] + [VM] * (len(ins) - 1),
        out_specs=tuple([VM] * len(shapes)),
        scratch_shapes=scratch,
        cost_estimate=pl.CostEstimate(
            flops=1000000000 * len(steps), bytes_accessed=1000000, transcendentals=500000
        ),
        compiler_params=grant(14),
        name="attend",
    )(*ins)


def gate_kernel(in_ref, gate_ref, mixed_ref, conv_ref, t_ref):
    conv = from_blocks(in_ref, t_ref)
    conv_ref[...] = conv.astype(BF)
    mixed_ref[...] = (gate_ref[...].astype(F32) * conv).astype(BF)


def gate_rows(blocks, gate):
    shape = jax.ShapeDtypeStruct((512, 256), BF)
    return pl.pallas_call(
        gate_kernel,
        out_shape=(shape, shape),
        in_specs=[VM, VM],
        out_specs=(VM, VM),
        scratch_shapes=[pltpu.VMEM((256, 512), F32)],
        compiler_params=grant(4),
        name="gate_rows",
    )(blocks, gate)


def spread_kernel(pos_ref, x_ref, w_ref, *outs):
    y, x = pos_ref[1], pos_ref[2]
    a_refs, b_refs = outs[:4], outs[4:]
    for dx in range(4):
        for dy in range(4):
            cols = pl.ds(pl.multiple_of(turned_place(y, x, dy, dx) * 256, 256), 256)
            part = jnp.dot(x_ref[...], w_ref[:, cols], preferred_element_type=F32).astype(BF)
            a_refs[dx][dy] = part[:, :128]
            b_refs[dy][dx] = part[:, 128:]


def spread_out(pos, mixed, w):
    shape = jax.ShapeDtypeStruct((4, 512, 128), BF)
    outs = pl.pallas_call(
        spread_kernel,
        out_shape=(shape,) * 8,
        in_specs=[SM, VM, VM],
        out_specs=(VM,) * 8,
        compiler_params=grant(10),
        name="spread_out",
    )(pos, mixed, w)
    return outs[:4], outs[4:]


def rows_kernel(d_ref, rows_ref, dgate_ref, l_ref, t_ref):
    carried = from_blocks(d_ref, t_ref)
    l_ref[:, 0:256] = (carried * rows_ref[1].astype(F32)).astype(BF)
    l_ref[:, 256:512] = (carried * rows_ref[0].astype(F32)).astype(BF)
    l_ref[:, 512:768] = dgate_ref[...]


def gradient_rows(d_blocks, pair, d_gate):
    return pl.pallas_call(
        rows_kernel,
        out_shape=jax.ShapeDtypeStruct((512, 768), BF),
        in_specs=[VM] * 3,
        out_specs=VM,
        scratch_shapes=[pltpu.VMEM((256, 512), F32)],
        compiler_params=grant(5),
        name="gradient_rows",
    )(d_blocks, pair, d_gate)


def piece_kernel(half, d, pos_ref, l_ref, w_ref, *refs):
    out_ref = refs[-1]
    y, x = pos_ref[1], pos_ref[2]

    if half == 1:

        @pl.when(pos_ref[0] == 0)
        def _():
            out_ref[...] = refs[0][...]

    @pl.when(pos_ref[0] == 1)
    def _():
        for pair in range(2):
            right = []
            for e in (2 * pair, 2 * pair + 1):
                place = turned_place(y, x, *((e, d) if half == 0 else (d, e)))
                start = pl.multiple_of(place * 256 + half * 128, 128)
                right.append(
                    jnp.concatenate([w_ref[k, pl.ds(start, 128), :] for k in range(3)], axis=1)
                )
            part = lax.dot_general(
                l_ref[...],
                jnp.concatenate(right),
                (((1,), (1,)), ((), ())),
                preferred_element_type=F32,
            ).astype(BF)
            out_ref[2 * pair] = part[:, :128]
            out_ref[2 * pair + 1] = part[:, 128:]


def input_piece(pos, rows, w, half, d, under=None):
    ins = [pos, rows, w] + ([] if under is None else [under])
    return pl.pallas_call(
        functools.partial(piece_kernel, half, d),
        out_shape=jax.ShapeDtypeStruct((4, 512, 128), BF),
        in_specs=[SM] + [VM] * (len(ins) - 1),
        out_specs=VM,
        cost_estimate=pl.CostEstimate(
            flops=2 * 512 * 768 * 512, bytes_accessed=2000000, transcendentals=0
        ),
        compiler_params=grant(16),
        name="input_piece",
    )(*ins)


def blank_kernel(*refs):
    pass


def blank(pos, *shapes):
    return pl.pallas_call(
        blank_kernel,
        out_shape=tuple(jax.ShapeDtypeStruct(shape, kind) for shape, kind in shapes),
        in_specs=[SM],
        out_specs=(ANYWHERE,) * len(shapes),
        compiler_params=grant(1),
        name="blank",
    )(pos)


def plane_pairs(axes, by):
    pairs = []
    for g in range(2):
        for y in range(4):
            for x in range(4):
                ty, tx = (y, (x + by) % 4) if axes[g] == "x" else ((y + by) % 4, x)
                pairs.append((g * 16 + y * 4 + x, g * 16 + ty * 4 + tx))
    return pairs


def along(value, axes, by):
    return lax.ppermute(value, HX, plane_pairs(axes, by))


def ring(value, by):
    return lax.ppermute(value, "seq", [(i, (i + by) % 8) for i in range(8)])


def swapped(value):
    return lax.ppermute(value, "grp", [(0, 1), (1, 0)])


def exchanged(value, axis):
    return lax.all_to_all(value, axis, 0, 0, tiled=True)


ORDER = (1, 3, 2)


def gather_product(half, step):
    near = {d: along(half, "xy", d) for d in ORDER}
    stack = jnp.stack([half] + [near[d] for d in (1, 2, 3)])
    mine = {d: along(stack, "yx", d) for d in ORDER}
    total = step((stack, swapped(stack)), ((True, 0), (False, 0)), None, False)
    for d in ORDER:
        mine[d], total = lax.optimization_barrier((mine[d], total))
    other = [swapped(mine[d]) for d in ORDER]
    total = step([mine[d] for d in ORDER], [(True, d) for d in ORDER], total, False)
    return step(other, [(False, d) for d in ORDER], total, True)


def added(first, others):
    total = first.astype(F32)
    for other in others:
        total += other.astype(F32)
    return total.astype(BF)


def scatter_features(a, b):
    ra = [along(a[d], "xx", d) for d in ORDER]
    rb = [along(b[d], "yy", d) for d in ORDER]
    sa, sb = added(a[0], ra), added(b[0], rb)
    ta = [along(sa[d], "yy", d) for d in ORDER]
    tb = [along(sb[d], "xx", d) for d in ORDER]
    return jnp.concatenate([added(sa[0], ta), added(sb[0], tb)], axis=1)


def scatter_input(pos, rows, w):
    pieces = {}
    for d in ORDER + (0,):
        pieces[d] = swapped(input_piece(pos, rows, w, 0, d))
    for d in ORDER + (0,):
        pieces[d] = input_piece(pos, rows, w, 1, d, pieces[d])
    row = added(pieces[0], [along(pieces[d], "xy", d) for d in ORDER])
    return added(row[0], [along(row[d], "yx", d) for d in ORDER])


def body(seq_in, w_proj, w_out, filters):
    g, y, x, z = (lax.axis_index(name) for name in ("grp", "hy", "hx", "seq"))
    teacher = g == 0
    pos = jnp.stack([g, y, x, z]).astype(jnp.int32)
    weights_in, weights_out = w_proj[0], w_out[0]
    length = 4096
    tap_scale = length ** (-0.5)
    tables = dft_constants()
    spec_shape = ((NK, 32, 256), F32)
    row_shape = ((512, 256), BF)

    weights_hbm = pltpu.with_memory_space_constraint(weights_in, pltpu.HBM)
    half = lax.dynamic_slice_in_dim(seq_in, g * 128, 128, 1)

    def project(blocks, marks, before, last):
        return project_part(pos, blocks, marks, weights_hbm, before, last)

    pair, single, carried = gather_product(half, project)

    def teach(operands):
        pair, q, carried = operands
        moved = (ring(pair, 1), ring(pair, -1))
        state = attend(pos, q, [pair], None, [(0, True)], False)
        for step in range(1, 5):
            moved, state = lax.optimization_barrier((moved, state))
            blocks, steps = moved, [(step, True), (step, False)]
            if step < 3:
                moved = (ring(blocks[0], 1), ring(blocks[1], -1))
            elif step == 3:
                moved = (ring(blocks[0], 1),)
            else:
                steps = steps[:1]
            state = attend(pos, q, blocks, state, steps, step == 4)
        return (state[0],) + tuple(blank(pos, row_shape, spec_shape, spec_shape))

    def learn(operands):
        pair, gate, carried = operands
        field = exchanged(carried, "seq")
        spec_h = filter_spectrum(filters, tables, tap_scale)
        conv, spec_u = convolve(field, spec_h, tables, False)
        mixed, conv_rows = gate_rows(exchanged(conv, "seq"), gate)
        return (mixed, conv_rows, spec_u, spec_h)

    mixed, conv_rows, spec_u, spec_h = lax.cond(g == 1, learn, teach, (pair, single, carried))
    y_own = scatter_features(*spread_out(pos, mixed, weights_out))
    sent = jnp.where(teacher, y_own[:, 128:], y_own[:, :128])
    kept = jnp.where(teacher, y_own[:, :128], y_own[:, 128:])
    got = swapped(sent)
    low, high = kept.astype(F32), got.astype(F32)
    diff = jnp.where(teacher, high - low, low - high).astype(BF)

    def gated(blocks, marks, before, last):
        extra = (conv_rows, single) if last else None
        return gated_part(pos, blocks, marks, weights_out, before, extra)

    d_conv, d_gate = gather_product(diff, gated)

    def rest(operands):
        return tuple(blank(pos, ((512, 768), BF), ((32, 4096), F32)))

    def learn_back(operands):
        d_conv, d_gate, pair, spec_u, spec_h = operands
        d_field, spec_d = convolve(exchanged(d_conv, "seq"), spec_h, tables, True)
        d_blocks = exchanged(d_field, "seq")
        d_taps = taps_gradient(spec_u, spec_d, tables, tap_scale)
        return (gradient_rows(d_blocks, pair, d_gate), d_taps)

    d_rows, d_taps = lax.cond(
        teacher, rest, learn_back, (d_conv, d_gate, pair, spec_u, spec_h)
    )
    lower = swapped(d_taps[:, :2048].astype(BF)).astype(F32)
    sums = scatter_input(pos, d_rows, weights_in)
    d_input = jnp.concatenate([swapped(sums), sums], axis=1)
    paired = jnp.where(teacher, y_own, d_input)[None]
    grad_filters = jnp.where(teacher, lower, d_taps[:, 2048:])
    return (paired, grad_filters)


def solution(mesh):
    fine = Mesh(mesh.devices.reshape(2, 4, 4, 8), ("grp", "hy", "hx", "seq"))
    return jax.shard_map(
        body,
        mesh=fine,
        in_specs=(
            P("seq", HEAD),
            P("grp", None, None, HEAD),
            P("grp", HEAD, None),
            P(HEAD + ("seq",), None),
        ),
        out_specs=(P("grp", "seq", HEAD), P(HEAD + ("seq",), "grp")),
        check_vma=False,
    )
```
